32 devices in a mesh: narrow: 4 (over x, core), wide: 8 (over z, y).
Axes of the slice: x: 2, y: 2, z: 4, core: 2. Of those that a mesh axis runs over, the one named last changes fastest.
Arguments:
- block_input: bfloat16 [2, 4096, 2048], P(None, ('narrow', 'wide')), may hold values from -6 to 6
- segment_ids: int32 [2, 4096], P(None, ('narrow', 'wide')), may hold values from 0 to 15, never falling along the last dimension, each value on 1 to 512 neighbouring positions
- cotangent: bfloat16 [2, 4096, 2048], P(None, ('narrow', 'wide')), may hold values from -6 to 6
- attn_gain: bfloat16 [2048], P(('narrow', 'wide')), may hold values from 0.099609375 to 1.8984375
- attn_shift: bfloat16 [2048], P(('narrow', 'wide')), may hold values from -3 to 3
- query_weight: bfloat16 [2048, 2048], P(('narrow', 'wide')), may hold values from -0.125 to 0.125
- query_bias: bfloat16 [2048], P(('narrow', 'wide')), may hold values from -3 to 3
- key_weight: bfloat16 [2048, 2048], P(('narrow', 'wide')), may hold values from -0.125 to 0.125
- value_weight: bfloat16 [2048, 2048], P(('narrow', 'wide')), may hold values from -0.125 to 0.125
- value_bias: bfloat16 [2048], P(('narrow', 'wide')), may hold values from -3 to 3
- out_weight: bfloat16 [2048, 2048], P(('narrow', 'wide')), may hold values from -1 to 1
- out_bias: bfloat16 [2048], P(('narrow', 'wide')), may hold values from -3 to 3
- mlp_gain: bfloat16 [2048], P(('narrow', 'wide')), may hold values from 0.099609375 to 1.8984375
- mlp_shift: bfloat16 [2048], P(('narrow', 'wide')), may hold values from -3 to 3
- up_weight: bfloat16 [2048, 8192], P(('narrow', 'wide')), may hold values from -0.125 to 0.125
- up_bias: bfloat16 [8192], P(('narrow', 'wide')), may hold values from -3 to 3
- down_weight: bfloat16 [8192, 2048], P(('narrow', 'wide')), may hold values from -0.0625 to 0.0625
- down_bias: bfloat16 [2048], P(('narrow', 'wide')), may hold values from -3 to 3
Outputs:
- block_output: bfloat16 [2, 4096, 2048], P(None, ('narrow', 'wide'))
- input_grad: float32 [2, 4096, 2048], P(None, ('narrow', 'wide'))
- attn_gain_grad: float32 [2048], P(('narrow', 'wide'))
- attn_shift_grad: float32 [2048], P(('narrow', 'wide'))
- query_weight_grad: float32 [2048, 2048], P(('narrow', 'wide'))
- query_bias_grad: float32 [2048], P(('narrow', 'wide'))
- key_weight_grad: float32 [2048, 2048], P(('narrow', 'wide'))
- value_weight_grad: float32 [2048, 2048], P(('narrow', 'wide'))
- value_bias_grad: float32 [2048], P(('narrow', 'wide'))
- out_weight_grad: float32 [2048, 2048], P(('narrow', 'wide'))
- out_bias_grad: float32 [2048], P(('narrow', 'wide'))
- mlp_gain_grad: float32 [2048], P(('narrow', 'wide'))
- mlp_shift_grad: float32 [2048], P(('narrow', 'wide'))
- up_weight_grad: float32 [2048, 8192], P(('narrow', 'wide'))
- up_bias_grad: float32 [8192], P(('narrow', 'wide'))
- down_weight_grad: float32 [8192, 2048], P(('narrow', 'wide'))
- down_bias_grad: float32 [2048], P(('narrow', 'wide'))
The draws below stay inside these ranges and needn't reach their ends.
Inputs may be any that keep to these rules, and one draw needn't show every extreme that they name: `segment_ids`: in each sequence the document numbers never fall, every number is used, each document has 1 to 512 tokens and the longest has exactly 512.
All inputs are finite; a program needn't handle non-finite values.
Results may differ from the reference program's by a relative error of at most 0.019.
Values may be sent and summed in bfloat16 or wider, within the bound.
No kernel may reach another device: no remote copies, remote signals or barrier semaphores. Data moves between devices by JAX's collectives and lax.ppermute only.
A program may use at most 448 MiB of HBM per device.

```python
import math
import jax
import jax.numpy as jnp
import numpy as np
from jax import lax

D = 2048
HEADS = 16
HEAD_DIM = 128
FF = 8192
BATCH = 2
SEQ = 4096
LONGEST = 512
DOCS = 16


def with_spikes(drawn, rng, source, target, parts, factor):
    def block_of(dim):
        return (jnp.arange(drawn.shape[dim]) // (drawn.shape[dim] // parts)).reshape((-1,) + (1,) * (drawn.ndim - 1 - dim))

    one_side = jax.random.permutation(rng, parts)[block_of(target)]
    second = (block_of(target) + parts // 2) % parts
    return jnp.where((block_of(source) == one_side) | (block_of(source) == second), factor * drawn, drawn)


def steps_of(rng, extent, shards, low, high):
    def one(dim, shards_of):
        draws = jax.random.uniform(jax.random.fold_in(jax.random.fold_in(rng, 6), dim), (shards_of,), jnp.float32, low / len(shards), high / len(shards))
        return jnp.repeat(jnp.exp(draws), extent[dim] // shards_of).reshape((-1,) + (1,) * (len(extent) - dim - 1))

    factor_of = one(*shards[0])
    for cut in shards[1:]:
        factor_of = factor_of * one(*cut)
    return factor_of


def profile(count, total, limit, slope):
    loads = [(1 << 20) // math.isqrt(grade ** slope) + 1 for grade in range(2, count + 1)]
    rest, counts = total - limit - (count - 1), [1] * (count - 1)
    while rest > 0:
        movable = [i for i in range(count - 1) if counts[i] < limit]
        pool, remaining = sum([loads[i] for i in movable]), rest
        for i in movable:
            extra = min(limit - counts[i], max(1, remaining * loads[i] // pool), rest)
            counts[i] = counts[i] + extra
            rest = rest - extra
    return np.array([limit] + counts)


def uneven_parts(stream_key, number_of, total, reach, lean):
    if number_of == 2:
        one = jax.random.randint(stream_key, (), max(1, total - reach), min(reach, total - 1) + 1)
        return jnp.stack([one, total - one])
    sizes = jnp.asarray(profile(number_of, total, reach, lean), jnp.int32)
    pairs = (number_of - 1) // 2
    giver, sink = sizes[1:1 + 2 * pairs:2], sizes[2:2 + 2 * pairs:2]
    margin = jnp.minimum(giver - 1, reach - sink)
    moved = jax.random.randint(jax.random.fold_in(stream_key, 1), (pairs,), 0, 1 << 20) % (margin + 1)
    sizes = sizes.at[1:1 + 2 * pairs:2].set(giver - moved).at[2:2 + 2 * pairs:2].set(sink + moved)
    return sizes[jax.random.permutation(jax.random.fold_in(stream_key, 2), number_of)]


def bell_draw(own_key, shape, width, reach, shards=(), kind=jnp.bfloat16):
    values = jax.random.normal(own_key, shape, jnp.float32) * width
    if len(shards) > 0:
        values = steps_of(own_key, shape, shards, -0.22, 0.18) * values
    return jnp.clip(values, min=-reach, max=reach).astype(kind)


def noise_with(stream_key, extent, scale, reach, cuts, heavy, held_as=jnp.bfloat16):
    array = scale * jax.random.normal(stream_key, extent, jnp.float32)
    if cuts:
        array = array * steps_of(stream_key, extent, cuts, -0.22, 0.18)
    return jnp.clip(with_spikes(array, jax.random.fold_in(stream_key, 3), *heavy), -reach, reach).astype(held_as)


def setup_inputs(seed: int = 0) -> dict:
    arg_keys = jax.random.split(jax.random.key(seed), 19)
    block_input = bell_draw(arg_keys[0], (BATCH, SEQ, D), 1.0, 6.0, ((1, 32),))
    segment_ids = jax.vmap(lambda own: jnp.searchsorted(jnp.cumsum(uneven_parts(own, DOCS, SEQ, LONGEST, 2)), jnp.arange(SEQ), side="right"))(jax.random.split(arg_keys[1], BATCH)).reshape((BATCH, SEQ)).astype(jnp.int32)
    cotangent = noise_with(arg_keys[2], (BATCH, SEQ, D), 1.0, 6.0, ((1, 32),), (1, 2, 32, 2.75))
    attn_gain = jnp.clip(1.0 + 0.18 * jax.random.normal(arg_keys[3], (D,), jnp.float32), 0.099609375, 1.8984375).astype(jnp.bfloat16)
    attn_shift = bell_draw(arg_keys[4], (D,), 0.3, 3.0, ((0, 32),))
    query_weight = bell_draw(arg_keys[5], (D, D), D ** -0.5, 0.125, ((0, 32),))
    query_bias = bell_draw(arg_keys[6], (D,), 0.5, 3.0, ((0, 32),))
    key_weight = bell_draw(arg_keys[7], (D, D), D ** -0.5, 0.125, ((0, 32),))
    value_weight = bell_draw(arg_keys[8], (D, D), D ** -0.5, 0.125, ((0, 32),))
    value_bias = bell_draw(arg_keys[9], (D,), 0.5, 3.0, ((0, 32),))
    out_weight = bell_draw(arg_keys[10], (D, D), (D // 64) ** -0.5, 1.0, ((0, 32),))
    out_bias = bell_draw(arg_keys[11], (D,), 0.5, 3.0, ((0, 32),))
    mlp_gain = jnp.clip(1.0 + 0.18 * jax.random.normal(arg_keys[12], (D,), jnp.float32), 0.099609375, 1.8984375).astype(jnp.bfloat16)
    mlp_shift = bell_draw(arg_keys[13], (D,), 0.3, 3.0, ((0, 32),))
    up_weight = bell_draw(arg_keys[14], (D, FF), D ** -0.5, 0.125, ((0, 32),))
    up_bias = bell_draw(arg_keys[15], (FF,), 0.5, 3.0, ((0, 32),))
    down_weight = bell_draw(arg_keys[16], (FF, D), FF ** -0.5, 0.0625, ((0, 32),))
    down_bias = bell_draw(arg_keys[17], (D,), 0.5, 3.0, ((0, 32),))
    return dict(block_input=block_input, segment_ids=segment_ids, cotangent=cotangent, attn_gain=attn_gain, attn_shift=attn_shift, query_weight=query_weight, query_bias=query_bias, key_weight=key_weight, value_weight=value_weight, value_bias=value_bias, out_weight=out_weight, out_bias=out_bias, mlp_gain=mlp_gain, mlp_shift=mlp_shift, up_weight=up_weight, up_bias=up_bias, down_weight=down_weight, down_bias=down_bias)


@jax.custom_vjp
def low(v):
    return lax.optimization_barrier(v.astype(jnp.bfloat16)).astype(jnp.float32)

@jax.custom_vjp
def low_back(v):
    return v

def low_keep(v):
    return (low(v), None)

def low_pass(kept, grad):
    return (grad,)

def back_keep(v):
    return (v, None)

def back_low(kept, grad):
    return (low(grad),)
low.defvjp(low_keep, low_pass)
low_back.defvjp(back_keep, back_low)
eps = 1e-05
neg_big = -1e+30

def matmul(left, right):
    return jnp.dot(left, right, precision=lax.Precision.HIGHEST, preferred_element_type=jnp.float32)

def normalize(values, gain, shift):
    center = lax.optimization_barrier(jnp.mean(values, axis=-1, keepdims=True))
    centered = values - center
    spread = lax.optimization_barrier(jnp.mean(centered * centered, axis=-1, keepdims=True))
    return centered * lax.rsqrt(spread + eps) * gain + shift

def attend(queries, key_rows, value_rows, segments):
    length = queries.shape[0]
    block_rows = min(512, length)
    positions = jnp.arange(length, dtype=jnp.int32)
    score_scale = 1.0 / math.sqrt(HEAD_DIM)

    def one_block(block_index):
        first_row = (block_index * block_rows).astype(jnp.int32)
        query_rows = lax.dynamic_slice_in_dim(queries, first_row, block_rows, 0)
        query_segs = lax.dynamic_slice_in_dim(segments, first_row, block_rows, 0)
        query_pos = lax.dynamic_slice_in_dim(positions, first_row, block_rows, 0)
        scores = jnp.einsum('qhd,khd->hqk', query_rows, key_rows, precision=lax.Precision.HIGHEST) * score_scale
        allowed = jnp.logical_and(query_segs[:, None] == segments[None, :], positions[None, :] <= query_pos[:, None])
        scores = low_back(jnp.where(allowed[None], scores, neg_big))
        attn_probs = low(jax.nn.softmax(scores, axis=-1))
        return jnp.einsum('hqk,khd->qhd', attn_probs, value_rows, precision=lax.Precision.HIGHEST)
    blocks = lax.map(jax.checkpoint(one_block), jnp.arange(length // block_rows, dtype=jnp.int32))
    return blocks.reshape(length, HEADS * HEAD_DIM)

def layer(inputs, segments, params):
    attn_gain, attn_shift, query_weight, query_bias, key_weight, value_weight, value_bias, out_weight, out_bias, mlp_gain, mlp_shift, up_weight, up_bias, down_weight, down_bias = params
    length = inputs.shape[0]
    first_norm = low(normalize(inputs, attn_gain, attn_shift))
    queries = low(low_back(matmul(first_norm, query_weight) + query_bias))
    key_rows = low(low_back(matmul(first_norm, key_weight)))
    value_rows = low(low_back(matmul(first_norm, value_weight) + value_bias))
    head_shape = (length, HEADS, HEAD_DIM)
    mixed = attend(queries.reshape(head_shape), key_rows.reshape(head_shape), value_rows.reshape(head_shape), segments)
    mixed = low(low_back(mixed))
    middle = inputs + low_back(matmul(mixed, out_weight) + out_bias)
    second_norm = low(normalize(middle, mlp_gain, mlp_shift))
    inner = low_back(matmul(second_norm, up_weight) + up_bias)
    hidden = low(jax.nn.gelu(inner, approximate=False))
    return middle + matmul(hidden, down_weight) + down_bias

def reference(block_input, segment_ids, cotangent, attn_gain, attn_shift, query_weight, query_bias, key_weight, value_weight, value_bias, out_weight, out_bias, mlp_gain, mlp_shift, up_weight, up_bias, down_weight, down_bias):
    params = tuple((item.astype(jnp.float32) for item in (attn_gain, attn_shift, query_weight, query_bias, key_weight, value_weight, value_bias, out_weight, out_bias, mlp_gain, mlp_shift, up_weight, up_bias, down_weight, down_bias)))

    def one_sequence(totals, items):
        sequence, segments, cotan_rows = items
        inputs = sequence.astype(jnp.float32)
        output, pullback = jax.vjp(lambda values, weights: layer(values, segments, weights), inputs, params)
        input_part, weight_part = pullback(cotan_rows.astype(jnp.float32))
        totals = jax.tree.map(jnp.add, totals, weight_part)
        return (totals, (output.astype(jnp.bfloat16), input_part))
    zeros = tuple((jnp.zeros_like(item) for item in params))
    totals, (outputs, input_grads) = lax.scan(one_sequence, zeros, (block_input, segment_ids, cotangent))
    return (outputs, input_grads, totals[0], totals[1], totals[2], totals[3], totals[4], totals[5], totals[6], totals[7], totals[8], totals[9], totals[10], totals[11], totals[12], totals[13], totals[14])
```

```python
import functools
import math

import jax
import jax.numpy as jnp
from jax import lax
from jax.experimental import pallas as pl
from jax.experimental.pallas import tpu as pltpu
from jax.sharding import PartitionSpec as P

HEADS = 16
NARROW, WIDE = "narrow", "wide"
BOTH = (NARROW, WIDE)
REACH = 4


eps = 1e-05
neg_big = -1e30


def shifted(value, axis, by):
    devices = lax.axis_size(axis)
    return lax.ppermute(value, axis, [(i, (i + by) % devices) for i in range(devices)])


def as_sent(value):

    def short(part):
        return part.astype(jnp.bfloat16) if part.dtype == jnp.float32 else part

    return jax.tree.map(short, value)


def normalize(values, gain, shift):
    center = jnp.mean(values, axis=-1, keepdims=True)
    centered = values - center
    spread = jnp.mean(centered * centered, axis=-1, keepdims=True)
    return centered * lax.rsqrt(spread + eps) * gain + shift


def gelu_exact(values):
    return jax.nn.gelu(values, approximate=False)


def matmul(left, right):
    return jnp.dot(left, right, preferred_element_type=jnp.float32)


def outer_sum(left, right):
    return lax.dot_general(
        left, right, (((0,), (0,)), ((), ())), preferred_element_type=jnp.float32
    )


def times_transpose(left, right):
    return lax.dot_general(
        left, right, (((1,), (1,)), ((), ())), preferred_element_type=jnp.float32
    )


def key_positions(first_row, row_count, tokens, narrow_size, wide_size):
    row_ids = first_row + jnp.arange(row_count, dtype=jnp.int32)
    source_wide = row_ids // (tokens * narrow_size)
    source_narrow = row_ids // tokens % narrow_size
    return (source_narrow * wide_size + source_wide) * tokens + row_ids % tokens


def block_mask(query_segs, query_pos, key_segs, key_pos):
    same_doc = query_segs[:, :, None] == key_segs[:, None, :]
    causal = key_pos[None, None, :] <= query_pos[None, :, None]
    return jnp.logical_and(same_doc, causal)


def raw_scores(query_rows, key_rows, score_scale, allowed):
    scores = (
        jnp.einsum("bqhd,bkhd->bhqk", query_rows, key_rows, preferred_element_type=jnp.float32)
        * score_scale
    )
    return jnp.where(allowed[:, None], scores, neg_big)


def forward_block(running, query_heads, key_block, value_block, allowed, score_scale):
    row_max, row_total, weighted = running
    scores = raw_scores(query_heads, key_block, score_scale, allowed)
    new_max = jnp.maximum(row_max, jnp.max(scores, axis=-1))
    rescale = jnp.exp(row_max - new_max)
    exp_terms = jnp.where(allowed[:, None], jnp.exp(scores - new_max[..., None]), 0.0)
    row_total = row_total * rescale + jnp.sum(exp_terms, axis=-1)
    added = jnp.einsum(
        "bhqk,bkhd->bqhd",
        exp_terms.astype(jnp.bfloat16),
        value_block,
        preferred_element_type=jnp.float32,
    )
    weighted = weighted * jnp.transpose(rescale, (0, 2, 1))[..., None] + added
    return (new_max, row_total, weighted)


def backward_block(
    query_grad,
    query_heads,
    dout_heads,
    key_block,
    value_block,
    allowed,
    delta,
    log_total,
    score_scale,
):
    scores = raw_scores(query_heads, key_block, score_scale, allowed)
    attn_probs = jnp.where(allowed[:, None], jnp.exp(scores - log_total[..., None]), 0.0)
    prob_grad = jnp.einsum(
        "bqhd,bkhd->bhqk", dout_heads, value_block, preferred_element_type=jnp.float32
    )
    score_grad = (attn_probs * (prob_grad - delta[..., None])).astype(jnp.bfloat16)
    query_grad = query_grad + score_scale * jnp.einsum(
        "bhqk,bkhd->bqhd", score_grad, key_block, preferred_element_type=jnp.float32
    )
    key_grad = score_scale * jnp.einsum(
        "bhqk,bqhd->bkhd", score_grad, query_heads, preferred_element_type=jnp.float32
    )
    value_grad = jnp.einsum(
        "bhqk,bqhd->bkhd",
        attn_probs.astype(jnp.bfloat16),
        dout_heads,
        preferred_element_type=jnp.float32,
    )
    return (query_grad, key_grad, value_grad)


def on_device_ring(
    block_input,
    segment_ids,
    cotangent,
    attn_gain,
    attn_shift,
    query_weight,
    query_bias,
    key_weight,
    value_weight,
    value_bias,
    out_weight,
    out_bias,
    mlp_gain,
    mlp_shift,
    up_weight,
    up_bias,
    down_weight,
    down_bias,
):
    batch, tokens, model_width = block_input.shape
    narrow_size = lax.axis_size(NARROW)
    wide_size = lax.axis_size(WIDE)
    wide_index = lax.axis_index(WIDE)
    group_rows = tokens * narrow_size
    heads_local = HEADS // narrow_size
    head_dim = model_width // HEADS
    score_scale = 1.0 / math.sqrt(head_dim)
    f32 = jnp.float32
    bf16 = jnp.bfloat16
    attn_set = (
        lax.all_gather(attn_gain, BOTH, axis=0, tiled=True),
        lax.all_gather(attn_shift, BOTH, axis=0, tiled=True),
        lax.all_gather(query_weight, BOTH, axis=0, tiled=True),
        lax.all_gather(query_bias, BOTH, axis=0, tiled=True),
        lax.all_gather(key_weight, BOTH, axis=0, tiled=True),
        lax.all_gather(value_weight, BOTH, axis=0, tiled=True),
        lax.all_gather(value_bias, BOTH, axis=0, tiled=True),
        lax.all_gather(out_weight, BOTH, axis=0, tiled=True),
        lax.all_gather(out_bias, BOTH, axis=0, tiled=True),
    )
    (
        gain_attn,
        shift_attn,
        query_full,
        qbias_full,
        key_full,
        value_full,
        vbias_full,
        out_full,
        obias_full,
    ) = attn_set
    inputs = block_input.astype(f32).reshape(-1, model_width)
    first_norm = normalize(inputs, gain_attn.astype(f32), shift_attn.astype(f32)).astype(bf16)
    split_shape = (batch, tokens, HEADS, head_dim)
    queries = (
        (matmul(first_norm, query_full) + qbias_full.astype(f32)).astype(bf16).reshape(split_shape)
    )
    key_rows = matmul(first_norm, key_full).astype(bf16).reshape(split_shape)
    value_rows = (
        (matmul(first_norm, value_full) + vbias_full.astype(f32)).astype(bf16).reshape(split_shape)
    )
    query_heads, key_heads, value_heads = (
        lax.all_to_all(queries, NARROW, split_axis=2, concat_axis=1, tiled=True),
        lax.all_to_all(key_rows, NARROW, split_axis=2, concat_axis=1, tiled=True),
        lax.all_to_all(value_rows, NARROW, split_axis=2, concat_axis=1, tiled=True),
    )
    query_segs = lax.all_gather(segment_ids, NARROW, axis=1, tiled=True)
    query_pos = key_positions(wide_index * group_rows, group_rows, tokens, narrow_size, wide_size)

    def block_allowed(cycle_step, seg_block):
        source = (wide_index - cycle_step) % wide_size
        key_pos = key_positions(source * group_rows, group_rows, tokens, narrow_size, wide_size)
        return block_mask(query_segs, query_pos, seg_block, key_pos)

    running = (
        jnp.full((batch, heads_local, group_rows), neg_big, f32),
        jnp.zeros((batch, heads_local, group_rows), f32),
        jnp.zeros((batch, group_rows, heads_local, head_dim), f32),
    )
    travelling = (key_heads, value_heads, query_segs)
    received = []
    for cycle_step in range(REACH + 1):
        if cycle_step > 0:
            travelling = shifted((travelling[0], travelling[1], travelling[2]), WIDE, 1)
        received.append(travelling)
        key_block, value_block, seg_block = travelling
        allowed = block_allowed(cycle_step, seg_block)
        running = forward_block(running, query_heads, key_block, value_block, allowed, score_scale)
    row_max, row_total, weighted = running
    attn_out = weighted / jnp.transpose(row_total, (0, 2, 1))[..., None]
    log_total = row_max + jnp.log(row_total)
    mixed = lax.all_to_all(
        attn_out.astype(bf16), NARROW, split_axis=1, concat_axis=2, tiled=True
    ).reshape(-1, model_width)
    middle = inputs + matmul(mixed, out_full) + obias_full.astype(f32)
    mlp_set = (
        lax.all_gather(mlp_gain, BOTH, axis=0, tiled=True),
        lax.all_gather(mlp_shift, BOTH, axis=0, tiled=True),
        lax.all_gather(up_weight, BOTH, axis=0, tiled=True),
        lax.all_gather(up_bias, BOTH, axis=0, tiled=True),
        lax.all_gather(down_weight, BOTH, axis=0, tiled=True),
        lax.all_gather(down_bias, BOTH, axis=0, tiled=True),
    )
    gain_mlp, shift_mlp, up_full, ubias_full, down_full, dbias_full = mlp_set
    second_norm = normalize(middle, gain_mlp.astype(f32), shift_mlp.astype(f32)).astype(bf16)
    inner = matmul(second_norm, up_full) + ubias_full.astype(f32)
    hidden = gelu_exact(inner).astype(bf16)
    output = middle + matmul(hidden, down_full) + dbias_full.astype(f32)
    block_output = output.astype(bf16).reshape(batch, tokens, model_width)
    mlp_set = (
        lax.all_gather(mlp_gain, BOTH, axis=0, tiled=True),
        lax.all_gather(mlp_shift, BOTH, axis=0, tiled=True),
        lax.all_gather(up_weight, BOTH, axis=0, tiled=True),
        lax.all_gather(up_bias, BOTH, axis=0, tiled=True),
        lax.all_gather(down_weight, BOTH, axis=0, tiled=True),
        lax.all_gather(down_bias, BOTH, axis=0, tiled=True),
    )
    gain_mlp, shift_mlp, up_full, ubias_full, down_full, dbias_full = mlp_set
    cotan_rows = cotangent.reshape(-1, model_width)
    down_grad = outer_sum(hidden, cotan_rows)
    dbias_grad = jnp.sum(cotan_rows.astype(f32), axis=0)
    hidden_grad = times_transpose(cotan_rows, down_full)
    gelu_pull = jax.vjp(gelu_exact, inner)[1]
    inner_grad = gelu_pull(hidden_grad)[0].astype(bf16)
    up_grad = outer_sum(second_norm, inner_grad)
    ubias_grad = jnp.sum(inner_grad.astype(f32), axis=0)
    second_grad = times_transpose(inner_grad, up_full)
    mlp_pull = jax.vjp(normalize, middle, gain_mlp.astype(f32), shift_mlp.astype(f32))[1]
    middle_part, mgain_grad, mshift_grad = mlp_pull(second_grad)
    middle_grad = cotan_rows.astype(f32) + middle_part
    mlp_shards = (
        lax.psum_scatter(mgain_grad, BOTH, scatter_dimension=0, tiled=True),
        lax.psum_scatter(mshift_grad, BOTH, scatter_dimension=0, tiled=True),
        lax.psum_scatter(up_grad, BOTH, scatter_dimension=0, tiled=True),
        lax.psum_scatter(ubias_grad, BOTH, scatter_dimension=0, tiled=True),
        lax.psum_scatter(down_grad, BOTH, scatter_dimension=0, tiled=True),
        lax.psum_scatter(dbias_grad, BOTH, scatter_dimension=0, tiled=True),
    )
    attn_set = (
        lax.all_gather(attn_gain, BOTH, axis=0, tiled=True),
        lax.all_gather(attn_shift, BOTH, axis=0, tiled=True),
        lax.all_gather(query_weight, BOTH, axis=0, tiled=True),
        lax.all_gather(query_bias, BOTH, axis=0, tiled=True),
        lax.all_gather(key_weight, BOTH, axis=0, tiled=True),
        lax.all_gather(value_weight, BOTH, axis=0, tiled=True),
        lax.all_gather(value_bias, BOTH, axis=0, tiled=True),
        lax.all_gather(out_weight, BOTH, axis=0, tiled=True),
        lax.all_gather(out_bias, BOTH, axis=0, tiled=True),
    )
    (
        gain_attn,
        shift_attn,
        query_full,
        qbias_full,
        key_full,
        value_full,
        vbias_full,
        out_full,
        obias_full,
    ) = attn_set
    branch_grad = middle_grad.astype(bf16)
    out_grad = outer_sum(mixed, branch_grad)
    obias_grad = jnp.sum(branch_grad.astype(f32), axis=0)
    mixed_grad = times_transpose(branch_grad, out_full).astype(bf16).reshape(split_shape)
    dout_heads = lax.all_to_all(mixed_grad, NARROW, split_axis=2, concat_axis=1, tiled=True)
    delta = jnp.transpose(jnp.sum(dout_heads.astype(f32) * attn_out, axis=-1), (0, 2, 1))
    travelling = (key_heads, value_heads, query_segs)
    received = []
    for cycle_step in range(REACH + 1):
        if cycle_step > 0:
            travelling = shifted((travelling[0], travelling[1], travelling[2]), WIDE, 1)
        received.append(travelling)
    query_grad = jnp.zeros((batch, group_rows, heads_local, head_dim), f32)
    key_terms = []
    value_terms = []
    for cycle_step in range(REACH + 1):
        key_block, value_block, seg_block = received[cycle_step]
        allowed = block_allowed(cycle_step, seg_block)
        query_grad, key_term, value_term = backward_block(
            query_grad,
            query_heads,
            dout_heads,
            key_block,
            value_block,
            allowed,
            delta,
            log_total,
            score_scale,
        )
        key_terms.append(key_term)
        value_terms.append(value_term)
    carried = (key_terms[REACH], value_terms[REACH])
    for cycle_step in range(REACH - 1, -1, -1):
        arrived = shifted((as_sent(carried[0]), as_sent(carried[1])), WIDE, -1)
        carried = (arrived[0] + key_terms[cycle_step], arrived[1] + value_terms[cycle_step])
    key_sum, value_sum = carried
    query_back, key_back, value_back = (
        lax.all_to_all(query_grad.astype(bf16), NARROW, split_axis=1, concat_axis=2, tiled=True),
        lax.all_to_all(key_sum.astype(bf16), NARROW, split_axis=1, concat_axis=2, tiled=True),
        lax.all_to_all(value_sum.astype(bf16), NARROW, split_axis=1, concat_axis=2, tiled=True),
    )
    query_back = query_back.reshape(-1, model_width)
    key_back = key_back.reshape(-1, model_width)
    value_back = value_back.reshape(-1, model_width)
    query_wgrad = outer_sum(first_norm, query_back)
    qbias_grad = jnp.sum(query_back.astype(f32), axis=0)
    key_wgrad = outer_sum(first_norm, key_back)
    value_wgrad = outer_sum(first_norm, value_back)
    vbias_grad = jnp.sum(value_back.astype(f32), axis=0)
    first_grad = (
        times_transpose(query_back, query_full)
        + times_transpose(key_back, key_full)
        + times_transpose(value_back, value_full)
    )
    attn_pull = jax.vjp(normalize, inputs, gain_attn.astype(f32), shift_attn.astype(f32))[1]
    input_part, again_grad, ashift_grad = attn_pull(first_grad)
    input_grad = (middle_grad + input_part).reshape(batch, tokens, model_width)
    attn_shards = (
        lax.psum_scatter(again_grad, BOTH, scatter_dimension=0, tiled=True),
        lax.psum_scatter(ashift_grad, BOTH, scatter_dimension=0, tiled=True),
        lax.psum_scatter(query_wgrad, BOTH, scatter_dimension=0, tiled=True),
        lax.psum_scatter(qbias_grad, BOTH, scatter_dimension=0, tiled=True),
        lax.psum_scatter(key_wgrad, BOTH, scatter_dimension=0, tiled=True),
        lax.psum_scatter(value_wgrad, BOTH, scatter_dimension=0, tiled=True),
        lax.psum_scatter(vbias_grad, BOTH, scatter_dimension=0, tiled=True),
        lax.psum_scatter(out_grad, BOTH, scatter_dimension=0, tiled=True),
        lax.psum_scatter(obias_grad, BOTH, scatter_dimension=0, tiled=True),
    )
    return (
        block_output,
        input_grad,
        attn_shards[0],
        attn_shards[1],
        attn_shards[2],
        attn_shards[3],
        attn_shards[4],
        attn_shards[5],
        attn_shards[6],
        attn_shards[7],
        attn_shards[8],
        mlp_shards[0],
        mlp_shards[1],
        mlp_shards[2],
        mlp_shards[3],
        mlp_shards[4],
        mlp_shards[5],
    )


def all_small(parts):
    packed = jnp.concatenate(parts)[None]
    return lax.all_gather(packed, BOTH, axis=0, tiled=True)


def fwd_kernel(segc_ref, segr_ref, qkv_ref, out_ref, lse_ref, *, blocks, scale2):
    half = blocks // 4
    for i in range(blocks):
        w0, n = 4 * (i % half), i // half
        q = qkv_ref[w0 : w0 + 4, 0, n].reshape(512, 128)
        lo = max(i - 1, 0)
        k = jnp.concatenate(
            [qkv_ref[4 * (j % half) : 4 * (j % half) + 4, 1, j // half] for j in range(lo, i + 1)]
        ).reshape(-1, 128)
        v = jnp.concatenate(
            [qkv_ref[4 * (j % half) : 4 * (j % half) + 4, 2, j // half] for j in range(lo, i + 1)]
        ).reshape(-1, 128)
        allowed = mask_of(segc_ref, segr_ref, i, lo)
        s = lax.dot_general(q, k, (((1,), (1,)), ((), ())), preferred_element_type=jnp.float32)
        s = jnp.where(allowed, s * scale2, neg_big)
        m = jnp.max(s, axis=-1, keepdims=True)
        p = jnp.exp2(s - m)
        total = jnp.sum(p, axis=-1, keepdims=True)
        o = jnp.dot(p.astype(jnp.bfloat16), v, preferred_element_type=jnp.float32)
        o = o / total
        out_ref[w0 : w0 + 4, n] = o.astype(jnp.bfloat16).reshape(4, 128, 128)
        lse_ref[i] = m + jnp.log2(total)


def mask_of(segc_ref, segr_ref, i, lo):
    keys = 512 * (i + 1 - lo)
    same = segc_ref[i] == segr_ref[:, 512 * lo : 512 * (i + 1)]
    rows = lax.broadcasted_iota(jnp.int32, (512, keys), 0) + 512 * (i - lo)
    cols = lax.broadcasted_iota(jnp.int32, (512, keys), 1)
    return jnp.logical_and(same, cols <= rows)


def bwd_kernel(segc_ref, segr_ref, qkv_ref, do_ref, lse_ref, grad_ref, dk_acc, dv_acc, *, blocks, scale, scale2):
    half = blocks // 4
    f32 = jnp.float32

    def at(j):
        return slice(4 * (j % half), 4 * (j % half) + 4), j // half

    for i in range(blocks):
        wi, n = at(i)
        q = qkv_ref[wi, 0, n].reshape(512, 128)
        do = do_ref[wi, n].reshape(512, 128)
        lo = max(i - 1, 0)
        k = jnp.concatenate([qkv_ref[at(j)[0], 1, at(j)[1]] for j in range(lo, i + 1)]).reshape(-1, 128)
        v = jnp.concatenate([qkv_ref[at(j)[0], 2, at(j)[1]] for j in range(lo, i + 1)]).reshape(-1, 128)
        allowed = mask_of(segc_ref, segr_ref, i, lo)
        s = lax.dot_general(q, k, (((1,), (1,)), ((), ())), preferred_element_type=f32)
        p = jnp.exp2(jnp.where(allowed, s * scale2, neg_big) - lse_ref[i])
        dp = lax.dot_general(do, v, (((1,), (1,)), ((), ())), preferred_element_type=f32)
        t = p * dp
        delta = jnp.sum(t, axis=-1, keepdims=True)
        ds = (t - p * delta).astype(jnp.bfloat16)
        dq = jnp.dot(ds, k, preferred_element_type=f32) * scale
        grad_ref[wi, 0, n] = dq.astype(jnp.bfloat16).reshape(4, 128, 128)
        dk = lax.dot_general(ds, q, (((0,), (0,)), ((), ())), preferred_element_type=f32)
        dv = lax.dot_general(
            p.astype(jnp.bfloat16), do, (((0,), (0,)), ((), ())), preferred_element_type=f32
        )
        if i > 0:
            wp, np_ = at(i - 1)
            grad_ref[wp, 1, np_] = (
                ((dk_acc[...] + dk[:512]) * scale).astype(jnp.bfloat16).reshape(4, 128, 128)
            )
            grad_ref[wp, 2, np_] = (dv_acc[...] + dv[:512]).astype(jnp.bfloat16).reshape(4, 128, 128)
        if i == blocks - 1:
            grad_ref[wi, 1, n] = (dk[-512:] * scale).astype(jnp.bfloat16).reshape(4, 128, 128)
            grad_ref[wi, 2, n] = dv[-512:].astype(jnp.bfloat16).reshape(4, 128, 128)
        else:
            dk_acc[...] = dk[-512:]
            dv_acc[...] = dv[-512:]


def whole_vmem(count):
    return [pl.BlockSpec(memory_space=pltpu.VMEM)] * count


def attend_fwd(segc, segr, qkv):
    blocks = segc.shape[0]
    wide, _, narrow, rows, width = qkv.shape
    scale2 = math.log2(math.e) / math.sqrt(width)
    return pl.pallas_call(
        functools.partial(fwd_kernel, blocks=blocks, scale2=scale2),
        out_shape=(
            jax.ShapeDtypeStruct((wide, narrow, rows, width), jnp.bfloat16),
            jax.ShapeDtypeStruct((blocks, 512, 1), jnp.float32),
        ),
        in_specs=whole_vmem(3),
        out_specs=tuple(whole_vmem(2)),
        compiler_params=pltpu.CompilerParams(vmem_limit_bytes=48 << 20),
        name="attend_fwd",
    )(segc, segr, qkv)


def attend_bwd(segc, segr, qkv, dout, lse):
    blocks = segc.shape[0]
    width = qkv.shape[-1]
    scale = 1.0 / math.sqrt(width)
    return pl.pallas_call(
        functools.partial(
            bwd_kernel, blocks=blocks, scale=scale, scale2=scale * math.log2(math.e)
        ),
        out_shape=jax.ShapeDtypeStruct(qkv.shape, jnp.bfloat16),
        in_specs=whole_vmem(5),
        out_specs=whole_vmem(1)[0],
        scratch_shapes=[pltpu.VMEM((512, width), jnp.float32)] * 2,
        compiler_params=pltpu.CompilerParams(vmem_limit_bytes=48 << 20),
        name="attend_bwd",
    )(segc, segr, qkv, dout, lse)


def narrow_gather(rows):
    return lax.all_gather(rows, NARROW, axis=0, tiled=True)


def narrow_scatter(partial):
    return lax.psum_scatter(
        partial.astype(jnp.bfloat16), NARROW, scatter_dimension=0, tiled=True
    ).astype(jnp.float32)


def wide_swap(parts):
    return lax.all_to_all(parts, WIDE, split_axis=0, concat_axis=0, tiled=True)


def narrow_swap(parts):
    return lax.all_to_all(parts, NARROW, split_axis=0, concat_axis=0, tiled=True)


def wide_gather(shard, axis):
    return lax.all_gather(shard, WIDE, axis=axis, tiled=True)


def wide_scatter(full, axis):
    return lax.psum_scatter(full.astype(jnp.bfloat16), WIDE, scatter_dimension=axis, tiled=True)


def on_device(
    block_input,
    segment_ids,
    cotangent,
    attn_gain,
    attn_shift,
    query_weight,
    query_bias,
    key_weight,
    value_weight,
    value_bias,
    out_weight,
    out_bias,
    mlp_gain,
    mlp_shift,
    up_weight,
    up_bias,
    down_weight,
    down_bias,
):
    f32 = jnp.float32
    bf16 = jnp.bfloat16
    batch, tokens, width = block_input.shape
    narrow = lax.axis_size(NARROW)
    wide = lax.axis_size(WIDE)
    me_n = lax.axis_index(NARROW)
    me_w = lax.axis_index(WIDE)
    rows = batch * tokens
    heads_local = HEADS // narrow
    head_dim = width // HEADS
    cols = heads_local * head_dim
    shard = width // (narrow * wide)

    qkv_shard = jnp.stack([query_weight, key_weight, value_weight], axis=1)
    qkv_shard = qkv_shard.reshape(shard, 3, narrow, cols).transpose(2, 0, 1, 3)
    qkv_shard = narrow_swap(qkv_shard.reshape(narrow, shard, 3 * cols))
    qkv_w = wide_gather(qkv_shard, 1).reshape(width, 3 * cols)
    out_w = wide_gather(out_weight, 0)
    ff_local = up_weight.shape[1] // narrow
    up_shard = narrow_swap(up_weight.reshape(shard, narrow, ff_local).transpose(1, 0, 2))
    up_w = wide_gather(up_shard, 1).reshape(width, ff_local)
    down_w = wide_gather(down_weight, 0)

    smalls = [
        attn_gain, attn_shift, out_bias, mlp_gain, mlp_shift, down_bias, query_bias, value_bias, up_bias
    ]
    small = all_small(smalls)

    def full_vector(k):
        return small[:, k * shard : (k + 1) * shard].reshape(-1).astype(f32)

    gain_attn, shift_attn, obias, gain_mlp, shift_mlp, dbias = [full_vector(k) for k in range(6)]
    mine = lax.dynamic_slice_in_dim(small, me_n * wide, wide, 0)
    qbias = mine[:, 6 * shard : 7 * shard].reshape(-1).astype(f32)
    vbias = mine[:, 7 * shard : 8 * shard].reshape(-1).astype(f32)
    ubias = mine[:, 8 * shard :].reshape(-1).astype(f32)
    qkv_bias = jnp.concatenate([qbias, jnp.zeros_like(qbias), vbias])

    segs = lax.all_gather(segment_ids[None], BOTH, axis=0, tiled=True)
    unit_segs = lax.dynamic_index_in_dim(segs, me_w // heads_local, 1, keepdims=False).reshape(-1)
    seq_blocks = unit_segs.shape[0] // 512
    segc = unit_segs.reshape(seq_blocks, 512, 1)
    segr = unit_segs.reshape(1, -1)

    inputs = block_input.astype(f32).reshape(rows, width)
    first_norm = narrow_gather(normalize(inputs, gain_attn, shift_attn).astype(bf16))
    qkv = (matmul(first_norm, qkv_w) + qkv_bias).astype(bf16)
    qkv = qkv.reshape(narrow, batch, tokens, 3, heads_local, head_dim).transpose(1, 4, 3, 0, 2, 5)
    qkv = wide_swap(qkv.reshape(wide, 3, narrow, tokens, head_dim))
    unit_out, lse = attend_fwd(segc, segr, qkv)
    mixed = wide_swap(unit_out)
    mixed = mixed.reshape(batch, heads_local, narrow, tokens, head_dim).transpose(2, 0, 3, 1, 4)
    mixed = mixed.reshape(narrow * rows, cols)
    middle = inputs + narrow_scatter(matmul(mixed, out_w)) + obias

    second_norm = narrow_gather(normalize(middle, gain_mlp, shift_mlp).astype(bf16))
    inner = matmul(second_norm, up_w) + ubias
    hidden = gelu_exact(inner).astype(bf16)
    output = middle + narrow_scatter(matmul(hidden, down_w)) + dbias
    block_output = output.astype(bf16).reshape(batch, tokens, width)

    cotan_own = cotangent.reshape(rows, width)
    cotan = narrow_gather(cotan_own)
    down_grad = wide_scatter(outer_sum(hidden, cotan), 0)
    hidden_grad = times_transpose(cotan, down_w)
    inner_grad = jax.vjp(gelu_exact, inner)[1](hidden_grad)[0].astype(bf16)
    up_grad = outer_sum(second_norm, inner_grad).reshape(narrow, wide * shard, ff_local)
    up_grad = narrow_swap(wide_scatter(up_grad, 1)).transpose(1, 0, 2).reshape(shard, -1)
    ubias_grad = jnp.sum(inner_grad.astype(f32), axis=0)
    second_grad = narrow_scatter(times_transpose(inner_grad, up_w))
    mlp_pull = jax.vjp(normalize, middle, gain_mlp, shift_mlp)[1]
    middle_part, mgain_grad, mshift_grad = mlp_pull(second_grad)
    dbias_grad = jnp.sum(cotan_own.astype(f32), axis=0)
    middle_grad = cotan_own.astype(f32) + middle_part

    branch_own = middle_grad.astype(bf16)
    obias_grad = jnp.sum(branch_own.astype(f32), axis=0)
    branch = narrow_gather(branch_own)
    mixed_grad = times_transpose(branch, out_w).astype(bf16)
    mixed_grad = mixed_grad.reshape(narrow, batch, tokens, heads_local, head_dim)
    dout = wide_swap(mixed_grad.transpose(1, 3, 0, 2, 4).reshape(wide, narrow, tokens, head_dim))
    out_grad = wide_scatter(outer_sum(mixed, branch), 0)
    unit_grads = attend_bwd(segc, segr, qkv, dout, lse)
    back = wide_swap(unit_grads)
    back = back.reshape(batch, heads_local, 3, narrow, tokens, head_dim).transpose(3, 0, 4, 2, 1, 5)
    back = back.reshape(narrow * rows, 3 * cols)
    qkv_grad = outer_sum(first_norm, back).reshape(narrow, wide * shard, 3 * cols)
    qkv_grad = narrow_swap(wide_scatter(qkv_grad, 1)).reshape(narrow, shard, 3, cols)
    qkv_grad = qkv_grad.transpose(2, 1, 0, 3).reshape(3, shard, width).astype(f32)
    back_sums = jnp.sum(back.astype(f32), axis=0)
    first_grad = narrow_scatter(times_transpose(back, qkv_w))
    attn_pull = jax.vjp(normalize, inputs, gain_attn, shift_attn)[1]
    input_part, again_grad, ashift_grad = attn_pull(first_grad)
    input_grad = (middle_grad + input_part).reshape(batch, tokens, width)

    fulls = [again_grad, ashift_grad, obias_grad, mgain_grad, mshift_grad, dbias_grad]
    fulls = jnp.concatenate([v.reshape(narrow * wide, shard) for v in fulls], axis=1)
    slices = [back_sums[:cols], back_sums[2 * cols :], ubias_grad]
    slices = jnp.concatenate([v.reshape(wide, -1) for v in slices], axis=1)
    placed = jnp.zeros((narrow * wide, slices.shape[1]), f32)
    placed = lax.dynamic_update_slice_in_dim(placed, slices, me_n * wide, 0)
    vectors = lax.psum_scatter(
        jnp.concatenate([fulls, placed], axis=1), BOTH, scatter_dimension=0, tiled=True
    ).reshape(-1)

    def vector(k):
        return vectors[k * shard : (k + 1) * shard]

    return (
        block_output,
        input_grad,
        vector(0),
        vector(1),
        qkv_grad[0],
        vector(6),
        qkv_grad[1],
        qkv_grad[2],
        vector(7),
        out_grad.astype(f32),
        vector(2),
        vector(3),
        vector(4),
        up_grad.astype(f32),
        vectors[8 * shard :],
        down_grad.astype(f32),
        vector(5),
    )


def body_of(mesh):
    def body(*args):
        batch, tokens, width = args[0].shape
        narrow, wide = mesh.shape[NARROW], mesh.shape[WIDE]
        one_unit = batch * (HEADS // narrow) == wide and tokens == 128 and narrow == 4
        return (on_device if one_unit else on_device_ring)(*args)

    return body


def solution(mesh):
    return jax.shard_map(
        body_of(mesh),
        mesh=mesh,
        in_specs=(
            P(None, BOTH, None),
            P(None, BOTH),
            P(None, BOTH, None),
            P(BOTH),
            P(BOTH),
            P(BOTH, None),
            P(BOTH),
            P(BOTH, None),
            P(BOTH, None),
            P(BOTH),
            P(BOTH, None),
            P(BOTH),
            P(BOTH),
            P(BOTH),
            P(BOTH, None),
            P(BOTH),
            P(BOTH, None),
            P(BOTH),
        ),
        out_specs=(
            P(None, BOTH, None),
            P(None, BOTH, None),
            P(BOTH),
            P(BOTH),
            P(BOTH, None),
            P(BOTH),
            P(BOTH, None),
            P(BOTH, None),
            P(BOTH),
            P(BOTH, None),
            P(BOTH),
            P(BOTH),
            P(BOTH),
            P(BOTH, None),
            P(BOTH),
            P(BOTH, None),
            P(BOTH),
        ),
        check_vma=False,
    )
```

```python
import functools
import math

import jax
import jax.numpy as jnp
from jax import lax
from jax.experimental import pallas as pl
from jax.experimental.pallas import tpu as pltpu
from jax.sharding import PartitionSpec as P

HEADS = 16
NARROW, WIDE = "narrow", "wide"
BOTH = (NARROW, WIDE)
REACH = 4


eps = 1e-05
neg_big = -1e30


def shifted(value, axis, by):
    devices = lax.axis_size(axis)
    return lax.ppermute(value, axis, [(i, (i + by) % devices) for i in range(devices)])


def as_sent(value):

    def short(part):
        return part.astype(jnp.bfloat16) if part.dtype == jnp.float32 else part

    return jax.tree.map(short, value)


def normalize(values, gain, shift):
    center = jnp.mean(values, axis=-1, keepdims=True)
    centered = values - center
    spread = jnp.mean(centered * centered, axis=-1, keepdims=True)
    return centered * lax.rsqrt(spread + eps) * gain + shift


def gelu_exact(values):
    return jax.nn.gelu(values, approximate=False)


def matmul(left, right):
    return jnp.dot(left, right, preferred_element_type=jnp.float32)


def outer_sum(left, right):
    return lax.dot_general(
        left, right, (((0,), (0,)), ((), ())), preferred_element_type=jnp.float32
    )


def times_transpose(left, right):
    return lax.dot_general(
        left, right, (((1,), (1,)), ((), ())), preferred_element_type=jnp.float32
    )


def key_positions(first_row, row_count, tokens, narrow_size, wide_size):
    row_ids = first_row + jnp.arange(row_count, dtype=jnp.int32)
    source_wide = row_ids // (tokens * narrow_size)
    source_narrow = row_ids // tokens % narrow_size
    return (source_narrow * wide_size + source_wide) * tokens + row_ids % tokens


def block_mask(query_segs, query_pos, key_segs, key_pos):
    same_doc = query_segs[:, :, None] == key_segs[:, None, :]
    causal = key_pos[None, None, :] <= query_pos[None, :, None]
    return jnp.logical_and(same_doc, causal)


def raw_scores(query_rows, key_rows, score_scale, allowed):
    scores = (
        jnp.einsum("bqhd,bkhd->bhqk", query_rows, key_rows, preferred_element_type=jnp.float32)
        * score_scale
    )
    return jnp.where(allowed[:, None], scores, neg_big)


def forward_block(running, query_heads, key_block, value_block, allowed, score_scale):
    row_max, row_total, weighted = running
    scores = raw_scores(query_heads, key_block, score_scale, allowed)
    new_max = jnp.maximum(row_max, jnp.max(scores, axis=-1))
    rescale = jnp.exp(row_max - new_max)
    exp_terms = jnp.where(allowed[:, None], jnp.exp(scores - new_max[..., None]), 0.0)
    row_total = row_total * rescale + jnp.sum(exp_terms, axis=-1)
    added = jnp.einsum(
        "bhqk,bkhd->bqhd",
        exp_terms.astype(jnp.bfloat16),
        value_block,
        preferred_element_type=jnp.float32,
    )
    weighted = weighted * jnp.transpose(rescale, (0, 2, 1))[..., None] + added
    return (new_max, row_total, weighted)


def backward_block(
    query_grad,
    query_heads,
    dout_heads,
    key_block,
    value_block,
    allowed,
    delta,
    log_total,
    score_scale,
):
    scores = raw_scores(query_heads, key_block, score_scale, allowed)
    attn_probs = jnp.where(allowed[:, None], jnp.exp(scores - log_total[..., None]), 0.0)
    prob_grad = jnp.einsum(
        "bqhd,bkhd->bhqk", dout_heads, value_block, preferred_element_type=jnp.float32
    )
    score_grad = (attn_probs * (prob_grad - delta[..., None])).astype(jnp.bfloat16)
    query_grad = query_grad + score_scale * jnp.einsum(
        "bhqk,bkhd->bqhd", score_grad, key_block, preferred_element_type=jnp.float32
    )
    key_grad = score_scale * jnp.einsum(
        "bhqk,bqhd->bkhd", score_grad, query_heads, preferred_element_type=jnp.float32
    )
    value_grad = jnp.einsum(
        "bhqk,bqhd->bkhd",
        attn_probs.astype(jnp.bfloat16),
        dout_heads,
        preferred_element_type=jnp.float32,
    )
    return (query_grad, key_grad, value_grad)


def on_device_ring(
    block_input,
    segment_ids,
    cotangent,
    attn_gain,
    attn_shift,
    query_weight,
    query_bias,
    key_weight,
    value_weight,
    value_bias,
    out_weight,
    out_bias,
    mlp_gain,
    mlp_shift,
    up_weight,
    up_bias,
    down_weight,
    down_bias,
):
    batch, tokens, model_width = block_input.shape
    narrow_size = lax.axis_size(NARROW)
    wide_size = lax.axis_size(WIDE)
    wide_index = lax.axis_index(WIDE)
    group_rows = tokens * narrow_size
    heads_local = HEADS // narrow_size
    head_dim = model_width // HEADS
    score_scale = 1.0 / math.sqrt(head_dim)
    f32 = jnp.float32
    bf16 = jnp.bfloat16
    attn_set = (
        lax.all_gather(attn_gain, BOTH, axis=0, tiled=True),
        lax.all_gather(attn_shift, BOTH, axis=0, tiled=True),
        lax.all_gather(query_weight, BOTH, axis=0, tiled=True),
        lax.all_gather(query_bias, BOTH, axis=0, tiled=True),
        lax.all_gather(key_weight, BOTH, axis=0, tiled=True),
        lax.all_gather(value_weight, BOTH, axis=0, tiled=True),
        lax.all_gather(value_bias, BOTH, axis=0, tiled=True),
        lax.all_gather(out_weight, BOTH, axis=0, tiled=True),
        lax.all_gather(out_bias, BOTH, axis=0, tiled=True),
    )
    (
        gain_attn,
        shift_attn,
        query_full,
        qbias_full,
        key_full,
        value_full,
        vbias_full,
        out_full,
        obias_full,
    ) = attn_set
    inputs = block_input.astype(f32).reshape(-1, model_width)
    first_norm = normalize(inputs, gain_attn.astype(f32), shift_attn.astype(f32)).astype(bf16)
    split_shape = (batch, tokens, HEADS, head_dim)
    queries = (
        (matmul(first_norm, query_full) + qbias_full.astype(f32)).astype(bf16).reshape(split_shape)
    )
    key_rows = matmul(first_norm, key_full).astype(bf16).reshape(split_shape)
    value_rows = (
        (matmul(first_norm, value_full) + vbias_full.astype(f32)).astype(bf16).reshape(split_shape)
    )
    query_heads, key_heads, value_heads = (
        lax.all_to_all(queries, NARROW, split_axis=2, concat_axis=1, tiled=True),
        lax.all_to_all(key_rows, NARROW, split_axis=2, concat_axis=1, tiled=True),
        lax.all_to_all(value_rows, NARROW, split_axis=2, concat_axis=1, tiled=True),
    )
    query_segs = lax.all_gather(segment_ids, NARROW, axis=1, tiled=True)
    query_pos = key_positions(wide_index * group_rows, group_rows, tokens, narrow_size, wide_size)

    def block_allowed(cycle_step, seg_block):
        source = (wide_index - cycle_step) % wide_size
        key_pos = key_positions(source * group_rows, group_rows, tokens, narrow_size, wide_size)
        return block_mask(query_segs, query_pos, seg_block, key_pos)

    running = (
        jnp.full((batch, heads_local, group_rows), neg_big, f32),
        jnp.zeros((batch, heads_local, group_rows), f32),
        jnp.zeros((batch, group_rows, heads_local, head_dim), f32),
    )
    travelling = (key_heads, value_heads, query_segs)
    received = []
    for cycle_step in range(REACH + 1):
        if cycle_step > 0:
            travelling = shifted((travelling[0], travelling[1], travelling[2]), WIDE, 1)
        received.append(travelling)
        key_block, value_block, seg_block = travelling
        allowed = block_allowed(cycle_step, seg_block)
        running = forward_block(running, query_heads, key_block, value_block, allowed, score_scale)
    row_max, row_total, weighted = running
    attn_out = weighted / jnp.transpose(row_total, (0, 2, 1))[..., None]
    log_total = row_max + jnp.log(row_total)
    mixed = lax.all_to_all(
        attn_out.astype(bf16), NARROW, split_axis=1, concat_axis=2, tiled=True
    ).reshape(-1, model_width)
    middle = inputs + matmul(mixed, out_full) + obias_full.astype(f32)
    mlp_set = (
        lax.all_gather(mlp_gain, BOTH, axis=0, tiled=True),
        lax.all_gather(mlp_shift, BOTH, axis=0, tiled=True),
        lax.all_gather(up_weight, BOTH, axis=0, tiled=True),
        lax.all_gather(up_bias, BOTH, axis=0, tiled=True),
        lax.all_gather(down_weight, BOTH, axis=0, tiled=True),
        lax.all_gather(down_bias, BOTH, axis=0, tiled=True),
    )
    gain_mlp, shift_mlp, up_full, ubias_full, down_full, dbias_full = mlp_set
    second_norm = normalize(middle, gain_mlp.astype(f32), shift_mlp.astype(f32)).astype(bf16)
    inner = matmul(second_norm, up_full) + ubias_full.astype(f32)
    hidden = gelu_exact(inner).astype(bf16)
    output = middle + matmul(hidden, down_full) + dbias_full.astype(f32)
    block_output = output.astype(bf16).reshape(batch, tokens, model_width)
    mlp_set = (
        lax.all_gather(mlp_gain, BOTH, axis=0, tiled=True),
        lax.all_gather(mlp_shift, BOTH, axis=0, tiled=True),
        lax.all_gather(up_weight, BOTH, axis=0, tiled=True),
        lax.all_gather(up_bias, BOTH, axis=0, tiled=True),
        lax.all_gather(down_weight, BOTH, axis=0, tiled=True),
        lax.all_gather(down_bias, BOTH, axis=0, tiled=True),
    )
    gain_mlp, shift_mlp, up_full, ubias_full, down_full, dbias_full = mlp_set
    cotan_rows = cotangent.reshape(-1, model_width)
    down_grad = outer_sum(hidden, cotan_rows)
    dbias_grad = jnp.sum(cotan_rows.astype(f32), axis=0)
    hidden_grad = times_transpose(cotan_rows, down_full)
    gelu_pull = jax.vjp(gelu_exact, inner)[1]
    inner_grad = gelu_pull(hidden_grad)[0].astype(bf16)
    up_grad = outer_sum(second_norm, inner_grad)
    ubias_grad = jnp.sum(inner_grad.astype(f32), axis=0)
    second_grad = times_transpose(inner_grad, up_full)
    mlp_pull = jax.vjp(normalize, middle, gain_mlp.astype(f32), shift_mlp.astype(f32))[1]
    middle_part, mgain_grad, mshift_grad = mlp_pull(second_grad)
    middle_grad = cotan_rows.astype(f32) + middle_part
    mlp_shards = (
        lax.psum_scatter(mgain_grad, BOTH, scatter_dimension=0, tiled=True),
        lax.psum_scatter(mshift_grad, BOTH, scatter_dimension=0, tiled=True),
        lax.psum_scatter(up_grad, BOTH, scatter_dimension=0, tiled=True),
        lax.psum_scatter(ubias_grad, BOTH, scatter_dimension=0, tiled=True),
        lax.psum_scatter(down_grad, BOTH, scatter_dimension=0, tiled=True),
        lax.psum_scatter(dbias_grad, BOTH, scatter_dimension=0, tiled=True),
    )
    attn_set = (
        lax.all_gather(attn_gain, BOTH, axis=0, tiled=True),
        lax.all_gather(attn_shift, BOTH, axis=0, tiled=True),
        lax.all_gather(query_weight, BOTH, axis=0, tiled=True),
        lax.all_gather(query_bias, BOTH, axis=0, tiled=True),
        lax.all_gather(key_weight, BOTH, axis=0, tiled=True),
        lax.all_gather(value_weight, BOTH, axis=0, tiled=True),
        lax.all_gather(value_bias, BOTH, axis=0, tiled=True),
        lax.all_gather(out_weight, BOTH, axis=0, tiled=True),
        lax.all_gather(out_bias, BOTH, axis=0, tiled=True),
    )
    (
        gain_attn,
        shift_attn,
        query_full,
        qbias_full,
        key_full,
        value_full,
        vbias_full,
        out_full,
        obias_full,
    ) = attn_set
    branch_grad = middle_grad.astype(bf16)
    out_grad = outer_sum(mixed, branch_grad)
    obias_grad = jnp.sum(branch_grad.astype(f32), axis=0)
    mixed_grad = times_transpose(branch_grad, out_full).astype(bf16).reshape(split_shape)
    dout_heads = lax.all_to_all(mixed_grad, NARROW, split_axis=2, concat_axis=1, tiled=True)
    delta = jnp.transpose(jnp.sum(dout_heads.astype(f32) * attn_out, axis=-1), (0, 2, 1))
    travelling = (key_heads, value_heads, query_segs)
    received = []
    for cycle_step in range(REACH + 1):
        if cycle_step > 0:
            travelling = shifted((travelling[0], travelling[1], travelling[2]), WIDE, 1)
        received.append(travelling)
    query_grad = jnp.zeros((batch, group_rows, heads_local, head_dim), f32)
    key_terms = []
    value_terms = []
    for cycle_step in range(REACH + 1):
        key_block, value_block, seg_block = received[cycle_step]
        allowed = block_allowed(cycle_step, seg_block)
        query_grad, key_term, value_term = backward_block(
            query_grad,
            query_heads,
            dout_heads,
            key_block,
            value_block,
            allowed,
            delta,
            log_total,
            score_scale,
        )
        key_terms.append(key_term)
        value_terms.append(value_term)
    carried = (key_terms[REACH], value_terms[REACH])
    for cycle_step in range(REACH - 1, -1, -1):
        arrived = shifted((as_sent(carried[0]), as_sent(carried[1])), WIDE, -1)
        carried = (arrived[0] + key_terms[cycle_step], arrived[1] + value_terms[cycle_step])
    key_sum, value_sum = carried
    query_back, key_back, value_back = (
        lax.all_to_all(query_grad.astype(bf16), NARROW, split_axis=1, concat_axis=2, tiled=True),
        lax.all_to_all(key_sum.astype(bf16), NARROW, split_axis=1, concat_axis=2, tiled=True),
        lax.all_to_all(value_sum.astype(bf16), NARROW, split_axis=1, concat_axis=2, tiled=True),
    )
    query_back = query_back.reshape(-1, model_width)
    key_back = key_back.reshape(-1, model_width)
    value_back = value_back.reshape(-1, model_width)
    query_wgrad = outer_sum(first_norm, query_back)
    qbias_grad = jnp.sum(query_back.astype(f32), axis=0)
    key_wgrad = outer_sum(first_norm, key_back)
    value_wgrad = outer_sum(first_norm, value_back)
    vbias_grad = jnp.sum(value_back.astype(f32), axis=0)
    first_grad = (
        times_transpose(query_back, query_full)
        + times_transpose(key_back, key_full)
        + times_transpose(value_back, value_full)
    )
    attn_pull = jax.vjp(normalize, inputs, gain_attn.astype(f32), shift_attn.astype(f32))[1]
    input_part, again_grad, ashift_grad = attn_pull(first_grad)
    input_grad = (middle_grad + input_part).reshape(batch, tokens, model_width)
    attn_shards = (
        lax.psum_scatter(again_grad, BOTH, scatter_dimension=0, tiled=True),
        lax.psum_scatter(ashift_grad, BOTH, scatter_dimension=0, tiled=True),
        lax.psum_scatter(query_wgrad, BOTH, scatter_dimension=0, tiled=True),
        lax.psum_scatter(qbias_grad, BOTH, scatter_dimension=0, tiled=True),
        lax.psum_scatter(key_wgrad, BOTH, scatter_dimension=0, tiled=True),
        lax.psum_scatter(value_wgrad, BOTH, scatter_dimension=0, tiled=True),
        lax.psum_scatter(vbias_grad, BOTH, scatter_dimension=0, tiled=True),
        lax.psum_scatter(out_grad, BOTH, scatter_dimension=0, tiled=True),
        lax.psum_scatter(obias_grad, BOTH, scatter_dimension=0, tiled=True),
    )
    return (
        block_output,
        input_grad,
        attn_shards[0],
        attn_shards[1],
        attn_shards[2],
        attn_shards[3],
        attn_shards[4],
        attn_shards[5],
        attn_shards[6],
        attn_shards[7],
        attn_shards[8],
        mlp_shards[0],
        mlp_shards[1],
        mlp_shards[2],
        mlp_shards[3],
        mlp_shards[4],
        mlp_shards[5],
    )


def flip(value, axis, bits):
    size = lax.axis_size(axis)
    return lax.ppermute(value, axis, [(i, i ^ bits) for i in range(size)])


def at(value, index, dim=0):
    return lax.dynamic_index_in_dim(value, index, dim, keepdims=False)


def cube(wide):
    steps = []
    bits = 1
    while bits < wide:
        steps.append((WIDE, bits))
        bits *= 2
    return steps + [(NARROW, 1), (NARROW, 2)]


def cube_gather(row):
    for axis, bits in cube(lax.axis_size(WIDE)):
        other = flip(row, axis, bits)
        high = (lax.axis_index(axis) & bits) > 0
        row = jnp.concatenate(
            [jnp.where(high, other, row), jnp.where(high, row, other)], axis=0
        )
    return row


def cube_scatter(table):
    wide = lax.axis_size(WIDE)
    steps = cube(wide)
    table = table.reshape((2,) * len(steps) + (table.shape[-1],))
    order = [len(steps) - 2, len(steps) - 1] + list(range(len(steps) - 2))[::-1]
    left = list(range(len(steps)))
    for k in order:
        axis, bits = steps[k]
        dim = len(left) - 1 - left.index(k)
        high = ((lax.axis_index(axis) & bits) > 0).astype(jnp.int32)
        table = at(table, high, dim) + flip(at(table, 1 - high, dim), axis, bits)
        left.remove(k)
    return table


def narrow_gather(own):
    across = flip(own, NARROW, 2)
    beside = flip(own, NARROW, 1)
    return jnp.concatenate([own, beside, across, flip(across, NARROW, 1)], axis=0)


def narrow_scatter(partial):
    f32 = jnp.float32
    parts = partial.reshape(4, -1, partial.shape[-1])
    far = flip(parts[3], NARROW, 1)
    near = flip(parts[1], NARROW, 1)
    passed = (parts[2].astype(f32) + far.astype(f32)).astype(jnp.bfloat16)
    across = flip(passed, NARROW, 2)
    return parts[0].astype(f32) + near.astype(f32) + across.astype(f32)


def narrow_swap(blocks):
    me = lax.axis_index(NARROW)
    result = jnp.zeros_like(blocks)
    for j in (3, 2, 1, 0):
        block = at(blocks, me ^ j)
        block = flip(block, NARROW, j) if j else block
        result = lax.dynamic_update_slice_in_dim(result, block[None], me ^ j, 0)
    return result


def ring_order(wide):
    return list(range(0, wide, 2)) + list(range(wide - 1, 0, -2))


def ring_at(position, wide):
    position = position % wide
    return jnp.where(position < wide // 2, 2 * position, 2 * (wide - 1 - position) + 1)


def ring_position(wide):
    me = lax.axis_index(WIDE)
    return jnp.where(me % 2 == 0, me // 2, wide - 1 - me // 2)


def ring_step(value, by):
    order = ring_order(lax.axis_size(WIDE))
    size = len(order)
    return lax.ppermute(
        value, WIDE, [(order[i], order[(i + by) % size]) for i in range(size)]
    )


def ring_gather(shard, axis):
    wide = lax.axis_size(WIDE)
    here = ring_position(wide)
    shape = list(shard.shape)
    shape.insert(axis, wide)
    full = jnp.zeros(shape, shard.dtype)

    def put(full, piece, position):
        return lax.dynamic_update_slice_in_dim(
            full, jnp.expand_dims(piece, axis), ring_at(position, wide), axis
        )

    full = put(full, shard, here)
    ahead = behind = shard
    for k in range(1, wide // 2 + 1):
        ahead = ring_step(ahead, 1)
        full = put(full, ahead, here - k + wide)
        if k < wide - wide // 2:
            behind = ring_step(behind, -1)
            full = put(full, behind, here + k)
    return full


def ring_scatter(full, axis):
    wide = lax.axis_size(WIDE)
    here = ring_position(wide)
    bf16, f32 = jnp.bfloat16, jnp.float32

    def local(position):
        return at(full, ring_at(position + wide, wide), axis).astype(f32)

    half = wide // 2
    ahead = behind = None
    for k in range(half, 0, -1):
        term = local(here + k)
        term = term if ahead is None else term + ahead
        ahead = ring_step(term.astype(bf16), 1).astype(f32)
        if k < wide - half:
            term = local(here - k)
            term = term if behind is None else term + behind
            behind = ring_step(term.astype(bf16), -1).astype(f32)
    return local(here) + ahead + behind


def wide_swap(parts):
    return [parts[0]] + [flip(parts[d], WIDE, d) for d in range(1, parts.shape[0])]


def wide_gather(shard, axis):
    return lax.all_gather(shard, WIDE, axis=axis, tiled=True)


def wide_scatter(full, axis):
    return lax.psum_scatter(full.astype(jnp.bfloat16), WIDE, scatter_dimension=axis, tiled=True)


def vmem_specs(count):
    return [pl.BlockSpec(memory_space=pltpu.VMEM)] * count


SMEM_SPEC = pl.BlockSpec(memory_space=pltpu.SMEM)
BIG = pltpu.CompilerParams(vmem_limit_bytes=48 << 20)
CONTRACT_LAST = (((1,), (1,)), ((), ()))
CONTRACT_FIRST = (((0,), (0,)), ((), ()))


def project_kernel(me_ref, rows_ref, weight_ref, bias_ref, out_ref, *, heads, by_last):
    me = me_ref[1]
    if by_last:
        acc = lax.dot_general(
            rows_ref[...], weight_ref[...], CONTRACT_LAST, preferred_element_type=jnp.float32
        )
    else:
        acc = jnp.dot(rows_ref[...], weight_ref[...], preferred_element_type=jnp.float32)
    acc = (acc + bias_ref[...]).astype(jnp.bfloat16)
    units, parts, _, tokens, head_dim = out_ref.shape
    for unit in range(units):
        b, h = divmod(unit, heads)
        for part in range(parts):
            c = (part * heads + h) * head_dim
            out_ref[unit ^ me, part, 0] = acc[b * tokens : (b + 1) * tokens, c : c + head_dim]


def project(me, rows, weight, bias, units, parts, heads, tokens, by_last):
    blocks, width = 4, rows.shape[1]
    head_dim = bias.shape[0] // (parts * heads)
    step = rows.shape[0] // blocks
    return pl.pallas_call(
        functools.partial(project_kernel, heads=heads, by_last=by_last),
        grid=(blocks,),
        out_shape=jax.ShapeDtypeStruct((units, parts, blocks, tokens, head_dim), jnp.bfloat16),
        in_specs=[
            SMEM_SPEC,
            pl.BlockSpec((step, width), lambda i: (i, 0)),
            pl.BlockSpec(weight.shape, lambda i: (0, 0), pipeline_mode=pl.Buffered(1)),
            pl.BlockSpec((1, bias.shape[0]), lambda i: (0, 0)),
        ],
        out_specs=pl.BlockSpec(
            (units, parts, 1, tokens, head_dim), lambda i: (0, 0, i, 0, 0)
        ),
        compiler_params=BIG,
        name="project",
    )(me, rows, weight, bias.reshape(1, -1))


def unproject_kernel(me_ref, *refs, heads, by_last):
    units = len(refs) - 4
    pieces, weight_ref, out_ref, rows_ref, held = refs[:units], *refs[units:]
    me = me_ref[1]
    for d in range(units):
        held[d ^ me] = pieces[d][:, 0]
    parts = held.shape[1]
    rows = jnp.concatenate(
        [
            jnp.concatenate(
                [held[b * heads + h, part] for part in range(parts) for h in range(heads)], axis=1
            )
            for b in range(units // heads)
        ],
        axis=0,
    )
    rows_ref[...] = rows
    if by_last:
        acc = lax.dot_general(
            rows, weight_ref[...], CONTRACT_LAST, preferred_element_type=jnp.float32
        )
    else:
        acc = jnp.dot(rows, weight_ref[...], preferred_element_type=jnp.float32)
    out_ref[...] = acc.astype(jnp.bfloat16)


def unproject(me, pieces, weight, heads, by_last):
    units = len(pieces)
    parts, blocks, tokens, head_dim = pieces[0].shape
    step = tokens * units // heads
    inner = parts * heads * head_dim
    width = weight.shape[0] if by_last else weight.shape[1]
    return pl.pallas_call(
        functools.partial(unproject_kernel, heads=heads, by_last=by_last),
        grid=(blocks,),
        out_shape=(
            jax.ShapeDtypeStruct((blocks * step, width), jnp.bfloat16),
            jax.ShapeDtypeStruct((blocks * step, inner), jnp.bfloat16),
        ),
        in_specs=[SMEM_SPEC]
        + [pl.BlockSpec((parts, 1, tokens, head_dim), lambda i: (0, i, 0, 0))] * units
        + [pl.BlockSpec(weight.shape, lambda i: (0, 0), pipeline_mode=pl.Buffered(1))],
        out_specs=(
            pl.BlockSpec((step, width), lambda i: (i, 0)),
            pl.BlockSpec((step, inner), lambda i: (i, 0)),
        ),
        scratch_shapes=[pltpu.VMEM((units, parts, tokens, head_dim), jnp.bfloat16)],
        compiler_params=BIG,
        name="unproject",
    )(me, *pieces, weight)


def mask_of(segc_ref, segr_ref, i, lo):
    keys = 512 * (i + 1 - lo)
    same = segc_ref[i] == segr_ref[:, 512 * lo : 512 * (i + 1)]
    rows = lax.broadcasted_iota(jnp.int32, (512, keys), 0) + 512 * (i - lo)
    cols = lax.broadcasted_iota(jnp.int32, (512, keys), 1)
    return jnp.logical_and(same, cols <= rows)


def collect(me_ref, pieces, held):
    for d, piece in enumerate(pieces):
        for j in range(4):
            held[d ^ me_ref[1], :, j ^ me_ref[0]] = piece[:, j]


def take(held, part, first, last, half):
    blocks = [
        held[4 * (i % half) : 4 * (i % half) + 4, part, i // half].reshape(512, -1)
        for i in range(first, last + 1)
    ]
    return blocks[0] if len(blocks) == 1 else jnp.concatenate(blocks, axis=0)


def give(me_ref, out_ref, part, i, half, rows):
    rows = rows.astype(out_ref.dtype).reshape(4, 128, -1)
    for c in range(4):
        out_ref[(4 * (i % half) + c) ^ me_ref[1], part, (i // half) ^ me_ref[0]] = rows[c]


def fwd_kernel(me_ref, segc_ref, segr_ref, *refs, blocks, scale2):
    pieces, (out_ref, lse_ref, held) = refs[:-3], refs[-3:]
    half = blocks // 4
    collect(me_ref, pieces, held)
    for i in range(blocks):
        lo = max(i - 1, 0)
        q = take(held, 0, i, i, half)
        k = take(held, 1, lo, i, half)
        v = take(held, 2, lo, i, half)
        s = lax.dot_general(q, k, CONTRACT_LAST, preferred_element_type=jnp.float32)
        s = jnp.where(mask_of(segc_ref, segr_ref, i, lo), s * scale2, neg_big)
        m = jnp.max(s, axis=-1, keepdims=True)
        p = jnp.exp2(s - m)
        total = jnp.sum(p, axis=-1, keepdims=True)
        o = jnp.dot(p.astype(jnp.bfloat16), v, preferred_element_type=jnp.float32)
        give(me_ref, out_ref, 0, i, half, o / total)
        lse_ref[i] = m + jnp.log2(total)


def bwd_kernel(me_ref, segc_ref, segr_ref, lse_ref, *refs, blocks, scale, scale2):
    grad_ref, held, held_do, dk_acc, dv_acc = refs[-5:]
    pieces, douts = refs[: (len(refs) - 5) // 2], refs[(len(refs) - 5) // 2 : -5]
    half = blocks // 4
    f32 = jnp.float32
    collect(me_ref, pieces, held)
    collect(me_ref, douts, held_do)
    for i in range(blocks):
        lo = max(i - 1, 0)
        q = take(held, 0, i, i, half)
        k = take(held, 1, lo, i, half)
        v = take(held, 2, lo, i, half)
        do = take(held_do, 0, i, i, half)
        s = lax.dot_general(q, k, CONTRACT_LAST, preferred_element_type=f32)
        s = jnp.where(mask_of(segc_ref, segr_ref, i, lo), s * scale2, neg_big)
        p = jnp.exp2(s - lse_ref[i])
        dp = lax.dot_general(do, v, CONTRACT_LAST, preferred_element_type=f32)
        t = p * dp
        delta = jnp.sum(t, axis=-1, keepdims=True)
        ds = (t - p * delta).astype(jnp.bfloat16)
        give(me_ref, grad_ref, 0, i, half, jnp.dot(ds, k, preferred_element_type=f32) * scale)
        dk = lax.dot_general(ds, q, CONTRACT_FIRST, preferred_element_type=f32)
        dv = lax.dot_general(
            p.astype(jnp.bfloat16), do, CONTRACT_FIRST, preferred_element_type=f32
        )
        if i > 0:
            give(me_ref, grad_ref, 1, i - 1, half, (dk_acc[...] + dk[:512]) * scale)
            give(me_ref, grad_ref, 2, i - 1, half, dv_acc[...] + dv[:512])
        if i == blocks - 1:
            give(me_ref, grad_ref, 1, i, half, dk[-512:] * scale)
            give(me_ref, grad_ref, 2, i, half, dv[-512:])
        else:
            dk_acc[...] = dk[-512:]
            dv_acc[...] = dv[-512:]


def attend_fwd(me, segc, segr, pieces):
    blocks, units = segc.shape[0], len(pieces)
    parts, narrow, rows, width = pieces[0].shape
    scale2 = math.log2(math.e) / math.sqrt(width)
    return pl.pallas_call(
        functools.partial(fwd_kernel, blocks=blocks, scale2=scale2),
        out_shape=(
            jax.ShapeDtypeStruct((units, 1, narrow, rows, width), jnp.bfloat16),
            jax.ShapeDtypeStruct((blocks, 512, 1), jnp.float32),
        ),
        in_specs=[SMEM_SPEC] + vmem_specs(2 + units),
        out_specs=tuple(vmem_specs(2)),
        scratch_shapes=[pltpu.VMEM((units, parts, narrow, rows, width), jnp.bfloat16)],
        compiler_params=BIG,
        name="attend_fwd",
    )(me, segc, segr, *pieces)


def attend_bwd(me, segc, segr, lse, pieces, douts):
    blocks, units = segc.shape[0], len(pieces)
    parts, narrow, rows, width = pieces[0].shape
    scale = 1.0 / math.sqrt(width)
    shape = (units, parts, narrow, rows, width)
    return pl.pallas_call(
        functools.partial(
            bwd_kernel, blocks=blocks, scale=scale, scale2=scale * math.log2(math.e)
        ),
        out_shape=jax.ShapeDtypeStruct(shape, jnp.bfloat16),
        in_specs=[SMEM_SPEC] + vmem_specs(3 + 2 * units),
        out_specs=vmem_specs(1)[0],
        scratch_shapes=[
            pltpu.VMEM(shape, jnp.bfloat16),
            pltpu.VMEM((units, 1, narrow, rows, width), jnp.bfloat16),
            pltpu.VMEM((512, width), jnp.float32),
            pltpu.VMEM((512, width), jnp.float32),
        ],
        compiler_params=BIG,
        name="attend_bwd",
    )(me, segc, segr, lse, *pieces, *douts)


def ff_kernel(rows_ref, weight_ref, bias_ref, pull_ref, hidden_ref, grad_ref, sum_ref):
    step = 256
    total = jnp.zeros((1, weight_ref.shape[1]), jnp.float32)
    for r in range(0, rows_ref.shape[0], step):
        x = jnp.dot(rows_ref[r : r + step], weight_ref[...], preferred_element_type=jnp.float32)
        x = x + bias_ref[...]
        below = 0.5 * (1.0 + lax.erf(x * math.sqrt(0.5)))
        hidden_ref[r : r + step] = (x * below).astype(jnp.bfloat16)
        slope = below + x * (jnp.exp(-0.5 * x * x) * (1.0 / math.sqrt(2.0 * math.pi)))
        grad = (pull_ref[r : r + step] * slope).astype(jnp.bfloat16)
        grad_ref[r : r + step] = grad
        total = total + jnp.sum(grad.astype(jnp.float32), axis=0, keepdims=True)
    sum_ref[...] = total


def feed_forward(rows, weight, bias, pull):
    count, width = rows.shape
    inner = weight.shape[1]
    step = 256
    return pl.pallas_call(
        ff_kernel,
        grid=(inner // step,),
        out_shape=(
            jax.ShapeDtypeStruct((count, inner), jnp.bfloat16),
            jax.ShapeDtypeStruct((count, inner), jnp.bfloat16),
            jax.ShapeDtypeStruct((1, inner), jnp.float32),
        ),
        in_specs=[
            pl.BlockSpec((count, width), lambda i: (0, 0), pipeline_mode=pl.Buffered(1)),
            pl.BlockSpec((width, step), lambda i: (0, i)),
            pl.BlockSpec((1, step), lambda i: (0, i)),
            pl.BlockSpec((count, step), lambda i: (0, i)),
        ],
        out_specs=(
            pl.BlockSpec((count, step), lambda i: (0, i)),
            pl.BlockSpec((count, step), lambda i: (0, i)),
            pl.BlockSpec((1, step), lambda i: (0, i)),
        ),
        compiler_params=BIG,
        name="feed_forward",
    )(rows, weight, bias.reshape(1, -1), pull)


def on_device(
    block_input,
    segment_ids,
    cotangent,
    attn_gain,
    attn_shift,
    query_weight,
    query_bias,
    key_weight,
    value_weight,
    value_bias,
    out_weight,
    out_bias,
    mlp_gain,
    mlp_shift,
    up_weight,
    up_bias,
    down_weight,
    down_bias,
):
    f32 = jnp.float32
    bf16 = jnp.bfloat16
    batch, tokens, width = block_input.shape
    narrow = lax.axis_size(NARROW)
    wide = lax.axis_size(WIDE)
    me_n = lax.axis_index(NARROW)
    me_w = lax.axis_index(WIDE)
    me = jnp.stack([me_n, me_w]).astype(jnp.int32)
    rows = batch * tokens
    heads = HEADS // narrow
    head_dim = width // HEADS
    cols = heads * head_dim
    shard = width // (narrow * wide)
    ff_local = up_weight.shape[1] // narrow

    smalls = [
        attn_gain, attn_shift, out_bias, mlp_gain, mlp_shift, down_bias, query_bias, value_bias, up_bias
    ]
    ids = segment_ids.astype(bf16).reshape(-1)
    small = cube_gather(jnp.concatenate(smalls + [ids])[None])
    ids = small[:, -batch * tokens :].reshape(narrow * wide, batch, tokens)
    unit_ids = at(ids, me_w // heads, 1).reshape(-1).astype(jnp.int32)
    segc = unit_ids.reshape(-1, 512, 1)
    segr = unit_ids.reshape(1, -1)

    def full_vector(k):
        return small[:, k * shard : (k + 1) * shard].reshape(-1).astype(f32)

    gain_attn, shift_attn, obias, gain_mlp, shift_mlp, dbias = [full_vector(k) for k in range(6)]
    mine = lax.dynamic_slice_in_dim(small, me_n * wide, wide, 0)
    qbias = mine[:, 6 * shard : 7 * shard].reshape(-1).astype(f32)
    vbias = mine[:, 7 * shard : 8 * shard].reshape(-1).astype(f32)
    ubias = mine[:, 8 * shard : 8 * shard + ff_local // wide].reshape(-1).astype(f32)
    qkv_bias = jnp.concatenate([qbias, jnp.zeros_like(qbias), vbias])

    qkv_shard = jnp.stack([query_weight, key_weight, value_weight], axis=1)
    qkv_shard = qkv_shard.reshape(shard, 3, narrow, cols).transpose(2, 0, 1, 3)
    qkv_shard = narrow_swap(qkv_shard.reshape(narrow, shard, 3 * cols))
    qkv_w = ring_gather(qkv_shard, 1).reshape(width, 3 * cols)
    down_w = wide_gather(down_weight, 0)
    up_shard = narrow_swap(up_weight.reshape(shard, narrow, ff_local).transpose(1, 0, 2))
    up_w = wide_gather(up_shard, 1).reshape(width, ff_local)
    out_w = wide_gather(out_weight, 0)

    inputs = block_input.astype(f32).reshape(rows, width)
    first_norm = narrow_gather(normalize(inputs, gain_attn, shift_attn).astype(bf16))
    sent = project(me, first_norm, qkv_w, qkv_bias, wide, 3, heads, tokens, False)
    qkv = wide_swap(sent)
    unit_out, lse = attend_fwd(me, segc, segr, qkv)
    partial, mixed = unproject(me, wide_swap(unit_out), out_w, heads, False)
    middle = inputs + narrow_scatter(partial) + obias

    cotan_own = cotangent.reshape(rows, width)
    cotan = narrow_gather(cotan_own)
    hidden_grad = times_transpose(cotan, down_w)
    second_norm = narrow_gather(normalize(middle, gain_mlp, shift_mlp).astype(bf16))
    hidden, inner_grad, ubias_grad = feed_forward(second_norm, up_w, ubias, hidden_grad)
    second_grad = narrow_scatter(times_transpose(inner_grad, up_w).astype(bf16))
    output = middle + narrow_scatter(matmul(hidden, down_w).astype(bf16)) + dbias
    block_output = output.astype(bf16).reshape(batch, tokens, width)
    down_grad = wide_scatter(outer_sum(hidden, cotan), 0)
    up_grad = outer_sum(second_norm, inner_grad).reshape(narrow, wide * shard, ff_local)
    up_grad = narrow_swap(wide_scatter(up_grad, 1)).transpose(1, 0, 2).reshape(shard, -1)
    mlp_pull = jax.vjp(normalize, middle, gain_mlp, shift_mlp)[1]
    middle_part, mgain_grad, mshift_grad = mlp_pull(second_grad)
    dbias_grad = jnp.sum(cotan_own.astype(f32), axis=0)
    middle_grad = cotan_own.astype(f32) + middle_part

    branch_own = middle_grad.astype(bf16)
    obias_grad = jnp.sum(branch_own.astype(f32), axis=0)
    branch = narrow_gather(branch_own)
    no_bias = jnp.zeros((cols,), f32)
    sent = project(me, branch, out_w, no_bias, wide, 1, heads, tokens, True)
    unit_grads = attend_bwd(me, segc, segr, lse, qkv, wide_swap(sent))
    out_grad = wide_scatter(outer_sum(mixed, branch), 0)
    partial, back = unproject(me, wide_swap(unit_grads), qkv_w, heads, True)
    first_grad = narrow_scatter(partial)
    qkv_grad = outer_sum(first_norm, back).astype(bf16).reshape(narrow, wide, shard, 3 * cols)
    qkv_grad = narrow_swap(ring_scatter(qkv_grad, 1).astype(bf16))
    qkv_grad = qkv_grad.reshape(narrow, shard, 3, cols)
    qkv_grad = qkv_grad.transpose(2, 1, 0, 3).reshape(3, shard, width).astype(f32)
    back_sums = jnp.sum(back.astype(f32), axis=0)
    attn_pull = jax.vjp(normalize, inputs, gain_attn, shift_attn)[1]
    input_part, again_grad, ashift_grad = attn_pull(first_grad)
    input_grad = (middle_grad + input_part).reshape(batch, tokens, width)

    fulls = [again_grad, ashift_grad, obias_grad, mgain_grad, mshift_grad, dbias_grad]
    fulls = jnp.concatenate([v.reshape(narrow * wide, shard) for v in fulls], axis=1)
    slices = [back_sums[:cols], back_sums[2 * cols :], ubias_grad]
    slices = jnp.concatenate([v.reshape(wide, -1) for v in slices], axis=1)
    placed = jnp.zeros((narrow * wide, slices.shape[1]), f32)
    placed = lax.dynamic_update_slice_in_dim(placed, slices, me_n * wide, 0)
    vectors = cube_scatter(jnp.concatenate([fulls, placed], axis=1))

    def vector(k):
        return vectors[k * shard : (k + 1) * shard]

    return (
        block_output,
        input_grad,
        vector(0),
        vector(1),
        qkv_grad[0],
        vector(6),
        qkv_grad[1],
        qkv_grad[2],
        vector(7),
        out_grad.astype(f32),
        vector(2),
        vector(3),
        vector(4),
        up_grad.astype(f32),
        vectors[8 * shard :],
        down_grad.astype(f32),
        vector(5),
    )


def body_of(mesh):
    def body(*args):
        batch, tokens, width = args[0].shape
        narrow, wide = mesh.shape[NARROW], mesh.shape[WIDE]
        one_unit = batch * (HEADS // narrow) == wide and tokens == 128 and narrow == 4
        return (on_device if one_unit else on_device_ring)(*args)

    return body


def solution(mesh):
    return jax.shard_map(
        body_of(mesh),
        mesh=mesh,
        in_specs=(
            P(None, BOTH, None),
            P(None, BOTH),
            P(None, BOTH, None),
            P(BOTH),
            P(BOTH),
            P(BOTH, None),
            P(BOTH),
            P(BOTH, None),
            P(BOTH, None),
            P(BOTH),
            P(BOTH, None),
            P(BOTH),
            P(BOTH),
            P(BOTH),
            P(BOTH, None),
            P(BOTH),
            P(BOTH, None),
            P(BOTH),
        ),
        out_specs=(
            P(None, BOTH, None),
            P(None, BOTH, None),
            P(BOTH),
            P(BOTH),
            P(BOTH, None),
            P(BOTH),
            P(BOTH, None),
            P(BOTH, None),
            P(BOTH),
            P(BOTH, None),
            P(BOTH),
            P(BOTH),
            P(BOTH),
            P(BOTH, None),
            P(BOTH),
            P(BOTH, None),
            P(BOTH),
        ),
        check_vma=False,
    )
```

```python
import functools
import math

import jax
import jax.numpy as jnp
from jax import lax
from jax.experimental import pallas as pl
from jax.experimental.pallas import tpu as pltpu
from jax.sharding import PartitionSpec as P

HEADS = 16
NARROW, WIDE = "narrow", "wide"
BOTH = (NARROW, WIDE)
REACH = 4


eps = 1e-05
neg_big = -1e30


def shifted(value, axis, by):
    devices = lax.axis_size(axis)
    return lax.ppermute(value, axis, [(i, (i + by) % devices) for i in range(devices)])


def as_sent(value):

    def short(part):
        return part.astype(jnp.bfloat16) if part.dtype == jnp.float32 else part

    return jax.tree.map(short, value)


def normalize(values, gain, shift):
    center = jnp.mean(values, axis=-1, keepdims=True)
    centered = values - center
    spread = jnp.mean(centered * centered, axis=-1, keepdims=True)
    return centered * lax.rsqrt(spread + eps) * gain + shift


def gelu_exact(values):
    return jax.nn.gelu(values, approximate=False)


def matmul(left, right):
    return jnp.dot(left, right, preferred_element_type=jnp.float32)


def outer_sum(left, right):
    return lax.dot_general(
        left, right, (((0,), (0,)), ((), ())), preferred_element_type=jnp.float32
    )


def times_transpose(left, right):
    return lax.dot_general(
        left, right, (((1,), (1,)), ((), ())), preferred_element_type=jnp.float32
    )


def key_positions(first_row, row_count, tokens, narrow_size, wide_size):
    row_ids = first_row + jnp.arange(row_count, dtype=jnp.int32)
    source_wide = row_ids // (tokens * narrow_size)
    source_narrow = row_ids // tokens % narrow_size
    return (source_narrow * wide_size + source_wide) * tokens + row_ids % tokens


def block_mask(query_segs, query_pos, key_segs, key_pos):
    same_doc = query_segs[:, :, None] == key_segs[:, None, :]
    causal = key_pos[None, None, :] <= query_pos[None, :, None]
    return jnp.logical_and(same_doc, causal)


def raw_scores(query_rows, key_rows, score_scale, allowed):
    scores = (
        jnp.einsum("bqhd,bkhd->bhqk", query_rows, key_rows, preferred_element_type=jnp.float32)
        * score_scale
    )
    return jnp.where(allowed[:, None], scores, neg_big)


def forward_block(running, query_heads, key_block, value_block, allowed, score_scale):
    row_max, row_total, weighted = running
    scores = raw_scores(query_heads, key_block, score_scale, allowed)
    new_max = jnp.maximum(row_max, jnp.max(scores, axis=-1))
    rescale = jnp.exp(row_max - new_max)
    exp_terms = jnp.where(allowed[:, None], jnp.exp(scores - new_max[..., None]), 0.0)
    row_total = row_total * rescale + jnp.sum(exp_terms, axis=-1)
    added = jnp.einsum(
        "bhqk,bkhd->bqhd",
        exp_terms.astype(jnp.bfloat16),
        value_block,
        preferred_element_type=jnp.float32,
    )
    weighted = weighted * jnp.transpose(rescale, (0, 2, 1))[..., None] + added
    return (new_max, row_total, weighted)


def backward_block(
    query_grad,
    query_heads,
    dout_heads,
    key_block,
    value_block,
    allowed,
    delta,
    log_total,
    score_scale,
):
    scores = raw_scores(query_heads, key_block, score_scale, allowed)
    attn_probs = jnp.where(allowed[:, None], jnp.exp(scores - log_total[..., None]), 0.0)
    prob_grad = jnp.einsum(
        "bqhd,bkhd->bhqk", dout_heads, value_block, preferred_element_type=jnp.float32
    )
    score_grad = (attn_probs * (prob_grad - delta[..., None])).astype(jnp.bfloat16)
    query_grad = query_grad + score_scale * jnp.einsum(
        "bhqk,bkhd->bqhd", score_grad, key_block, preferred_element_type=jnp.float32
    )
    key_grad = score_scale * jnp.einsum(
        "bhqk,bqhd->bkhd", score_grad, query_heads, preferred_element_type=jnp.float32
    )
    value_grad = jnp.einsum(
        "bhqk,bqhd->bkhd",
        attn_probs.astype(jnp.bfloat16),
        dout_heads,
        preferred_element_type=jnp.float32,
    )
    return (query_grad, key_grad, value_grad)


def on_device_ring(
    block_input,
    segment_ids,
    cotangent,
    attn_gain,
    attn_shift,
    query_weight,
    query_bias,
    key_weight,
    value_weight,
    value_bias,
    out_weight,
    out_bias,
    mlp_gain,
    mlp_shift,
    up_weight,
    up_bias,
    down_weight,
    down_bias,
):
    batch, tokens, model_width = block_input.shape
    narrow_size = lax.axis_size(NARROW)
    wide_size = lax.axis_size(WIDE)
    wide_index = lax.axis_index(WIDE)
    group_rows = tokens * narrow_size
    heads_local = HEADS // narrow_size
    head_dim = model_width // HEADS
    score_scale = 1.0 / math.sqrt(head_dim)
    f32 = jnp.float32
    bf16 = jnp.bfloat16
    attn_set = (
        lax.all_gather(attn_gain, BOTH, axis=0, tiled=True),
        lax.all_gather(attn_shift, BOTH, axis=0, tiled=True),
        lax.all_gather(query_weight, BOTH, axis=0, tiled=True),
        lax.all_gather(query_bias, BOTH, axis=0, tiled=True),
        lax.all_gather(key_weight, BOTH, axis=0, tiled=True),
        lax.all_gather(value_weight, BOTH, axis=0, tiled=True),
        lax.all_gather(value_bias, BOTH, axis=0, tiled=True),
        lax.all_gather(out_weight, BOTH, axis=0, tiled=True),
        lax.all_gather(out_bias, BOTH, axis=0, tiled=True),
    )
    (
        gain_attn,
        shift_attn,
        query_full,
        qbias_full,
        key_full,
        value_full,
        vbias_full,
        out_full,
        obias_full,
    ) = attn_set
    inputs = block_input.astype(f32).reshape(-1, model_width)
    first_norm = normalize(inputs, gain_attn.astype(f32), shift_attn.astype(f32)).astype(bf16)
    split_shape = (batch, tokens, HEADS, head_dim)
    queries = (
        (matmul(first_norm, query_full) + qbias_full.astype(f32)).astype(bf16).reshape(split_shape)
    )
    key_rows = matmul(first_norm, key_full).astype(bf16).reshape(split_shape)
    value_rows = (
        (matmul(first_norm, value_full) + vbias_full.astype(f32)).astype(bf16).reshape(split_shape)
    )
    query_heads, key_heads, value_heads = (
        lax.all_to_all(queries, NARROW, split_axis=2, concat_axis=1, tiled=True),
        lax.all_to_all(key_rows, NARROW, split_axis=2, concat_axis=1, tiled=True),
        lax.all_to_all(value_rows, NARROW, split_axis=2, concat_axis=1, tiled=True),
    )
    query_segs = lax.all_gather(segment_ids, NARROW, axis=1, tiled=True)
    query_pos = key_positions(wide_index * group_rows, group_rows, tokens, narrow_size, wide_size)

    def block_allowed(cycle_step, seg_block):
        source = (wide_index - cycle_step) % wide_size
        key_pos = key_positions(source * group_rows, group_rows, tokens, narrow_size, wide_size)
        return block_mask(query_segs, query_pos, seg_block, key_pos)

    running = (
        jnp.full((batch, heads_local, group_rows), neg_big, f32),
        jnp.zeros((batch, heads_local, group_rows), f32),
        jnp.zeros((batch, group_rows, heads_local, head_dim), f32),
    )
    travelling = (key_heads, value_heads, query_segs)
    received = []
    for cycle_step in range(REACH + 1):
        if cycle_step > 0:
            travelling = shifted((travelling[0], travelling[1], travelling[2]), WIDE, 1)
        received.append(travelling)
        key_block, value_block, seg_block = travelling
        allowed = block_allowed(cycle_step, seg_block)
        running = forward_block(running, query_heads, key_block, value_block, allowed, score_scale)
    row_max, row_total, weighted = running
    attn_out = weighted / jnp.transpose(row_total, (0, 2, 1))[..., None]
    log_total = row_max + jnp.log(row_total)
    mixed = lax.all_to_all(
        attn_out.astype(bf16), NARROW, split_axis=1, concat_axis=2, tiled=True
    ).reshape(-1, model_width)
    middle = inputs + matmul(mixed, out_full) + obias_full.astype(f32)
    mlp_set = (
        lax.all_gather(mlp_gain, BOTH, axis=0, tiled=True),
        lax.all_gather(mlp_shift, BOTH, axis=0, tiled=True),
        lax.all_gather(up_weight, BOTH, axis=0, tiled=True),
        lax.all_gather(up_bias, BOTH, axis=0, tiled=True),
        lax.all_gather(down_weight, BOTH, axis=0, tiled=True),
        lax.all_gather(down_bias, BOTH, axis=0, tiled=True),
    )
    gain_mlp, shift_mlp, up_full, ubias_full, down_full, dbias_full = mlp_set
    second_norm = normalize(middle, gain_mlp.astype(f32), shift_mlp.astype(f32)).astype(bf16)
    inner = matmul(second_norm, up_full) + ubias_full.astype(f32)
    hidden = gelu_exact(inner).astype(bf16)
    output = middle + matmul(hidden, down_full) + dbias_full.astype(f32)
    block_output = output.astype(bf16).reshape(batch, tokens, model_width)
    mlp_set = (
        lax.all_gather(mlp_gain, BOTH, axis=0, tiled=True),
        lax.all_gather(mlp_shift, BOTH, axis=0, tiled=True),
        lax.all_gather(up_weight, BOTH, axis=0, tiled=True),
        lax.all_gather(up_bias, BOTH, axis=0, tiled=True),
        lax.all_gather(down_weight, BOTH, axis=0, tiled=True),
        lax.all_gather(down_bias, BOTH, axis=0, tiled=True),
    )
    gain_mlp, shift_mlp, up_full, ubias_full, down_full, dbias_full = mlp_set
    cotan_rows = cotangent.reshape(-1, model_width)
    down_grad = outer_sum(hidden, cotan_rows)
    dbias_grad = jnp.sum(cotan_rows.astype(f32), axis=0)
    hidden_grad = times_transpose(cotan_rows, down_full)
    gelu_pull = jax.vjp(gelu_exact, inner)[1]
    inner_grad = gelu_pull(hidden_grad)[0].astype(bf16)
    up_grad = outer_sum(second_norm, inner_grad)
    ubias_grad = jnp.sum(inner_grad.astype(f32), axis=0)
    second_grad = times_transpose(inner_grad, up_full)
    mlp_pull = jax.vjp(normalize, middle, gain_mlp.astype(f32), shift_mlp.astype(f32))[1]
    middle_part, mgain_grad, mshift_grad = mlp_pull(second_grad)
    middle_grad = cotan_rows.astype(f32) + middle_part
    mlp_shards = (
        lax.psum_scatter(mgain_grad, BOTH, scatter_dimension=0, tiled=True),
        lax.psum_scatter(mshift_grad, BOTH, scatter_dimension=0, tiled=True),
        lax.psum_scatter(up_grad, BOTH, scatter_dimension=0, tiled=True),
        lax.psum_scatter(ubias_grad, BOTH, scatter_dimension=0, tiled=True),
        lax.psum_scatter(down_grad, BOTH, scatter_dimension=0, tiled=True),
        lax.psum_scatter(dbias_grad, BOTH, scatter_dimension=0, tiled=True),
    )
    attn_set = (
        lax.all_gather(attn_gain, BOTH, axis=0, tiled=True),
        lax.all_gather(attn_shift, BOTH, axis=0, tiled=True),
        lax.all_gather(query_weight, BOTH, axis=0, tiled=True),
        lax.all_gather(query_bias, BOTH, axis=0, tiled=True),
        lax.all_gather(key_weight, BOTH, axis=0, tiled=True),
        lax.all_gather(value_weight, BOTH, axis=0, tiled=True),
        lax.all_gather(value_bias, BOTH, axis=0, tiled=True),
        lax.all_gather(out_weight, BOTH, axis=0, tiled=True),
        lax.all_gather(out_bias, BOTH, axis=0, tiled=True),
    )
    (
        gain_attn,
        shift_attn,
        query_full,
        qbias_full,
        key_full,
        value_full,
        vbias_full,
        out_full,
        obias_full,
    ) = attn_set
    branch_grad = middle_grad.astype(bf16)
    out_grad = outer_sum(mixed, branch_grad)
    obias_grad = jnp.sum(branch_grad.astype(f32), axis=0)
    mixed_grad = times_transpose(branch_grad, out_full).astype(bf16).reshape(split_shape)
    dout_heads = lax.all_to_all(mixed_grad, NARROW, split_axis=2, concat_axis=1, tiled=True)
    delta = jnp.transpose(jnp.sum(dout_heads.astype(f32) * attn_out, axis=-1), (0, 2, 1))
    travelling = (key_heads, value_heads, query_segs)
    received = []
    for cycle_step in range(REACH + 1):
        if cycle_step > 0:
            travelling = shifted((travelling[0], travelling[1], travelling[2]), WIDE, 1)
        received.append(travelling)
    query_grad = jnp.zeros((batch, group_rows, heads_local, head_dim), f32)
    key_terms = []
    value_terms = []
    for cycle_step in range(REACH + 1):
        key_block, value_block, seg_block = received[cycle_step]
        allowed = block_allowed(cycle_step, seg_block)
        query_grad, key_term, value_term = backward_block(
            query_grad,
            query_heads,
            dout_heads,
            key_block,
            value_block,
            allowed,
            delta,
            log_total,
            score_scale,
        )
        key_terms.append(key_term)
        value_terms.append(value_term)
    carried = (key_terms[REACH], value_terms[REACH])
    for cycle_step in range(REACH - 1, -1, -1):
        arrived = shifted((as_sent(carried[0]), as_sent(carried[1])), WIDE, -1)
        carried = (arrived[0] + key_terms[cycle_step], arrived[1] + value_terms[cycle_step])
    key_sum, value_sum = carried
    query_back, key_back, value_back = (
        lax.all_to_all(query_grad.astype(bf16), NARROW, split_axis=1, concat_axis=2, tiled=True),
        lax.all_to_all(key_sum.astype(bf16), NARROW, split_axis=1, concat_axis=2, tiled=True),
        lax.all_to_all(value_sum.astype(bf16), NARROW, split_axis=1, concat_axis=2, tiled=True),
    )
    query_back = query_back.reshape(-1, model_width)
    key_back = key_back.reshape(-1, model_width)
    value_back = value_back.reshape(-1, model_width)
    query_wgrad = outer_sum(first_norm, query_back)
    qbias_grad = jnp.sum(query_back.astype(f32), axis=0)
    key_wgrad = outer_sum(first_norm, key_back)
    value_wgrad = outer_sum(first_norm, value_back)
    vbias_grad = jnp.sum(value_back.astype(f32), axis=0)
    first_grad = (
        times_transpose(query_back, query_full)
        + times_transpose(key_back, key_full)
        + times_transpose(value_back, value_full)
    )
    attn_pull = jax.vjp(normalize, inputs, gain_attn.astype(f32), shift_attn.astype(f32))[1]
    input_part, again_grad, ashift_grad = attn_pull(first_grad)
    input_grad = (middle_grad + input_part).reshape(batch, tokens, model_width)
    attn_shards = (
        lax.psum_scatter(again_grad, BOTH, scatter_dimension=0, tiled=True),
        lax.psum_scatter(ashift_grad, BOTH, scatter_dimension=0, tiled=True),
        lax.psum_scatter(query_wgrad, BOTH, scatter_dimension=0, tiled=True),
        lax.psum_scatter(qbias_grad, BOTH, scatter_dimension=0, tiled=True),
        lax.psum_scatter(key_wgrad, BOTH, scatter_dimension=0, tiled=True),
        lax.psum_scatter(value_wgrad, BOTH, scatter_dimension=0, tiled=True),
        lax.psum_scatter(vbias_grad, BOTH, scatter_dimension=0, tiled=True),
        lax.psum_scatter(out_grad, BOTH, scatter_dimension=0, tiled=True),
        lax.psum_scatter(obias_grad, BOTH, scatter_dimension=0, tiled=True),
    )
    return (
        block_output,
        input_grad,
        attn_shards[0],
        attn_shards[1],
        attn_shards[2],
        attn_shards[3],
        attn_shards[4],
        attn_shards[5],
        attn_shards[6],
        attn_shards[7],
        attn_shards[8],
        mlp_shards[0],
        mlp_shards[1],
        mlp_shards[2],
        mlp_shards[3],
        mlp_shards[4],
        mlp_shards[5],
    )


def flip(value, axis, bits):
    size = lax.axis_size(axis)
    return lax.ppermute(value, axis, [(i, i ^ bits) for i in range(size)])


def at(value, index, dim=0):
    return lax.dynamic_index_in_dim(value, index, dim, keepdims=False)


def cube(wide):
    steps = []
    bits = 1
    while bits < wide:
        steps.append((WIDE, bits))
        bits *= 2
    return steps + [(NARROW, 1), (NARROW, 2)]


def cube_gather(row):
    for axis, bits in cube(lax.axis_size(WIDE)):
        other = flip(row, axis, bits)
        high = (lax.axis_index(axis) & bits) > 0
        row = jnp.concatenate(
            [jnp.where(high, other, row), jnp.where(high, row, other)], axis=0
        )
    return row


def cube_scatter(table):
    wide = lax.axis_size(WIDE)
    steps = cube(wide)
    table = table.reshape((2,) * len(steps) + (table.shape[-1],))
    order = [len(steps) - 2, len(steps) - 1] + list(range(len(steps) - 2))[::-1]
    left = list(range(len(steps)))
    for k in order:
        axis, bits = steps[k]
        dim = len(left) - 1 - left.index(k)
        high = ((lax.axis_index(axis) & bits) > 0).astype(jnp.int32)
        table = at(table, high, dim) + flip(at(table, 1 - high, dim), axis, bits)
        left.remove(k)
    return table


def narrow_gather(own):
    across = flip(own, NARROW, 2)
    beside = flip(own, NARROW, 1)
    return jnp.concatenate([own, beside, across, flip(across, NARROW, 1)], axis=0)


def narrow_scatter(partial):
    f32 = jnp.float32
    parts = partial.reshape(4, -1, partial.shape[-1])
    far = flip(parts[3], NARROW, 1)
    near = flip(parts[1], NARROW, 1)
    passed = (parts[2].astype(f32) + far.astype(f32)).astype(jnp.bfloat16)
    across = flip(passed, NARROW, 2)
    return parts[0].astype(f32) + near.astype(f32) + across.astype(f32)


def hold(value, *events):
    return lax.optimization_barrier((value,) + events)[0]


def bit_of(axis, bits):
    return (lax.axis_index(axis) & bits) > 0


def in_order(relative):
    swap = bit_of(NARROW, 1)
    r = [
        jnp.where(swap, relative[k ^ 1], relative[k]) for k in range(4)
    ]
    swap = bit_of(NARROW, 2)
    return jnp.stack([jnp.where(swap, r[k ^ 2], r[k]) for k in range(4)])


def narrow_swap(block_of):
    me = lax.axis_index(NARROW)
    return in_order([
        flip(block_of(me ^ j), NARROW, j) if j else block_of(me) for j in range(4)
    ])


def pair_swap(block_of):
    me = lax.axis_index(WIDE) & 1
    own, other = block_of(me), flip(block_of(1 - me), WIDE, 1)
    high = me > 0
    return jnp.stack([jnp.where(high, other, own), jnp.where(high, own, other)])


def spread(own):
    half = own.shape[1] // 2
    over_y = flip(own, WIDE, 1)
    over_x = flip(own, NARROW, 2)
    both = jnp.concatenate(
        [flip(over_y[:, :half], NARROW, 2), flip(over_x[:, half:], WIDE, 1)], axis=1
    )
    near = [own, over_x, over_y, both]
    return jnp.concatenate(near + [flip(part, NARROW, 1) for part in near], axis=0)


def fold(partial):
    f32, bf16 = jnp.float32, jnp.bfloat16
    parts = partial.reshape(8, -1, partial.shape[-1])
    half = partial.shape[-1] // 2
    both, over_y, over_x, own = [
        parts[k].astype(f32) + flip(parts[4 + k], NARROW, 1).astype(f32) for k in (3, 2, 1, 0)
    ]
    both = both.astype(bf16)
    first = flip(both[:, :half], WIDE, 1).astype(f32)
    last = flip(both[:, half:], NARROW, 2).astype(f32)
    over_x = jnp.concatenate([over_x[:, :half] + first, over_x[:, half:]], axis=1).astype(bf16)
    over_y = jnp.concatenate([over_y[:, :half], over_y[:, half:] + last], axis=1).astype(bf16)
    return own + flip(over_x, NARROW, 2).astype(f32) + flip(over_y, WIDE, 1).astype(f32)


def columns(wide):
    return [list(range(y, wide, 2)) for y in range(2)]


def z_gather(shard, axis):
    groups = columns(lax.axis_size(WIDE))
    return lax.all_gather(shard, WIDE, axis=axis, tiled=True, axis_index_groups=groups)


def z_scatter(full, axis):
    groups = columns(lax.axis_size(WIDE))
    return lax.psum_scatter(
        full.astype(jnp.bfloat16), WIDE, scatter_dimension=axis, tiled=True, axis_index_groups=groups
    )


def ring_order(wide):
    return list(range(0, wide, 2)) + list(range(wide - 1, 0, -2))


def ring_at(position, wide):
    position = position % wide
    return jnp.where(position < wide // 2, 2 * position, 2 * (wide - 1 - position) + 1)


def ring_position(wide):
    me = lax.axis_index(WIDE)
    return jnp.where(me % 2 == 0, me // 2, wide - 1 - me // 2)


def ring_step(value, by):
    order = ring_order(lax.axis_size(WIDE))
    size = len(order)
    return lax.ppermute(
        value, WIDE, [(order[i], order[(i + by) % size]) for i in range(size)]
    )


def ring_gather(shard, axis):
    wide = lax.axis_size(WIDE)
    here = ring_position(wide)
    shape = list(shard.shape)
    shape.insert(axis, wide)
    full = jnp.zeros(shape, shard.dtype)

    def put(full, piece, position):
        return lax.dynamic_update_slice_in_dim(
            full, jnp.expand_dims(piece, axis), ring_at(position, wide), axis
        )

    full = put(full, shard, here)
    ahead = behind = shard
    for k in range(1, wide // 2 + 1):
        ahead = ring_step(ahead, 1)
        full = put(full, ahead, here - k + wide)
        if k < wide - wide // 2:
            behind = ring_step(behind, -1)
            full = put(full, behind, here + k)
    return full


def ring_scatter(full, axis):
    wide = lax.axis_size(WIDE)
    here = ring_position(wide)
    bf16, f32 = jnp.bfloat16, jnp.float32

    def local(position):
        return at(full, ring_at(position + wide, wide), axis).astype(f32)

    half = wide // 2
    ahead = behind = None
    for k in range(half, 0, -1):
        term = local(here + k)
        term = term if ahead is None else term + ahead
        ahead = ring_step(term.astype(bf16), 1).astype(f32)
        if k < wide - half:
            term = local(here - k)
            term = term if behind is None else term + behind
            behind = ring_step(term.astype(bf16), -1).astype(f32)
    return local(here) + ahead + behind


def wide_swap(parts):
    return [parts[0]] + [flip(parts[d], WIDE, d) for d in range(1, parts.shape[0])]


def wide_gather(shard, axis):
    return lax.all_gather(shard, WIDE, axis=axis, tiled=True)


def wide_scatter(full, axis):
    return lax.psum_scatter(full.astype(jnp.bfloat16), WIDE, scatter_dimension=axis, tiled=True)


def vmem_specs(count):
    return [pl.BlockSpec(memory_space=pltpu.VMEM)] * count


SMEM_SPEC = pl.BlockSpec(memory_space=pltpu.SMEM)
BIG = pltpu.CompilerParams(vmem_limit_bytes=48 << 20)
CONTRACT_LAST = (((1,), (1,)), ((), ()))
CONTRACT_FIRST = (((0,), (0,)), ((), ()))


def project_kernel(me_ref, rows_ref, weight_ref, bias_ref, out_ref, *, heads, by_last):
    me = me_ref[1]
    if by_last:
        acc = lax.dot_general(
            rows_ref[...], weight_ref[...], CONTRACT_LAST, preferred_element_type=jnp.float32
        )
    else:
        acc = jnp.dot(rows_ref[...], weight_ref[...], preferred_element_type=jnp.float32)
    acc = (acc + bias_ref[...]).astype(jnp.bfloat16)
    units, parts, _, tokens, head_dim = out_ref.shape
    for unit in range(units):
        b, h = divmod(unit, heads)
        for part in range(parts):
            c = (part * heads + h) * head_dim
            out_ref[unit ^ me, part, 0] = acc[b * tokens : (b + 1) * tokens, c : c + head_dim]


def project(me, rows, weight, bias, units, parts, heads, tokens, by_last):
    blocks, width = 4, rows.shape[1]
    head_dim = bias.shape[0] // (parts * heads)
    step = rows.shape[0] // blocks
    return pl.pallas_call(
        functools.partial(project_kernel, heads=heads, by_last=by_last),
        grid=(blocks,),
        out_shape=jax.ShapeDtypeStruct((units, parts, blocks, tokens, head_dim), jnp.bfloat16),
        in_specs=[
            SMEM_SPEC,
            pl.BlockSpec((step, width), lambda i: (i, 0)),
            pl.BlockSpec(weight.shape, lambda i: (0, 0), pipeline_mode=pl.Buffered(1)),
            pl.BlockSpec((1, bias.shape[0]), lambda i: (0, 0)),
        ],
        out_specs=pl.BlockSpec(
            (units, parts, 1, tokens, head_dim), lambda i: (0, 0, i, 0, 0)
        ),
        compiler_params=BIG,
        name="project",
    )(me, rows, weight, bias.reshape(1, -1))


def unproject_kernel(me_ref, *refs, heads, by_last):
    units = len(refs) - 4
    pieces, weight_ref, out_ref, rows_ref, held = refs[:units], *refs[units:]
    me = me_ref[1]
    for d in range(units):
        held[d ^ me] = pieces[d][:, 0]
    parts = held.shape[1]
    rows = jnp.concatenate(
        [
            jnp.concatenate(
                [held[b * heads + h, part] for part in range(parts) for h in range(heads)], axis=1
            )
            for b in range(units // heads)
        ],
        axis=0,
    )
    rows_ref[...] = rows
    if by_last:
        acc = lax.dot_general(
            rows, weight_ref[...], CONTRACT_LAST, preferred_element_type=jnp.float32
        )
    else:
        acc = jnp.dot(rows, weight_ref[...], preferred_element_type=jnp.float32)
    out_ref[...] = acc.astype(jnp.bfloat16)


def unproject(me, pieces, weight, heads, by_last):
    units = len(pieces)
    parts, blocks, tokens, head_dim = pieces[0].shape
    step = tokens * units // heads
    inner = parts * heads * head_dim
    width = weight.shape[0] if by_last else weight.shape[1]
    return pl.pallas_call(
        functools.partial(unproject_kernel, heads=heads, by_last=by_last),
        grid=(blocks,),
        out_shape=(
            jax.ShapeDtypeStruct((blocks * step, width), jnp.bfloat16),
            jax.ShapeDtypeStruct((blocks * step, inner), jnp.bfloat16),
        ),
        in_specs=[SMEM_SPEC]
        + [pl.BlockSpec((parts, 1, tokens, head_dim), lambda i: (0, i, 0, 0))] * units
        + [pl.BlockSpec(weight.shape, lambda i: (0, 0), pipeline_mode=pl.Buffered(1))],
        out_specs=(
            pl.BlockSpec((step, width), lambda i: (i, 0)),
            pl.BlockSpec((step, inner), lambda i: (i, 0)),
        ),
        scratch_shapes=[pltpu.VMEM((units, parts, tokens, head_dim), jnp.bfloat16)],
        compiler_params=BIG,
        name="unproject",
    )(me, *pieces, weight)


def mask_of(segc_ref, segr_ref, i, lo):
    keys = 512 * (i + 1 - lo)
    same = segc_ref[i] == segr_ref[:, 512 * lo : 512 * (i + 1)]
    rows = lax.broadcasted_iota(jnp.int32, (512, keys), 0) + 512 * (i - lo)
    cols = lax.broadcasted_iota(jnp.int32, (512, keys), 1)
    return jnp.logical_and(same, cols <= rows)


def collect(me_ref, pieces, held):
    for d, piece in enumerate(pieces):
        for j in range(4):
            held[d ^ me_ref[1], :, j ^ me_ref[0]] = piece[:, j]


def take(held, part, first, last, half):
    blocks = [
        held[4 * (i % half) : 4 * (i % half) + 4, part, i // half].reshape(512, -1)
        for i in range(first, last + 1)
    ]
    return blocks[0] if len(blocks) == 1 else jnp.concatenate(blocks, axis=0)


def give(me_ref, out_ref, part, i, half, rows):
    rows = rows.astype(out_ref.dtype).reshape(4, 128, -1)
    for c in range(4):
        out_ref[(4 * (i % half) + c) ^ me_ref[1], part, (i // half) ^ me_ref[0]] = rows[c]


def fwd_kernel(me_ref, segc_ref, segr_ref, *refs, blocks, scale2):
    pieces, (out_ref, lse_ref, held) = refs[:-3], refs[-3:]
    half = blocks // 4
    collect(me_ref, pieces, held)
    for i in range(blocks):
        lo = max(i - 1, 0)
        q = take(held, 0, i, i, half)
        k = take(held, 1, lo, i, half)
        v = take(held, 2, lo, i, half)
        s = lax.dot_general(q, k, CONTRACT_LAST, preferred_element_type=jnp.float32)
        s = jnp.where(mask_of(segc_ref, segr_ref, i, lo), s * scale2, neg_big)
        m = jnp.max(s, axis=-1, keepdims=True)
        p = jnp.exp2(s - m)
        total = jnp.sum(p, axis=-1, keepdims=True)
        o = jnp.dot(p.astype(jnp.bfloat16), v, preferred_element_type=jnp.float32)
        give(me_ref, out_ref, 0, i, half, o / total)
        lse_ref[i] = m + jnp.log2(total)


def bwd_kernel(me_ref, segc_ref, segr_ref, lse_ref, *refs, blocks, scale, scale2):
    grad_ref, held, held_do, dk_acc, dv_acc = refs[-5:]
    pieces, douts = refs[: (len(refs) - 5) // 2], refs[(len(refs) - 5) // 2 : -5]
    half = blocks // 4
    f32 = jnp.float32
    collect(me_ref, pieces, held)
    collect(me_ref, douts, held_do)
    for i in range(blocks):
        lo = max(i - 1, 0)
        q = take(held, 0, i, i, half)
        k = take(held, 1, lo, i, half)
        v = take(held, 2, lo, i, half)
        do = take(held_do, 0, i, i, half)
        s = lax.dot_general(q, k, CONTRACT_LAST, preferred_element_type=f32)
        s = jnp.where(mask_of(segc_ref, segr_ref, i, lo), s * scale2, neg_big)
        p = jnp.exp2(s - lse_ref[i])
        dp = lax.dot_general(do, v, CONTRACT_LAST, preferred_element_type=f32)
        t = p * dp
        delta = jnp.sum(t, axis=-1, keepdims=True)
        ds = (t - p * delta).astype(jnp.bfloat16)
        give(me_ref, grad_ref, 0, i, half, jnp.dot(ds, k, preferred_element_type=f32) * scale)
        dk = lax.dot_general(ds, q, CONTRACT_FIRST, preferred_element_type=f32)
        dv = lax.dot_general(
            p.astype(jnp.bfloat16), do, CONTRACT_FIRST, preferred_element_type=f32
        )
        if i > 0:
            give(me_ref, grad_ref, 1, i - 1, half, (dk_acc[...] + dk[:512]) * scale)
            give(me_ref, grad_ref, 2, i - 1, half, dv_acc[...] + dv[:512])
        if i == blocks - 1:
            give(me_ref, grad_ref, 1, i, half, dk[-512:] * scale)
            give(me_ref, grad_ref, 2, i, half, dv[-512:])
        else:
            dk_acc[...] = dk[-512:]
            dv_acc[...] = dv[-512:]


def attend_fwd(me, segc, segr, pieces):
    blocks, units = segc.shape[0], len(pieces)
    parts, narrow, rows, width = pieces[0].shape
    scale2 = math.log2(math.e) / math.sqrt(width)
    return pl.pallas_call(
        functools.partial(fwd_kernel, blocks=blocks, scale2=scale2),
        out_shape=(
            jax.ShapeDtypeStruct((units, 1, narrow, rows, width), jnp.bfloat16),
            jax.ShapeDtypeStruct((blocks, 512, 1), jnp.float32),
        ),
        in_specs=[SMEM_SPEC] + vmem_specs(2 + units),
        out_specs=tuple(vmem_specs(2)),
        scratch_shapes=[pltpu.VMEM((units, parts, narrow, rows, width), jnp.bfloat16)],
        compiler_params=BIG,
        name="attend_fwd",
    )(me, segc, segr, *pieces)


def attend_bwd(me, segc, segr, lse, pieces, douts):
    blocks, units = segc.shape[0], len(pieces)
    parts, narrow, rows, width = pieces[0].shape
    scale = 1.0 / math.sqrt(width)
    shape = (units, parts, narrow, rows, width)
    return pl.pallas_call(
        functools.partial(
            bwd_kernel, blocks=blocks, scale=scale, scale2=scale * math.log2(math.e)
        ),
        out_shape=jax.ShapeDtypeStruct(shape, jnp.bfloat16),
        in_specs=[SMEM_SPEC] + vmem_specs(3 + 2 * units),
        out_specs=vmem_specs(1)[0],
        scratch_shapes=[
            pltpu.VMEM(shape, jnp.bfloat16),
            pltpu.VMEM((units, 1, narrow, rows, width), jnp.bfloat16),
            pltpu.VMEM((512, width), jnp.float32),
            pltpu.VMEM((512, width), jnp.float32),
        ],
        compiler_params=BIG,
        name="attend_bwd",
    )(me, segc, segr, lse, *pieces, *douts)


def ff_kernel(rows_ref, weight_ref, bias_ref, pull_ref, hidden_ref, grad_ref, sum_ref):
    step = 256
    total = jnp.zeros((1, weight_ref.shape[1]), jnp.float32)
    for r in range(0, rows_ref.shape[0], step):
        x = jnp.dot(rows_ref[r : r + step], weight_ref[...], preferred_element_type=jnp.float32)
        x = x + bias_ref[...]
        below = 0.5 * (1.0 + lax.erf(x * math.sqrt(0.5)))
        hidden_ref[r : r + step] = (x * below).astype(jnp.bfloat16)
        slope = below + x * (jnp.exp(-0.5 * x * x) * (1.0 / math.sqrt(2.0 * math.pi)))
        grad = (pull_ref[r : r + step] * slope).astype(jnp.bfloat16)
        grad_ref[r : r + step] = grad
        total = total + jnp.sum(grad.astype(jnp.float32), axis=0, keepdims=True)
    sum_ref[...] = total


def feed_forward(rows, weight, bias, pull):
    count, width = rows.shape
    inner = weight.shape[1]
    step = 256
    return pl.pallas_call(
        ff_kernel,
        grid=(inner // step,),
        out_shape=(
            jax.ShapeDtypeStruct((count, inner), jnp.bfloat16),
            jax.ShapeDtypeStruct((count, inner), jnp.bfloat16),
            jax.ShapeDtypeStruct((1, inner), jnp.float32),
        ),
        in_specs=[
            pl.BlockSpec((count, width), lambda i: (0, 0), pipeline_mode=pl.Buffered(1)),
            pl.BlockSpec((width, step), lambda i: (0, i)),
            pl.BlockSpec((1, step), lambda i: (0, i)),
            pl.BlockSpec((count, step), lambda i: (0, i)),
        ],
        out_specs=(
            pl.BlockSpec((count, step), lambda i: (0, i)),
            pl.BlockSpec((count, step), lambda i: (0, i)),
            pl.BlockSpec((1, step), lambda i: (0, i)),
        ),
        compiler_params=BIG,
        name="feed_forward",
    )(rows, weight, bias.reshape(1, -1), pull)


def on_device(
    block_input,
    segment_ids,
    cotangent,
    attn_gain,
    attn_shift,
    query_weight,
    query_bias,
    key_weight,
    value_weight,
    value_bias,
    out_weight,
    out_bias,
    mlp_gain,
    mlp_shift,
    up_weight,
    up_bias,
    down_weight,
    down_bias,
):
    f32 = jnp.float32
    bf16 = jnp.bfloat16
    batch, tokens, width = block_input.shape
    narrow = lax.axis_size(NARROW)
    wide = lax.axis_size(WIDE)
    me_n = lax.axis_index(NARROW)
    me_w = lax.axis_index(WIDE)
    me = jnp.stack([me_n, me_w]).astype(jnp.int32)
    rows = batch * tokens
    heads = HEADS // narrow
    head_dim = width // HEADS
    cols = heads * head_dim
    shard = width // (narrow * wide)
    deep = wide // 2
    ff_shard = up_bias.shape[0]
    ff_local = ff_shard * deep
    me_y = me_w & 1

    smalls = [
        attn_gain, attn_shift, out_bias, mlp_gain, mlp_shift, down_bias, query_bias, value_bias, up_bias
    ]
    ids = segment_ids.astype(bf16).reshape(-1)
    small = cube_gather(jnp.concatenate(smalls + [ids])[None])
    ids = small[:, -batch * tokens :].reshape(narrow * wide, batch, tokens)
    unit_ids = at(ids, me_w // heads, 1).reshape(-1).astype(jnp.int32)
    segc = unit_ids.reshape(-1, 512, 1)
    segr = unit_ids.reshape(1, -1)

    def full_vector(k):
        return small[:, k * shard : (k + 1) * shard].reshape(-1).astype(f32)

    gain_attn, shift_attn, obias, gain_mlp, shift_mlp, dbias = [full_vector(k) for k in range(6)]
    mine = lax.dynamic_slice_in_dim(small, me_n * wide, wide, 0)
    qbias = mine[:, 6 * shard : 7 * shard].reshape(-1).astype(f32)
    vbias = mine[:, 7 * shard : 8 * shard].reshape(-1).astype(f32)
    ubias = mine[:, 8 * shard : 8 * shard + ff_shard].reshape(deep, 2, ff_shard)
    ubias = at(ubias, me_y, 1).reshape(-1).astype(f32)
    qkv_bias = jnp.concatenate([qbias, jnp.zeros_like(qbias), vbias])

    def qkv_block(n):
        return jnp.concatenate(
            [
                lax.dynamic_slice_in_dim(weight, n * cols, cols, 1)
                for weight in (query_weight, key_weight, value_weight)
            ],
            axis=1,
        )

    qkv_w = ring_gather(narrow_swap(qkv_block), 1).reshape(width, 3 * cols)
    out_w = wide_gather(out_weight, 0)

    inputs = block_input.astype(f32).reshape(rows, width)
    first_norm = narrow_gather(normalize(inputs, gain_attn, shift_attn).astype(bf16))
    cotan_own = cotangent.reshape(rows, width)
    cotan = spread(hold(cotan_own, first_norm))

    down_w = z_gather(hold(down_weight, qkv_w), 0)
    up_cols = hold(up_weight, first_norm).reshape(shard, narrow, deep, 2, ff_shard)
    up_shard = pair_swap(lambda y: at(up_cols, y, 3).reshape(shard, narrow, ff_local))
    up_pair = up_shard
    up_shard = narrow_swap(lambda n: at(up_pair, n, 2))
    up_shard = up_shard.reshape(narrow, 2 * shard, ff_local)
    up_w = z_gather(hold(up_shard, qkv_w), 1).reshape(width, ff_local)

    sent = project(me, first_norm, qkv_w, qkv_bias, wide, 3, heads, tokens, False)
    qkv = wide_swap(sent)
    unit_out, lse = attend_fwd(me, segc, segr, qkv)
    partial, mixed = unproject(me, wide_swap(unit_out), out_w, heads, False)
    middle = inputs + narrow_scatter(partial) + obias

    hidden_grad = times_transpose(cotan, down_w)
    second_norm = spread(normalize(middle, gain_mlp, shift_mlp).astype(bf16))
    hidden, inner_grad, ubias_grad = feed_forward(second_norm, up_w, ubias, hidden_grad)
    second_part = times_transpose(inner_grad, up_w).astype(bf16)
    second_grad = fold(second_part)
    hidden_late = hold(hidden, second_part)
    down_grad = z_scatter(outer_sum(hidden_late, cotan), 0)
    up_grad = outer_sum(second_norm, hold(inner_grad, second_part))
    up_grad = z_scatter(up_grad.reshape(narrow, 2 * deep * shard, ff_local), 1)
    mlp_pull = jax.vjp(normalize, middle, gain_mlp, shift_mlp)[1]
    middle_part, mgain_grad, mshift_grad = mlp_pull(second_grad)
    dbias_grad = jnp.sum(cotan_own.astype(f32), axis=0)
    middle_grad = cotan_own.astype(f32) + middle_part

    branch_own = middle_grad.astype(bf16)
    obias_grad = jnp.sum(branch_own.astype(f32), axis=0)
    branch = narrow_gather(branch_own)
    no_bias = jnp.zeros((cols,), f32)
    sent = project(me, branch, out_w, no_bias, wide, 1, heads, tokens, True)
    unit_grads = attend_bwd(me, segc, segr, lse, qkv, wide_swap(sent))
    out_grad = wide_scatter(outer_sum(mixed, hold(branch, sent)), 0)
    output = middle + fold(matmul(hold(hidden, unit_grads), down_w).astype(bf16)) + dbias
    block_output = output.astype(bf16).reshape(batch, tokens, width)
    up_grad = up_grad.reshape(narrow, 2, shard, ff_local)
    up_rows = up_grad
    up_swapped = narrow_swap(lambda n: at(up_rows, n))
    up_back = pair_swap(lambda y: at(up_swapped, y, 1))
    up_back = up_back.reshape(2, narrow, shard, deep, ff_shard).transpose(2, 1, 3, 0, 4)
    up_back = up_back.reshape(shard, -1)
    partial, back = unproject(me, wide_swap(unit_grads), qkv_w, heads, True)
    first_grad = narrow_scatter(partial)
    qkv_grad = outer_sum(first_norm, back).astype(bf16).reshape(narrow, wide, shard, 3 * cols)
    qkv_grad = ring_scatter(qkv_grad, 1).astype(bf16)
    qkv_rows = qkv_grad
    qkv_grad = narrow_swap(lambda n: at(qkv_rows, n)).reshape(narrow, shard, 3, cols)
    qkv_grad = qkv_grad.transpose(2, 1, 0, 3).reshape(3, shard, width).astype(f32)
    back_sums = jnp.sum(back.astype(f32), axis=0)
    attn_pull = jax.vjp(normalize, inputs, gain_attn, shift_attn)[1]
    input_part, again_grad, ashift_grad = attn_pull(first_grad)
    input_grad = (middle_grad + input_part).reshape(batch, tokens, width)

    fulls = [again_grad, ashift_grad, obias_grad, mgain_grad, mshift_grad, dbias_grad]
    fulls = jnp.concatenate([v.reshape(narrow * wide, shard) for v in fulls], axis=1)
    ubias_rows = jnp.zeros((deep, 2, ff_shard), f32)
    ubias_rows = lax.dynamic_update_slice_in_dim(
        ubias_rows, ubias_grad.reshape(deep, 1, ff_shard), me_y, 1
    )
    slices = [back_sums[:cols], back_sums[2 * cols :], ubias_rows]
    slices = jnp.concatenate([v.reshape(wide, -1) for v in slices], axis=1)
    placed = jnp.zeros((narrow * wide, slices.shape[1]), f32)
    placed = lax.dynamic_update_slice_in_dim(placed, slices, me_n * wide, 0)
    vectors = cube_scatter(jnp.concatenate([fulls, placed], axis=1))

    def vector(k):
        return vectors[k * shard : (k + 1) * shard]

    return (
        block_output,
        input_grad,
        vector(0),
        vector(1),
        qkv_grad[0],
        vector(6),
        qkv_grad[1],
        qkv_grad[2],
        vector(7),
        out_grad.astype(f32),
        vector(2),
        vector(3),
        vector(4),
        up_back.astype(f32),
        vectors[8 * shard :],
        down_grad.astype(f32),
        vector(5),
    )


def body_of(mesh):
    def body(*args):
        batch, tokens, width = args[0].shape
        narrow, wide = mesh.shape[NARROW], mesh.shape[WIDE]
        one_unit = batch * (HEADS // narrow) == wide and tokens == 128 and narrow == 4
        return (on_device if one_unit else on_device_ring)(*args)

    return body


def solution(mesh):
    return jax.shard_map(
        body_of(mesh),
        mesh=mesh,
        in_specs=(
            P(None, BOTH, None),
            P(None, BOTH),
            P(None, BOTH, None),
            P(BOTH),
            P(BOTH),
            P(BOTH, None),
            P(BOTH),
            P(BOTH, None),
            P(BOTH, None),
            P(BOTH),
            P(BOTH, None),
            P(BOTH),
            P(BOTH),
            P(BOTH),
            P(BOTH, None),
            P(BOTH),
            P(BOTH, None),
            P(BOTH),
        ),
        out_specs=(
            P(None, BOTH, None),
            P(None, BOTH, None),
            P(BOTH),
            P(BOTH),
            P(BOTH, None),
            P(BOTH),
            P(BOTH, None),
            P(BOTH, None),
            P(BOTH),
            P(BOTH, None),
            P(BOTH),
            P(BOTH),
            P(BOTH),
            P(BOTH, None),
            P(BOTH),
            P(BOTH, None),
            P(BOTH),
        ),
        check_vma=False,
    )
```

```python
import functools
import math
import jax
import jax.numpy as jnp
from jax import lax
from jax.experimental import pallas as pl
from jax.experimental.pallas import tpu as pltpu
from jax.sharding import PartitionSpec as P
HEADS = 16
NARROW, WIDE = "narrow", "wide"
BOTH = (NARROW, WIDE)
REACH = 4
eps = 1e-05
neg_big = -1e30


def shifted(value, axis, by):
    devices = lax.axis_size(axis)
    return lax.ppermute(value, axis, [(i, (i + by) % devices) for i in range(devices)])


def as_sent(value):

    def short(part):
        return part.astype(jnp.bfloat16) if part.dtype == jnp.float32 else part

    return jax.tree.map(short, value)


def normalize(values, gain, shift):
    center = jnp.mean(values, axis=-1, keepdims=True)
    centered = values - center
    spread = jnp.mean(centered * centered, axis=-1, keepdims=True)
    return centered * lax.rsqrt(spread + eps) * gain + shift


def gelu_exact(values):
    return jax.nn.gelu(values, approximate=False)


def matmul(left, right):
    return jnp.dot(left, right, preferred_element_type=jnp.float32)


def outer_sum(left, right):
    return lax.dot_general(
        left, right, (((0,), (0,)), ((), ())), preferred_element_type=jnp.float32
    )


def times_transpose(left, right):
    return lax.dot_general(
        left, right, (((1,), (1,)), ((), ())), preferred_element_type=jnp.float32
    )


def key_positions(first_row, row_count, tokens, narrow_size, wide_size):
    row_ids = first_row + jnp.arange(row_count, dtype=jnp.int32)
    source_wide = row_ids // (tokens * narrow_size)
    source_narrow = row_ids // tokens % narrow_size
    return (source_narrow * wide_size + source_wide) * tokens + row_ids % tokens


def block_mask(query_segs, query_pos, key_segs, key_pos):
    same_doc = query_segs[:, :, None] == key_segs[:, None, :]
    causal = key_pos[None, None, :] <= query_pos[None, :, None]
    return jnp.logical_and(same_doc, causal)


def raw_scores(query_rows, key_rows, score_scale, allowed):
    scores = (
        jnp.einsum("bqhd,bkhd->bhqk", query_rows, key_rows, preferred_element_type=jnp.float32)
        * score_scale
    )
    return jnp.where(allowed[:, None], scores, neg_big)


def forward_block(running, query_heads, key_block, value_block, allowed, score_scale):
    row_max, row_total, weighted = running
    scores = raw_scores(query_heads, key_block, score_scale, allowed)
    new_max = jnp.maximum(row_max, jnp.max(scores, axis=-1))
    rescale = jnp.exp(row_max - new_max)
    exp_terms = jnp.where(allowed[:, None], jnp.exp(scores - new_max[..., None]), 0.0)
    row_total = row_total * rescale + jnp.sum(exp_terms, axis=-1)
    added = jnp.einsum(
        "bhqk,bkhd->bqhd",
        exp_terms.astype(jnp.bfloat16),
        value_block,
        preferred_element_type=jnp.float32,
    )
    weighted = weighted * jnp.transpose(rescale, (0, 2, 1))[..., None] + added
    return (new_max, row_total, weighted)


def backward_block(
    query_grad,
    query_heads,
    dout_heads,
    key_block,
    value_block,
    allowed,
    delta,
    log_total,
    score_scale,
):
    scores = raw_scores(query_heads, key_block, score_scale, allowed)
    attn_probs = jnp.where(allowed[:, None], jnp.exp(scores - log_total[..., None]), 0.0)
    prob_grad = jnp.einsum(
        "bqhd,bkhd->bhqk", dout_heads, value_block, preferred_element_type=jnp.float32
    )
    score_grad = (attn_probs * (prob_grad - delta[..., None])).astype(jnp.bfloat16)
    query_grad = query_grad + score_scale * jnp.einsum(
        "bhqk,bkhd->bqhd", score_grad, key_block, preferred_element_type=jnp.float32
    )
    key_grad = score_scale * jnp.einsum(
        "bhqk,bqhd->bkhd", score_grad, query_heads, preferred_element_type=jnp.float32
    )
    value_grad = jnp.einsum(
        "bhqk,bqhd->bkhd",
        attn_probs.astype(jnp.bfloat16),
        dout_heads,
        preferred_element_type=jnp.float32,
    )
    return (query_grad, key_grad, value_grad)


def on_device_ring(
    block_input,
    segment_ids,
    cotangent,
    attn_gain,
    attn_shift,
    query_weight,
    query_bias,
    key_weight,
    value_weight,
    value_bias,
    out_weight,
    out_bias,
    mlp_gain,
    mlp_shift,
    up_weight,
    up_bias,
    down_weight,
    down_bias,
):
    batch, tokens, model_width = block_input.shape
    narrow_size = lax.axis_size(NARROW)
    wide_size = lax.axis_size(WIDE)
    wide_index = lax.axis_index(WIDE)
    group_rows = tokens * narrow_size
    heads_local = HEADS // narrow_size
    head_dim = model_width // HEADS
    score_scale = 1.0 / math.sqrt(head_dim)
    f32 = jnp.float32
    bf16 = jnp.bfloat16
    attn_set = (
        lax.all_gather(attn_gain, BOTH, axis=0, tiled=True),
        lax.all_gather(attn_shift, BOTH, axis=0, tiled=True),
        lax.all_gather(query_weight, BOTH, axis=0, tiled=True),
        lax.all_gather(query_bias, BOTH, axis=0, tiled=True),
        lax.all_gather(key_weight, BOTH, axis=0, tiled=True),
        lax.all_gather(value_weight, BOTH, axis=0, tiled=True),
        lax.all_gather(value_bias, BOTH, axis=0, tiled=True),
        lax.all_gather(out_weight, BOTH, axis=0, tiled=True),
        lax.all_gather(out_bias, BOTH, axis=0, tiled=True),
    )
    (
        gain_attn,
        shift_attn,
        query_full,
        qbias_full,
        key_full,
        value_full,
        vbias_full,
        out_full,
        obias_full,
    ) = attn_set
    inputs = block_input.astype(f32).reshape(-1, model_width)
    first_norm = normalize(inputs, gain_attn.astype(f32), shift_attn.astype(f32)).astype(bf16)
    split_shape = (batch, tokens, HEADS, head_dim)
    queries = (
        (matmul(first_norm, query_full) + qbias_full.astype(f32)).astype(bf16).reshape(split_shape)
    )
    key_rows = matmul(first_norm, key_full).astype(bf16).reshape(split_shape)
    value_rows = (
        (matmul(first_norm, value_full) + vbias_full.astype(f32)).astype(bf16).reshape(split_shape)
    )
    query_heads, key_heads, value_heads = (
        lax.all_to_all(queries, NARROW, split_axis=2, concat_axis=1, tiled=True),
        lax.all_to_all(key_rows, NARROW, split_axis=2, concat_axis=1, tiled=True),
        lax.all_to_all(value_rows, NARROW, split_axis=2, concat_axis=1, tiled=True),
    )
    query_segs = lax.all_gather(segment_ids, NARROW, axis=1, tiled=True)
    query_pos = key_positions(wide_index * group_rows, group_rows, tokens, narrow_size, wide_size)

    def block_allowed(cycle_step, seg_block):
        source = (wide_index - cycle_step) % wide_size
        key_pos = key_positions(source * group_rows, group_rows, tokens, narrow_size, wide_size)
        return block_mask(query_segs, query_pos, seg_block, key_pos)

    running = (
        jnp.full((batch, heads_local, group_rows), neg_big, f32),
        jnp.zeros((batch, heads_local, group_rows), f32),
        jnp.zeros((batch, group_rows, heads_local, head_dim), f32),
    )
    travelling = (key_heads, value_heads, query_segs)
    received = []
    for cycle_step in range(REACH + 1):
        if cycle_step > 0:
            travelling = shifted((travelling[0], travelling[1], travelling[2]), WIDE, 1)
        received.append(travelling)
        key_block, value_block, seg_block = travelling
        allowed = block_allowed(cycle_step, seg_block)
        running = forward_block(running, query_heads, key_block, value_block, allowed, score_scale)
    row_max, row_total, weighted = running
    attn_out = weighted / jnp.transpose(row_total, (0, 2, 1))[..., None]
    log_total = row_max + jnp.log(row_total)
    mixed = lax.all_to_all(
        attn_out.astype(bf16), NARROW, split_axis=1, concat_axis=2, tiled=True
    ).reshape(-1, model_width)
    middle = inputs + matmul(mixed, out_full) + obias_full.astype(f32)
    mlp_set = (
        lax.all_gather(mlp_gain, BOTH, axis=0, tiled=True),
        lax.all_gather(mlp_shift, BOTH, axis=0, tiled=True),
        lax.all_gather(up_weight, BOTH, axis=0, tiled=True),
        lax.all_gather(up_bias, BOTH, axis=0, tiled=True),
        lax.all_gather(down_weight, BOTH, axis=0, tiled=True),
        lax.all_gather(down_bias, BOTH, axis=0, tiled=True),
    )
    gain_mlp, shift_mlp, up_full, ubias_full, down_full, dbias_full = mlp_set
    second_norm = normalize(middle, gain_mlp.astype(f32), shift_mlp.astype(f32)).astype(bf16)
    inner = matmul(second_norm, up_full) + ubias_full.astype(f32)
    hidden = gelu_exact(inner).astype(bf16)
    output = middle + matmul(hidden, down_full) + dbias_full.astype(f32)
    block_output = output.astype(bf16).reshape(batch, tokens, model_width)
    mlp_set = (
        lax.all_gather(mlp_gain, BOTH, axis=0, tiled=True),
        lax.all_gather(mlp_shift, BOTH, axis=0, tiled=True),
        lax.all_gather(up_weight, BOTH, axis=0, tiled=True),
        lax.all_gather(up_bias, BOTH, axis=0, tiled=True),
        lax.all_gather(down_weight, BOTH, axis=0, tiled=True),
        lax.all_gather(down_bias, BOTH, axis=0, tiled=True),
    )
    gain_mlp, shift_mlp, up_full, ubias_full, down_full, dbias_full = mlp_set
    cotan_rows = cotangent.reshape(-1, model_width)
    down_grad = outer_sum(hidden, cotan_rows)
    dbias_grad = jnp.sum(cotan_rows.astype(f32), axis=0)
    hidden_grad = times_transpose(cotan_rows, down_full)
    gelu_pull = jax.vjp(gelu_exact, inner)[1]
    inner_grad = gelu_pull(hidden_grad)[0].astype(bf16)
    up_grad = outer_sum(second_norm, inner_grad)
    ubias_grad = jnp.sum(inner_grad.astype(f32), axis=0)
    second_grad = times_transpose(inner_grad, up_full)
    mlp_pull = jax.vjp(normalize, middle, gain_mlp.astype(f32), shift_mlp.astype(f32))[1]
    middle_part, mgain_grad, mshift_grad = mlp_pull(second_grad)
    middle_grad = cotan_rows.astype(f32) + middle_part
    mlp_shards = (
        lax.psum_scatter(mgain_grad, BOTH, scatter_dimension=0, tiled=True),
        lax.psum_scatter(mshift_grad, BOTH, scatter_dimension=0, tiled=True),
        lax.psum_scatter(up_grad, BOTH, scatter_dimension=0, tiled=True),
        lax.psum_scatter(ubias_grad, BOTH, scatter_dimension=0, tiled=True),
        lax.psum_scatter(down_grad, BOTH, scatter_dimension=0, tiled=True),
        lax.psum_scatter(dbias_grad, BOTH, scatter_dimension=0, tiled=True),
    )
    attn_set = (
        lax.all_gather(attn_gain, BOTH, axis=0, tiled=True),
        lax.all_gather(attn_shift, BOTH, axis=0, tiled=True),
        lax.all_gather(query_weight, BOTH, axis=0, tiled=True),
        lax.all_gather(query_bias, BOTH, axis=0, tiled=True),
        lax.all_gather(key_weight, BOTH, axis=0, tiled=True),
        lax.all_gather(value_weight, BOTH, axis=0, tiled=True),
        lax.all_gather(value_bias, BOTH, axis=0, tiled=True),
        lax.all_gather(out_weight, BOTH, axis=0, tiled=True),
        lax.all_gather(out_bias, BOTH, axis=0, tiled=True),
    )
    (
        gain_attn,
        shift_attn,
        query_full,
        qbias_full,
        key_full,
        value_full,
        vbias_full,
        out_full,
        obias_full,
    ) = attn_set
    branch_grad = middle_grad.astype(bf16)
    out_grad = outer_sum(mixed, branch_grad)
    obias_grad = jnp.sum(branch_grad.astype(f32), axis=0)
    mixed_grad = times_transpose(branch_grad, out_full).astype(bf16).reshape(split_shape)
    dout_heads = lax.all_to_all(mixed_grad, NARROW, split_axis=2, concat_axis=1, tiled=True)
    delta = jnp.transpose(jnp.sum(dout_heads.astype(f32) * attn_out, axis=-1), (0, 2, 1))
    travelling = (key_heads, value_heads, query_segs)
    received = []
    for cycle_step in range(REACH + 1):
        if cycle_step > 0:
            travelling = shifted((travelling[0], travelling[1], travelling[2]), WIDE, 1)
        received.append(travelling)
    query_grad = jnp.zeros((batch, group_rows, heads_local, head_dim), f32)
    key_terms = []
    value_terms = []
    for cycle_step in range(REACH + 1):
        key_block, value_block, seg_block = received[cycle_step]
        allowed = block_allowed(cycle_step, seg_block)
        query_grad, key_term, value_term = backward_block(
            query_grad,
            query_heads,
            dout_heads,
            key_block,
            value_block,
            allowed,
            delta,
            log_total,
            score_scale,
        )
        key_terms.append(key_term)
        value_terms.append(value_term)
    carried = (key_terms[REACH], value_terms[REACH])
    for cycle_step in range(REACH - 1, -1, -1):
        arrived = shifted((as_sent(carried[0]), as_sent(carried[1])), WIDE, -1)
        carried = (arrived[0] + key_terms[cycle_step], arrived[1] + value_terms[cycle_step])
    key_sum, value_sum = carried
    query_back, key_back, value_back = (
        lax.all_to_all(query_grad.astype(bf16), NARROW, split_axis=1, concat_axis=2, tiled=True),
        lax.all_to_all(key_sum.astype(bf16), NARROW, split_axis=1, concat_axis=2, tiled=True),
        lax.all_to_all(value_sum.astype(bf16), NARROW, split_axis=1, concat_axis=2, tiled=True),
    )
    query_back = query_back.reshape(-1, model_width)
    key_back = key_back.reshape(-1, model_width)
    value_back = value_back.reshape(-1, model_width)
    query_wgrad = outer_sum(first_norm, query_back)
    qbias_grad = jnp.sum(query_back.astype(f32), axis=0)
    key_wgrad = outer_sum(first_norm, key_back)
    value_wgrad = outer_sum(first_norm, value_back)
    vbias_grad = jnp.sum(value_back.astype(f32), axis=0)
    first_grad = (
        times_transpose(query_back, query_full)
        + times_transpose(key_back, key_full)
        + times_transpose(value_back, value_full)
    )
    attn_pull = jax.vjp(normalize, inputs, gain_attn.astype(f32), shift_attn.astype(f32))[1]
    input_part, again_grad, ashift_grad = attn_pull(first_grad)
    input_grad = (middle_grad + input_part).reshape(batch, tokens, model_width)
    attn_shards = (
        lax.psum_scatter(again_grad, BOTH, scatter_dimension=0, tiled=True),
        lax.psum_scatter(ashift_grad, BOTH, scatter_dimension=0, tiled=True),
        lax.psum_scatter(query_wgrad, BOTH, scatter_dimension=0, tiled=True),
        lax.psum_scatter(qbias_grad, BOTH, scatter_dimension=0, tiled=True),
        lax.psum_scatter(key_wgrad, BOTH, scatter_dimension=0, tiled=True),
        lax.psum_scatter(value_wgrad, BOTH, scatter_dimension=0, tiled=True),
        lax.psum_scatter(vbias_grad, BOTH, scatter_dimension=0, tiled=True),
        lax.psum_scatter(out_grad, BOTH, scatter_dimension=0, tiled=True),
        lax.psum_scatter(obias_grad, BOTH, scatter_dimension=0, tiled=True),
    )
    return (
        block_output,
        input_grad,
        attn_shards[0],
        attn_shards[1],
        attn_shards[2],
        attn_shards[3],
        attn_shards[4],
        attn_shards[5],
        attn_shards[6],
        attn_shards[7],
        attn_shards[8],
        mlp_shards[0],
        mlp_shards[1],
        mlp_shards[2],
        mlp_shards[3],
        mlp_shards[4],
        mlp_shards[5],
    )


def flip(value, axis, bits):
    size = lax.axis_size(axis)
    return lax.ppermute(value, axis, [(i, i ^ bits) for i in range(size)])


def at(value, index, dim=0):
    return lax.dynamic_index_in_dim(value, index, dim, keepdims=False)


def cube(wide):
    steps = []
    bits = 1
    while bits < wide:
        steps.append((WIDE, bits))
        bits *= 2
    return steps + [(NARROW, 1), (NARROW, 2)]


def cube_gather(row):
    for axis, bits in cube(lax.axis_size(WIDE)):
        other = flip(row, axis, bits)
        high = (lax.axis_index(axis) & bits) > 0
        row = jnp.concatenate(
            [jnp.where(high, other, row), jnp.where(high, row, other)], axis=0
        )
    return row


def cube_scatter(table):
    wide = lax.axis_size(WIDE)
    steps = cube(wide)
    table = table.reshape((2,) * len(steps) + (table.shape[-1],))
    order = [len(steps) - 2, len(steps) - 1] + list(range(len(steps) - 2))[::-1]
    left = list(range(len(steps)))
    for k in order:
        axis, bits = steps[k]
        dim = len(left) - 1 - left.index(k)
        high = ((lax.axis_index(axis) & bits) > 0).astype(jnp.int32)
        table = at(table, high, dim) + flip(at(table, 1 - high, dim), axis, bits)
        left.remove(k)
    return table


def narrow_gather(own, *made):
    across = flip(own, NARROW, 2)
    beside = flip(own, NARROW, 1)
    across = hold(across, *made) if made else across
    return [own, beside, across, flip(across, NARROW, 1)]


def narrow_scatter(parts):
    f32 = jnp.float32
    far = flip(parts[3], NARROW, 1)
    near = flip(parts[1], NARROW, 1)
    passed = (parts[2].astype(f32) + far.astype(f32)).astype(jnp.bfloat16)
    across = flip(passed, NARROW, 2)
    return parts[0].astype(f32) + near.astype(f32) + across.astype(f32)


def hold(value, *events):
    return lax.optimization_barrier((value,) + events)[0]


def bit_of(axis, bits):
    return (lax.axis_index(axis) & bits) > 0


def in_order(relative):
    swap = bit_of(NARROW, 1)
    r = [
        jnp.where(swap, relative[k ^ 1], relative[k]) for k in range(4)
    ]
    swap = bit_of(NARROW, 2)
    return jnp.stack([jnp.where(swap, r[k ^ 2], r[k]) for k in range(4)])


def narrow_blocks(block_of):
    me = lax.axis_index(NARROW)
    return [flip(block_of(me ^ j), NARROW, j) if j else block_of(me) for j in range(4)]


def narrow_swap(block_of):
    return in_order(narrow_blocks(block_of))


def pair_swap(block_of):
    me = lax.axis_index(WIDE) & 1
    own, other = block_of(me), flip(block_of(1 - me), WIDE, 1)
    high = me > 0
    return jnp.stack([jnp.where(high, other, own), jnp.where(high, own, other)])


def spread_near(own):
    half = own.shape[1] // 2
    over_y = flip(own, WIDE, 1)
    over_x = flip(own, NARROW, 2)
    both = jnp.concatenate(
        [flip(over_y[:, :half], NARROW, 2), flip(over_x[:, half:], WIDE, 1)], axis=1
    )
    return [own, over_x, over_y, both]


def spread(own):
    near = spread_near(own)
    return near + [flip(part, NARROW, 1) for part in near]


def fold(far, near, made=None):
    f32, bf16 = jnp.float32, jnp.bfloat16
    width = far.shape[-1]
    half = width // 2
    far, near = far.reshape(4, -1, width), near.reshape(4, -1, width)
    far = flip(far, NARROW, 1)
    both = (near[3].astype(f32) + far[3].astype(f32)).astype(bf16)
    own, over_x, over_y = [near[k].astype(f32) + far[k].astype(f32) for k in range(3)]
    first = flip(both[:, :half], WIDE, 1).astype(f32)
    last = flip(both[:, half:], NARROW, 2).astype(f32)
    over_x = jnp.concatenate([over_x[:, :half] + first, over_x[:, half:]], axis=1).astype(bf16)
    over_y = jnp.concatenate([over_y[:, :half], over_y[:, half:] + last], axis=1).astype(bf16)
    last = flip(over_x, NARROW, 2)
    if made is not None:
        last = hold(last, made(over_x))
    return own + last.astype(f32) + flip(over_y, WIDE, 1).astype(f32)


def columns(wide):
    return [list(range(y, wide, 2)) for y in range(2)]


def z_gather(shard, axis):
    groups = columns(lax.axis_size(WIDE))
    return lax.all_gather(shard, WIDE, axis=axis, tiled=True, axis_index_groups=groups)


def z_scatter(full, axis):
    groups = columns(lax.axis_size(WIDE))
    return lax.psum_scatter(
        full.astype(jnp.bfloat16), WIDE, scatter_dimension=axis, tiled=True, axis_index_groups=groups
    )


def ring_order(wide):
    return list(range(0, wide, 2)) + list(range(wide - 1, 0, -2))


def ring_at(position, wide):
    position = position % wide
    return jnp.where(position < wide // 2, 2 * position, 2 * (wide - 1 - position) + 1)


def ring_position(wide):
    me = lax.axis_index(WIDE)
    return jnp.where(me % 2 == 0, me // 2, wide - 1 - me // 2)


def ring_step(value, by):
    order = ring_order(lax.axis_size(WIDE))
    size = len(order)
    return lax.ppermute(
        value, WIDE, [(order[i], order[(i + by) % size]) for i in range(size)]
    )


def ring_gather(shard):
    wide = lax.axis_size(WIDE)
    here = ring_position(wide)
    middle = shard.shape[-1] // 2
    full = jnp.zeros((wide,) + shard.shape, shard.dtype)

    def put(full, piece, position):
        return lax.dynamic_update_slice_in_dim(
            full, piece[None], ring_at(position + wide, wide), 0
        )

    full = put(full, shard, here)
    ahead = behind = shard
    for k in range(1, wide // 2):
        ahead, behind = ring_step(ahead, 1), ring_step(behind, -1)
        full = put(put(full, ahead, here - k), behind, here + k)
    ahead = ring_step(ahead[..., :middle], 1)
    behind = ring_step(behind[..., middle:], -1)
    return put(full, jnp.concatenate([ahead, behind], axis=-1), here + wide // 2)


def ring_scatter(full, beside):
    wide = lax.axis_size(WIDE)
    here = ring_position(wide)
    bf16, f32 = jnp.bfloat16, jnp.float32
    middle = full.shape[-1] // 2

    def local(position):
        return at(full, ring_at(position + wide, wide))

    far = local(here + wide // 2)
    ahead, behind = lax.optimization_barrier((far[..., :middle], far[..., middle:]))
    event = ahead
    stage = 0
    for k in range(wide // 2 - 1, -1, -1):
        ahead, behind = ring_step(ahead, 1).astype(f32), ring_step(behind, -1).astype(f32)
        values = beside(stage, event)
        stage += 1
        if k == 0:
            break
        to_ahead, to_behind = local(here + k).astype(f32), local(here - k).astype(f32)
        if k == wide // 2 - 1:
            to_ahead = jnp.concatenate(
                [to_ahead[..., :middle] + ahead, to_ahead[..., middle:]], axis=-1
            )
            to_behind = jnp.concatenate(
                [to_behind[..., :middle], to_behind[..., middle:] + behind], axis=-1
            )
        else:
            to_ahead, to_behind = to_ahead + ahead, to_behind + behind
        ahead, behind = lax.optimization_barrier(
            (to_ahead.astype(bf16), to_behind.astype(bf16)) + values
        )[:2]
    return local(here).astype(f32) + ahead + behind


def wide_swap(parts):
    return lax.all_to_all(parts, WIDE, split_axis=0, concat_axis=0, tiled=True)


def wide_gather(shard, axis):
    return lax.all_gather(shard, WIDE, axis=axis, tiled=True)


def wide_scatter(full, axis):
    return lax.psum_scatter(full.astype(jnp.bfloat16), WIDE, scatter_dimension=axis, tiled=True)


def vmem_specs(count):
    return [pl.BlockSpec(memory_space=pltpu.VMEM)] * count


SMEM_SPEC = pl.BlockSpec(memory_space=pltpu.SMEM)
BIG = pltpu.CompilerParams(vmem_limit_bytes=48 << 20)
CONTRACT_LAST = (((1,), (1,)), ((), ()))
CONTRACT_FIRST = (((0,), (0,)), ((), ()))


def project_kernel(*refs, heads, by_last):
    rows, (weight_ref, bias_ref, out_ref) = refs[:-3], refs[-3:]
    units, parts, _, tokens, head_dim = out_ref.shape
    for j, rows_ref in enumerate(rows):

        @pl.when(pl.program_id(0) == j)
        def _():
            if by_last:
                acc = lax.dot_general(
                    rows_ref[...], weight_ref[...], CONTRACT_LAST, preferred_element_type=jnp.float32
                )
            else:
                acc = jnp.dot(rows_ref[...], weight_ref[...], preferred_element_type=jnp.float32)
            acc = (acc + bias_ref[...]).astype(jnp.bfloat16)
            for unit in range(units):
                b, h = divmod(unit, heads)
                for part in range(parts):
                    c = (part * heads + h) * head_dim
                    out_ref[unit, part, 0] = acc[
                        b * tokens : (b + 1) * tokens, c : c + head_dim
                    ]


def resident(shape):
    return pl.BlockSpec(shape, lambda i: (0,) * len(shape), pipeline_mode=pl.Buffered(1))


def project(rows, weight, bias, units, parts, heads, tokens, by_last):
    blocks = len(rows)
    head_dim = bias.shape[0] // (parts * heads)
    return pl.pallas_call(
        functools.partial(project_kernel, heads=heads, by_last=by_last),
        grid=(blocks,),
        out_shape=jax.ShapeDtypeStruct((units, parts, blocks, tokens, head_dim), jnp.bfloat16),
        in_specs=[resident(block.shape) for block in rows]
        + [resident(weight.shape), resident((1, bias.shape[0]))],
        out_specs=pl.BlockSpec(
            (units, parts, 1, tokens, head_dim), lambda i: (0, 0, i, 0, 0)
        ),
        compiler_params=BIG,
        name="project",
    )(*rows, weight, bias.reshape(1, -1))


def project_parts_kernel(*refs, heads, blocks):
    rows, weights, (bias_ref, out_ref) = refs[:blocks], refs[blocks:-2], refs[-2:]
    units, parts, _, tokens, head_dim = out_ref.shape
    depth = rows[0].shape[1] // len(weights)
    for j, rows_ref in enumerate(rows):

        @pl.when(pl.program_id(0) == j)
        def _():
            acc = bias_ref[...]
            for k, weight_ref in enumerate(weights):
                acc = acc + jnp.dot(
                    rows_ref[:, k * depth : (k + 1) * depth],
                    weight_ref[...].reshape(depth, -1),
                    preferred_element_type=jnp.float32,
                )
            acc = acc.astype(jnp.bfloat16)
            for unit in range(units):
                b, h = divmod(unit, heads)
                for part in range(parts):
                    c = (part * heads + h) * head_dim
                    out_ref[unit, part, 0] = acc[b * tokens : (b + 1) * tokens, c : c + head_dim]


def project_parts(rows, weight, bias, units, parts, heads, tokens):
    blocks, head_dim = len(rows), bias.shape[0] // (parts * heads)
    wide, narrow, shard, _ = weight.shape
    width = bias.shape[0]
    return pl.pallas_call(
        functools.partial(project_parts_kernel, heads=heads, blocks=blocks),
        grid=(blocks,),
        out_shape=jax.ShapeDtypeStruct((units, parts, blocks, tokens, head_dim), jnp.bfloat16),
        in_specs=[resident(block.shape) for block in rows]
        + [
            pl.BlockSpec(
                (wide, 1, shard, width), lambda i, k=k: (0, k, 0, 0), pipeline_mode=pl.Buffered(1)
            )
            for k in range(narrow)
        ]
        + [resident((1, bias.shape[0]))],
        out_specs=pl.BlockSpec((units, parts, 1, tokens, head_dim), lambda i: (0, 0, i, 0, 0)),
        compiler_params=BIG,
        name="project_parts",
    )(*rows, *[weight] * narrow, bias.reshape(1, -1))


def times_parts_kernel(rows_ref, weight_ref, out_ref):
    inner = rows_ref.shape[1]
    weight = weight_ref[...].reshape(out_ref.shape[1], -1)[:, :inner]
    acc = lax.dot_general(
        rows_ref[...], weight, CONTRACT_LAST, preferred_element_type=jnp.float32
    )
    out_ref[...] = acc.astype(jnp.bfloat16)


def times_parts(rows, block, count, weight):
    gathered, narrow, shard, _ = weight.shape
    inner = rows.shape[1]
    step = gathered * shard
    return pl.pallas_call(
        times_parts_kernel,
        grid=(narrow,),
        out_shape=jax.ShapeDtypeStruct((count, narrow * step), jnp.bfloat16),
        in_specs=[
            pl.BlockSpec((count, inner), lambda i: (block, 0), pipeline_mode=pl.Buffered(1)),
            pl.BlockSpec((gathered, 1, shard, inner), lambda i: (0, i, 0, 0)),
        ],
        out_specs=pl.BlockSpec((count, step), lambda i: (0, i)),
        compiler_params=BIG,
        name="times_parts",
    )(rows, weight)


def wide_outer_kernel(*refs):
    lefts, (right_ref, extra_ref, out_ref) = refs[:-3], refs[-3:]
    pair, narrow, shard, total = out_ref.shape
    width = right_ref.shape[1]
    more = total - width
    for n in range(narrow):
        left = jnp.concatenate([ref[...] for ref in lefts[n::narrow]], axis=0)
        acc = lax.dot_general(
            left, right_ref[...], CONTRACT_FIRST, preferred_element_type=jnp.float32
        )
        for y in range(pair):
            out_ref[y, n, :, :width] = acc[y * shard : (y + 1) * shard].astype(jnp.bfloat16)
        for y in range(pair):
            out_ref[y, n, :, width:] = extra_ref[
                y * shard : (y + 1) * shard, n * more : (n + 1) * more
            ]


def wide_outer(lefts, right, extra, wide):
    shard, narrow, width = extra.shape[0] // wide, 4, right.shape[1]
    more = extra.shape[1] // narrow
    block = lefts[0].shape[0]
    deep = wide // 2
    return pl.pallas_call(
        wide_outer_kernel,
        grid=(deep,),
        out_shape=jax.ShapeDtypeStruct((wide, narrow, shard, width + more), jnp.bfloat16),
        in_specs=[
            pl.BlockSpec((block, 2 * shard), lambda i, n=n: (0, n * deep + i))
            for _ in lefts
            for n in range(narrow)
        ]
        + [
            resident(right.shape),
            pl.BlockSpec((2 * shard, extra.shape[1]), lambda i: (i, 0)),
        ],
        out_specs=pl.BlockSpec((2, narrow, shard, width + more), lambda i: (i, 0, 0, 0)),
        compiler_params=BIG,
        name="wide_outer",
    )(*[left for left in lefts for _ in range(narrow)], right, extra)


def row_block(parts_ref, j, b, heads):
    return jnp.concatenate(
        [
            parts_ref[b * heads + h, part, j]
            for part in range(parts_ref.shape[1])
            for h in range(heads)
        ],
        axis=1,
    )


def unproject_kernel(parts_ref, weight_ref, *refs, heads, order):
    outs, rows_ref = refs[:-1], refs[-1]
    for step, j in enumerate(order):

        @pl.when(pl.program_id(0) == step)
        def _():
            rows = jnp.concatenate(
                [row_block(parts_ref, j, b, heads) for b in range(parts_ref.shape[0] // heads)],
                axis=0,
            )
            rows_ref[j] = rows
            acc = jnp.dot(rows, weight_ref[...], preferred_element_type=jnp.float32)
            outs[j][...] = acc.astype(jnp.bfloat16)


def unproject(parts, weight, heads):
    units, count, blocks, tokens, head_dim = parts.shape
    step = tokens * units // heads
    inner = count * heads * head_dim
    width = weight.shape[1]
    results = pl.pallas_call(
        functools.partial(unproject_kernel, heads=heads, order=(3, 1, 2, 0)),
        grid=(blocks,),
        out_shape=[jax.ShapeDtypeStruct((step, width), jnp.bfloat16)] * blocks
        + [jax.ShapeDtypeStruct((blocks, step, inner), jnp.bfloat16)],
        in_specs=[resident(parts.shape), resident(weight.shape)],
        out_specs=[pl.BlockSpec((step, width), lambda i: (0, 0))] * blocks
        + [pl.BlockSpec((blocks, step, inner), lambda i: (0, 0, 0))],
        compiler_params=BIG,
        name="unproject",
    )(parts, weight)
    return results[:blocks], results[blocks].reshape(blocks * step, inner)


def join_kernel(parts_ref, rows_ref, *, heads, order):
    units, tokens = parts_ref.shape[0], parts_ref.shape[3]
    row = 0
    for j in order:
        for b in range(units // heads):
            rows_ref[row : row + tokens] = row_block(parts_ref, j, b, heads)
            row += tokens


def join(parts, heads, order):
    units, count, blocks, tokens, head_dim = parts.shape
    return pl.pallas_call(
        functools.partial(join_kernel, heads=heads, order=order),
        out_shape=jax.ShapeDtypeStruct(
            (blocks * tokens * units // heads, count * heads * head_dim), jnp.bfloat16
        ),
        in_specs=vmem_specs(1),
        out_specs=vmem_specs(1)[0],
        compiler_params=BIG,
        name="join",
    )(parts)


def mask_of(segc_ref, segr_ref, i, lo):
    keys = 512 * (i + 1 - lo)
    same = segc_ref[i] == segr_ref[:, 512 * lo : 512 * (i + 1)]
    rows = lax.broadcasted_iota(jnp.int32, (512, keys), 0) + 512 * (i - lo)
    cols = lax.broadcasted_iota(jnp.int32, (512, keys), 1)
    return jnp.logical_and(same, cols <= rows)


def take(me_ref, parts_ref, part, first, last, half):
    blocks = [
        parts_ref[4 * (i % half) : 4 * (i % half) + 4, part, (i // half) ^ me_ref[0]].reshape(512, -1)
        for i in range(first, last + 1)
    ]
    return blocks[0] if len(blocks) == 1 else jnp.concatenate(blocks, axis=0)


def give(me_ref, out_ref, part, i, half, rows):
    rows = rows.astype(out_ref.dtype).reshape(4, 128, -1)
    out_ref[4 * (i % half) : 4 * (i % half) + 4, part, (i // half) ^ me_ref[0]] = rows


def fwd_kernel(me_ref, segc_ref, segr_ref, parts_ref, out_ref, lse_ref, *, blocks, scale2):
    half = blocks // 4
    for i in range(blocks):
        lo = max(i - 1, 0)
        q = take(me_ref, parts_ref, 0, i, i, half)
        k = take(me_ref, parts_ref, 1, lo, i, half)
        v = take(me_ref, parts_ref, 2, lo, i, half)
        s = lax.dot_general(q, k, CONTRACT_LAST, preferred_element_type=jnp.float32)
        s = jnp.where(mask_of(segc_ref, segr_ref, i, lo), s * scale2, neg_big)
        m = jnp.max(s, axis=-1, keepdims=True)
        p = jnp.exp2(s - m)
        total = jnp.sum(p, axis=-1, keepdims=True)
        o = jnp.dot(p.astype(jnp.bfloat16), v, preferred_element_type=jnp.float32)
        give(me_ref, out_ref, 0, i, half, o / total)
        lse_ref[i] = m + jnp.log2(total)


def bwd_kernel(
    me_ref, segc_ref, segr_ref, lse_ref, parts_ref, do_ref, grad_ref, dk_acc, dv_acc, *, blocks, scale, scale2
):
    half = blocks // 4
    f32 = jnp.float32
    for i in range(blocks):
        lo = max(i - 1, 0)
        q = take(me_ref, parts_ref, 0, i, i, half)
        k = take(me_ref, parts_ref, 1, lo, i, half)
        v = take(me_ref, parts_ref, 2, lo, i, half)
        do = take(me_ref, do_ref, 0, i, i, half)
        s = lax.dot_general(q, k, CONTRACT_LAST, preferred_element_type=f32)
        s = jnp.where(mask_of(segc_ref, segr_ref, i, lo), s * scale2, neg_big)
        p = jnp.exp2(s - lse_ref[i])
        dp = lax.dot_general(do, v, CONTRACT_LAST, preferred_element_type=f32)
        t = p * dp
        delta = jnp.sum(t, axis=-1, keepdims=True)
        ds = (t - p * delta).astype(jnp.bfloat16)
        give(me_ref, grad_ref, 0, i, half, jnp.dot(ds, k, preferred_element_type=f32) * scale)
        dk = lax.dot_general(ds, q, CONTRACT_FIRST, preferred_element_type=f32)
        dv = lax.dot_general(
            p.astype(jnp.bfloat16), do, CONTRACT_FIRST, preferred_element_type=f32
        )
        if i > 0:
            give(me_ref, grad_ref, 1, i - 1, half, (dk_acc[...] + dk[:512]) * scale)
            give(me_ref, grad_ref, 2, i - 1, half, dv_acc[...] + dv[:512])
        if i == blocks - 1:
            give(me_ref, grad_ref, 1, i, half, dk[-512:] * scale)
            give(me_ref, grad_ref, 2, i, half, dv[-512:])
        else:
            dk_acc[...] = dk[-512:]
            dv_acc[...] = dv[-512:]


def attend_fwd(me, segc, segr, parts):
    blocks = segc.shape[0]
    units, _, narrow, rows, width = parts.shape
    scale2 = math.log2(math.e) / math.sqrt(width)
    return pl.pallas_call(
        functools.partial(fwd_kernel, blocks=blocks, scale2=scale2),
        out_shape=(
            jax.ShapeDtypeStruct((units, 1, narrow, rows, width), jnp.bfloat16),
            jax.ShapeDtypeStruct((blocks, 512, 1), jnp.float32),
        ),
        in_specs=[SMEM_SPEC] + vmem_specs(3),
        out_specs=tuple(vmem_specs(2)),
        compiler_params=BIG,
        name="attend_fwd",
    )(me, segc, segr, parts)


def attend_bwd(me, segc, segr, lse, parts, dout):
    blocks = segc.shape[0]
    width = parts.shape[-1]
    scale = 1.0 / math.sqrt(width)
    return pl.pallas_call(
        functools.partial(
            bwd_kernel, blocks=blocks, scale=scale, scale2=scale * math.log2(math.e)
        ),
        out_shape=jax.ShapeDtypeStruct(parts.shape, jnp.bfloat16),
        in_specs=[SMEM_SPEC] + vmem_specs(5),
        out_specs=vmem_specs(1)[0],
        scratch_shapes=[pltpu.VMEM((512, width), jnp.float32)] * 2,
        compiler_params=BIG,
        name="attend_bwd",
    )(me, segc, segr, lse, parts, dout)


def ff_kernel(*refs, count):
    rows, weights, (bias_ref, hidden_ref, slope_ref) = refs[:count], refs[count:-3], refs[-3:]
    step = rows[0].shape[0]
    depth = rows[0].shape[1] // len(weights)
    for k, rows_ref in enumerate(rows):
        r = k * step
        x = bias_ref[...]
        for n, weight_ref in enumerate(weights):
            x = x + jnp.dot(
                rows_ref[:, n * depth : (n + 1) * depth],
                weight_ref[...].reshape(depth, -1),
                preferred_element_type=jnp.float32,
            )
        below = 0.5 * (1.0 + lax.erf(x * math.sqrt(0.5)))
        hidden_ref[r : r + step] = (x * below).astype(jnp.bfloat16)
        slope_ref[r : r + step] = below + x * (
            jnp.exp(-0.5 * x * x) * (1.0 / math.sqrt(2.0 * math.pi))
        )


def feed_forward(rows, weight, bias):
    count = len(rows) * rows[0].shape[0]
    deep, narrow, shard, inner = weight.shape
    step = 256
    return pl.pallas_call(
        functools.partial(ff_kernel, count=len(rows)),
        grid=(inner // step,),
        out_shape=(
            jax.ShapeDtypeStruct((count, inner), jnp.bfloat16),
            jax.ShapeDtypeStruct((count, inner), jnp.float32),
        ),
        in_specs=[resident(block.shape) for block in rows]
        + [
            pl.BlockSpec((deep, 1, shard, step), lambda i, n=n: (0, n, 0, i)) for n in range(narrow)
        ]
        + [pl.BlockSpec((1, step), lambda i: (0, i))],
        out_specs=(
            pl.BlockSpec((count, step), lambda i: (0, i)),
            pl.BlockSpec((count, step), lambda i: (0, i)),
        ),
        compiler_params=BIG,
        name="feed_forward",
    )(*rows, *[weight] * narrow, bias.reshape(1, -1))


def pull_kernel(rows_ref, weight_ref, slope_ref, grad_ref, sum_ref):
    step = 256
    total = jnp.zeros((1, weight_ref.shape[0]), jnp.float32)
    for r in range(0, rows_ref.shape[0], step):
        pull = lax.dot_general(
            rows_ref[r : r + step],
            weight_ref[...],
            CONTRACT_LAST,
            preferred_element_type=jnp.float32,
        )
        grad = (pull * slope_ref[r : r + step]).astype(jnp.bfloat16)
        grad_ref[r : r + step] = grad
        total = total + jnp.sum(grad.astype(jnp.float32), axis=0, keepdims=True)
    sum_ref[...] = total


def pull_back(rows, weight, slope):
    count, inner = slope.shape
    width = weight.shape[1]
    step = 256
    return pl.pallas_call(
        pull_kernel,
        grid=(inner // step,),
        out_shape=(
            jax.ShapeDtypeStruct((count, inner), jnp.bfloat16),
            jax.ShapeDtypeStruct((1, inner), jnp.float32),
        ),
        in_specs=[
            resident(rows.shape),
            pl.BlockSpec((step, width), lambda i: (i, 0)),
            pl.BlockSpec((count, step), lambda i: (0, i)),
        ],
        out_specs=(
            pl.BlockSpec((count, step), lambda i: (0, i)),
            pl.BlockSpec((1, step), lambda i: (0, i)),
        ),
        compiler_params=BIG,
        name="pull_back",
    )(rows, weight, slope)


def pick_kernel(me_ref, weight_ref, out_ref):
    _, narrow, shard, inner = out_ref.shape
    high = (me_ref[1] & 1) > 0
    step = 256
    for n in range(narrow):
        for z in range(inner // step):
            c = (n * (inner // step) + z) * 2 * step
            low_part = weight_ref[:, c : c + step]
            high_part = weight_ref[:, c + step : c + 2 * step]
            cols = slice(z * step, (z + 1) * step)
            out_ref[0, n, :, cols] = jnp.where(high, high_part, low_part)
            out_ref[1, n, :, cols] = jnp.where(high, low_part, high_part)


def pick(me, weight, narrow):
    shard, total = weight.shape
    return pl.pallas_call(
        pick_kernel,
        out_shape=jax.ShapeDtypeStruct((2, narrow, shard, total // (2 * narrow)), weight.dtype),
        in_specs=[SMEM_SPEC] + vmem_specs(1),
        out_specs=vmem_specs(1)[0],
        compiler_params=BIG,
        name="pick",
    )(me, weight)


def on_device(
    block_input,
    segment_ids,
    cotangent,
    attn_gain,
    attn_shift,
    query_weight,
    query_bias,
    key_weight,
    value_weight,
    value_bias,
    out_weight,
    out_bias,
    mlp_gain,
    mlp_shift,
    up_weight,
    up_bias,
    down_weight,
    down_bias,
):
    f32 = jnp.float32
    bf16 = jnp.bfloat16
    batch, tokens, width = block_input.shape
    narrow = lax.axis_size(NARROW)
    wide = lax.axis_size(WIDE)
    me_n = lax.axis_index(NARROW)
    me_w = lax.axis_index(WIDE)
    me = jnp.stack([me_n, me_w]).astype(jnp.int32)
    rows = batch * tokens
    heads = HEADS // narrow
    head_dim = width // HEADS
    cols = heads * head_dim
    shard = width // (narrow * wide)
    deep = wide // 2
    ff_shard = up_bias.shape[0]
    ff_local = ff_shard * deep
    me_y = me_w & 1

    def qkv_block(n):
        return jnp.concatenate(
            [
                lax.dynamic_slice_in_dim(weight, n * cols, cols, 1)
                for weight in (query_weight, key_weight, value_weight)
            ],
            axis=1,
        )

    out_w = wide_gather(out_weight, 0)
    qkv_shard = narrow_swap(qkv_block)
    attn_parts = ring_gather(qkv_shard)

    smalls = [
        attn_gain, attn_shift, out_bias, mlp_gain, mlp_shift, down_bias, query_bias, value_bias, up_bias
    ]
    ids = segment_ids.astype(bf16).reshape(-1)
    small = cube_gather(hold(jnp.concatenate(smalls + [ids])[None], qkv_shard))

    def full_vector(k):
        return small[:, k * shard : (k + 1) * shard].reshape(-1).astype(f32)

    gain_attn, shift_attn, obias, gain_mlp, shift_mlp, dbias = [full_vector(k) for k in range(6)]
    mine = lax.dynamic_slice_in_dim(small, me_n * wide, wide, 0)
    qbias = mine[:, 6 * shard : 7 * shard].reshape(-1).astype(f32)
    vbias = mine[:, 7 * shard : 8 * shard].reshape(-1).astype(f32)
    ubias = mine[:, 8 * shard : 8 * shard + ff_shard].reshape(deep, 2, ff_shard)
    ubias = at(ubias, me_y, 1).reshape(-1).astype(f32)
    qkv_bias = jnp.concatenate([qbias, jnp.zeros_like(qbias), vbias])

    inputs = block_input.astype(f32).reshape(rows, width)
    first_norm = narrow_gather(normalize(inputs, gain_attn, shift_attn).astype(bf16))
    cotan_own = cotangent.reshape(rows, width)
    attn_parts = hold(attn_parts, out_w)
    sent = project_parts(first_norm, attn_parts, qkv_bias, wide, 3, heads, tokens)
    qkv = wide_swap(sent)

    picked = pick(me, hold(up_weight, first_norm[3]), narrow)
    high = me_y > 0
    here, there = picked[0], flip(hold(picked[1], sent), WIDE, 1)
    up_pair = jnp.stack([jnp.where(high, there, here), jnp.where(high, here, there)], axis=1)
    up_shard = narrow_swap(lambda n: at(up_pair, n)).reshape(narrow, 2 * shard, ff_local)
    ids = hold(small, sent)[:, -batch * tokens :].reshape(narrow * wide, batch, tokens)
    unit_ids = at(ids, me_w // heads, 1).reshape(-1).astype(jnp.int32)
    segc = unit_ids.reshape(-1, 512, 1)
    segr = unit_ids.reshape(1, -1)
    qkv = hold(qkv, up_shard)
    unit_out, lse = attend_fwd(me, segc, segr, qkv)
    up_parts = z_gather(hold(up_shard, unit_out)[None], 0)
    unit_back = wide_swap(unit_out)
    near = spread_near(hold(cotan_own, unit_out))
    unit_back = hold(unit_back, *near)
    cotan = jnp.concatenate(near + [flip(hold(part, unit_back), NARROW, 1) for part in near], axis=0)
    partial, mixed = unproject(unit_back, out_w, heads)
    middle = inputs + narrow_scatter(partial) + obias
    down_late, middle = lax.optimization_barrier((down_weight, middle, up_parts, cotan))[:2]
    down_w = z_gather(down_late, 0)

    second_norm = spread(normalize(middle, gain_mlp, shift_mlp).astype(bf16))
    hidden, slope = feed_forward(second_norm, up_parts, ubias)
    down_grad = outer_sum(hidden, cotan).astype(bf16)
    slope = hold(slope, down_grad)
    down_grad = z_scatter(down_grad, 0)
    inner_grad, ubias_grad = pull_back(cotan, down_w, slope)
    split = inner_grad.shape[0] // 2
    far = times_parts(inner_grad, 1, split, up_parts)
    near = times_parts(hold(inner_grad, far), 0, split, up_parts)
    norm_rows = jnp.concatenate(second_norm, axis=0)
    up_made = []

    def make_up_grad(event):
        up_made.append(outer_sum(norm_rows, hold(inner_grad, event)).astype(bf16))
        return up_made[0]

    second_grad = fold(far, near, make_up_grad)
    mlp_pull = jax.vjp(normalize, middle, gain_mlp, shift_mlp)[1]
    middle_part, mgain_grad, mshift_grad = mlp_pull(second_grad)
    middle_grad = cotan_own.astype(f32) + middle_part
    branch_own = middle_grad.astype(bf16)
    dbias_grad = jnp.sum(cotan_own.astype(f32), axis=0)

    obias_grad = jnp.sum(branch_own.astype(f32), axis=0)
    hidden_late = hold(hidden, branch_own)
    out_far = matmul(hidden_late[split:], down_w).astype(bf16)
    out_near = matmul(hidden_late[:split], down_w).astype(bf16)
    branch = narrow_gather(branch_own, out_far, out_near)
    up_grad = hold(up_made[0], branch[2], down_grad)
    up_grad = z_scatter(up_grad.reshape(narrow, 2 * deep * shard, ff_local), 1)
    no_bias = jnp.zeros((cols,), f32)
    sent = project(branch, out_w, no_bias, wide, 1, heads, tokens, True)
    out_grad = outer_sum(hold(mixed, sent), jnp.concatenate(branch, axis=0)).astype(bf16)
    output = middle + fold(out_far, out_near) + dbias
    block_output = output.astype(bf16).reshape(batch, tokens, width)
    dout = hold(wide_swap(sent), out_grad, block_output)
    unit_grads = attend_bwd(me, segc, segr, lse, qkv, dout)
    grads = wide_swap(unit_grads)
    up_rows = hold(up_grad, unit_grads).reshape(narrow, 2, shard, ff_local)
    up_swapped = narrow_swap(lambda n: at(up_rows, n))
    up_back = pair_swap(lambda y: at(up_swapped, y, 1))
    up_back = up_back.reshape(2, narrow, shard, deep, ff_shard).transpose(2, 1, 3, 0, 4)
    up_back = up_back.reshape(shard, -1).astype(f32)
    down_grad = down_grad.astype(f32)
    grads = hold(grads, up_back)
    order = (1, 3, 0, 2)
    back = join(grads, heads, order)
    sums = wide_outer([first_norm[j] for j in order], back, out_grad, wide)
    made = {}

    def beside(stage, event):
        if stage == 0:
            late = hold(back, event)
            far = times_parts(late, 0, 2 * rows, attn_parts)
            near = times_parts(hold(late, far), 1, 2 * rows, attn_parts)
            made["far"] = far.reshape(2, rows, width)
            made["near"] = near.reshape(2, rows, width)
            return far, near
        if stage == 1:
            near, far = made["near"], made["far"]
            made["first"] = narrow_scatter([near[0], far[0], near[1], far[1]])
            return (made["first"],)
        if stage == 2:
            attn_pull = jax.vjp(normalize, inputs, gain_attn, shift_attn)[1]
            input_part, again_grad, ashift_grad = attn_pull(made["first"])
            made["pulled"] = middle_grad + input_part, again_grad, ashift_grad
            return made["pulled"] + (down_grad,)
        return ()

    qkv_rows = ring_scatter(sums, beside).astype(bf16)
    out_grad = qkv_rows[..., 3 * cols :].transpose(1, 0, 2).reshape(shard, width)
    qkv_rows = qkv_rows[..., : 3 * cols]
    swapped = narrow_blocks(lambda n: at(qkv_rows, n))
    qkv_grad = in_order(swapped).reshape(narrow, shard, 3, cols)
    qkv_grad = qkv_grad.transpose(2, 1, 0, 3).reshape(3, shard, width).astype(f32)
    back_sums = jnp.sum(back.astype(f32), axis=0)
    input_grad, again_grad, ashift_grad = made["pulled"]
    input_grad = input_grad.reshape(batch, tokens, width)

    fulls = [again_grad, ashift_grad, obias_grad, mgain_grad, mshift_grad, dbias_grad]
    fulls = jnp.concatenate([v.reshape(narrow * wide, shard) for v in fulls], axis=1)
    ubias_rows = jnp.zeros((deep, 2, ff_shard), f32)
    ubias_rows = lax.dynamic_update_slice_in_dim(
        ubias_rows,
        ubias_grad.reshape(deep, 1, ff_shard),
        me_y,
        1,
    )
    slices = [back_sums[:cols], back_sums[2 * cols :], ubias_rows]
    slices = jnp.concatenate([v.reshape(wide, -1) for v in slices], axis=1)
    placed = jnp.zeros((narrow * wide, slices.shape[1]), f32)
    placed = lax.dynamic_update_slice_in_dim(placed, slices, me_n * wide, 0)
    vectors = cube_scatter(hold(jnp.concatenate([fulls, placed], axis=1), swapped[1]))

    def vector(k):
        return vectors[k * shard : (k + 1) * shard]

    return (
        block_output,
        input_grad,
        vector(0),
        vector(1),
        qkv_grad[0],
        vector(6),
        qkv_grad[1],
        qkv_grad[2],
        vector(7),
        out_grad.astype(f32),
        vector(2),
        vector(3),
        vector(4),
        up_back,
        vectors[8 * shard :],
        down_grad,
        vector(5),
    )


def body_of(mesh):
    def body(*args):
        batch, tokens, width = args[0].shape
        narrow, wide = mesh.shape[NARROW], mesh.shape[WIDE]
        one_unit = batch * (HEADS // narrow) == wide and tokens == 128 and narrow == 4
        return (on_device if one_unit else on_device_ring)(*args)

    return body


def solution(mesh):
    return jax.shard_map(
        body_of(mesh),
        mesh=mesh,
        in_specs=(
            P(None, BOTH, None),
            P(None, BOTH),
            P(None, BOTH, None),
            P(BOTH),
            P(BOTH),
            P(BOTH, None),
            P(BOTH),
            P(BOTH, None),
            P(BOTH, None),
            P(BOTH),
            P(BOTH, None),
            P(BOTH),
            P(BOTH),
            P(BOTH),
            P(BOTH, None),
            P(BOTH),
            P(BOTH, None),
            P(BOTH),
        ),
        out_specs=(
            P(None, BOTH, None),
            P(None, BOTH, None),
            P(BOTH),
            P(BOTH),
            P(BOTH, None),
            P(BOTH),
            P(BOTH, None),
            P(BOTH, None),
            P(BOTH),
            P(BOTH, None),
            P(BOTH),
            P(BOTH),
            P(BOTH),
            P(BOTH, None),
            P(BOTH),
            P(BOTH, None),
            P(BOTH),
        ),
        check_vma=False,
    )
```

```python
import functools
import math
import jax
import jax.numpy as jnp
from jax import lax
from jax.experimental import pallas as pl
from jax.experimental.pallas import tpu as pltpu
from jax.sharding import PartitionSpec as P
HEADS = 16
NARROW, WIDE = "narrow", "wide"
BOTH = (NARROW, WIDE)
REACH = 4
eps = 1e-05
neg_big = -1e30


def shifted(value, axis, by):
    devices = lax.axis_size(axis)
    return lax.ppermute(value, axis, [(i, (i + by) % devices) for i in range(devices)])


def as_sent(value):

    def short(part):
        return part.astype(jnp.bfloat16) if part.dtype == jnp.float32 else part

    return jax.tree.map(short, value)


def normalize(values, gain, shift):
    center = jnp.mean(values, axis=-1, keepdims=True)
    centered = values - center
    spread = jnp.mean(centered * centered, axis=-1, keepdims=True)
    return centered * lax.rsqrt(spread + eps) * gain + shift


def gelu_exact(values):
    return jax.nn.gelu(values, approximate=False)


def matmul(left, right):
    return jnp.dot(left, right, preferred_element_type=jnp.float32)


def outer_sum(left, right):
    return lax.dot_general(
        left, right, (((0,), (0,)), ((), ())), preferred_element_type=jnp.float32
    )


def times_transpose(left, right):
    return lax.dot_general(
        left, right, (((1,), (1,)), ((), ())), preferred_element_type=jnp.float32
    )


def key_positions(first_row, row_count, tokens, narrow_size, wide_size):
    row_ids = first_row + jnp.arange(row_count, dtype=jnp.int32)
    source_wide = row_ids // (tokens * narrow_size)
    source_narrow = row_ids // tokens % narrow_size
    return (source_narrow * wide_size + source_wide) * tokens + row_ids % tokens


def block_mask(query_segs, query_pos, key_segs, key_pos):
    same_doc = query_segs[:, :, None] == key_segs[:, None, :]
    causal = key_pos[None, None, :] <= query_pos[None, :, None]
    return jnp.logical_and(same_doc, causal)


def raw_scores(query_rows, key_rows, score_scale, allowed):
    scores = (
        jnp.einsum("bqhd,bkhd->bhqk", query_rows, key_rows, preferred_element_type=jnp.float32)
        * score_scale
    )
    return jnp.where(allowed[:, None], scores, neg_big)


def forward_block(running, query_heads, key_block, value_block, allowed, score_scale):
    row_max, row_total, weighted = running
    scores = raw_scores(query_heads, key_block, score_scale, allowed)
    new_max = jnp.maximum(row_max, jnp.max(scores, axis=-1))
    rescale = jnp.exp(row_max - new_max)
    exp_terms = jnp.where(allowed[:, None], jnp.exp(scores - new_max[..., None]), 0.0)
    row_total = row_total * rescale + jnp.sum(exp_terms, axis=-1)
    added = jnp.einsum(
        "bhqk,bkhd->bqhd",
        exp_terms.astype(jnp.bfloat16),
        value_block,
        preferred_element_type=jnp.float32,
    )
    weighted = weighted * jnp.transpose(rescale, (0, 2, 1))[..., None] + added
    return (new_max, row_total, weighted)


def backward_block(
    query_grad,
    query_heads,
    dout_heads,
    key_block,
    value_block,
    allowed,
    delta,
    log_total,
    score_scale,
):
    scores = raw_scores(query_heads, key_block, score_scale, allowed)
    attn_probs = jnp.where(allowed[:, None], jnp.exp(scores - log_total[..., None]), 0.0)
    prob_grad = jnp.einsum(
        "bqhd,bkhd->bhqk", dout_heads, value_block, preferred_element_type=jnp.float32
    )
    score_grad = (attn_probs * (prob_grad - delta[..., None])).astype(jnp.bfloat16)
    query_grad = query_grad + score_scale * jnp.einsum(
        "bhqk,bkhd->bqhd", score_grad, key_block, preferred_element_type=jnp.float32
    )
    key_grad = score_scale * jnp.einsum(
        "bhqk,bqhd->bkhd", score_grad, query_heads, preferred_element_type=jnp.float32
    )
    value_grad = jnp.einsum(
        "bhqk,bqhd->bkhd",
        attn_probs.astype(jnp.bfloat16),
        dout_heads,
        preferred_element_type=jnp.float32,
    )
    return (query_grad, key_grad, value_grad)


def on_device_ring(
    block_input,
    segment_ids,
    cotangent,
    attn_gain,
    attn_shift,
    query_weight,
    query_bias,
    key_weight,
    value_weight,
    value_bias,
    out_weight,
    out_bias,
    mlp_gain,
    mlp_shift,
    up_weight,
    up_bias,
    down_weight,
    down_bias,
):
    batch, tokens, model_width = block_input.shape
    narrow_size = lax.axis_size(NARROW)
    wide_size = lax.axis_size(WIDE)
    wide_index = lax.axis_index(WIDE)
    group_rows = tokens * narrow_size
    heads_local = HEADS // narrow_size
    head_dim = model_width // HEADS
    score_scale = 1.0 / math.sqrt(head_dim)
    f32 = jnp.float32
    bf16 = jnp.bfloat16
    attn_set = (
        lax.all_gather(attn_gain, BOTH, axis=0, tiled=True),
        lax.all_gather(attn_shift, BOTH, axis=0, tiled=True),
        lax.all_gather(query_weight, BOTH, axis=0, tiled=True),
        lax.all_gather(query_bias, BOTH, axis=0, tiled=True),
        lax.all_gather(key_weight, BOTH, axis=0, tiled=True),
        lax.all_gather(value_weight, BOTH, axis=0, tiled=True),
        lax.all_gather(value_bias, BOTH, axis=0, tiled=True),
        lax.all_gather(out_weight, BOTH, axis=0, tiled=True),
        lax.all_gather(out_bias, BOTH, axis=0, tiled=True),
    )
    (
        gain_attn,
        shift_attn,
        query_full,
        qbias_full,
        key_full,
        value_full,
        vbias_full,
        out_full,
        obias_full,
    ) = attn_set
    inputs = block_input.astype(f32).reshape(-1, model_width)
    first_norm = normalize(inputs, gain_attn.astype(f32), shift_attn.astype(f32)).astype(bf16)
    split_shape = (batch, tokens, HEADS, head_dim)
    queries = (
        (matmul(first_norm, query_full) + qbias_full.astype(f32)).astype(bf16).reshape(split_shape)
    )
    key_rows = matmul(first_norm, key_full).astype(bf16).reshape(split_shape)
    value_rows = (
        (matmul(first_norm, value_full) + vbias_full.astype(f32)).astype(bf16).reshape(split_shape)
    )
    query_heads, key_heads, value_heads = (
        lax.all_to_all(queries, NARROW, split_axis=2, concat_axis=1, tiled=True),
        lax.all_to_all(key_rows, NARROW, split_axis=2, concat_axis=1, tiled=True),
        lax.all_to_all(value_rows, NARROW, split_axis=2, concat_axis=1, tiled=True),
    )
    query_segs = lax.all_gather(segment_ids, NARROW, axis=1, tiled=True)
    query_pos = key_positions(wide_index * group_rows, group_rows, tokens, narrow_size, wide_size)

    def block_allowed(cycle_step, seg_block):
        source = (wide_index - cycle_step) % wide_size
        key_pos = key_positions(source * group_rows, group_rows, tokens, narrow_size, wide_size)
        return block_mask(query_segs, query_pos, seg_block, key_pos)

    running = (
        jnp.full((batch, heads_local, group_rows), neg_big, f32),
        jnp.zeros((batch, heads_local, group_rows), f32),
        jnp.zeros((batch, group_rows, heads_local, head_dim), f32),
    )
    travelling = (key_heads, value_heads, query_segs)
    received = []
    for cycle_step in range(REACH + 1):
        if cycle_step > 0:
            travelling = shifted((travelling[0], travelling[1], travelling[2]), WIDE, 1)
        received.append(travelling)
        key_block, value_block, seg_block = travelling
        allowed = block_allowed(cycle_step, seg_block)
        running = forward_block(running, query_heads, key_block, value_block, allowed, score_scale)
    row_max, row_total, weighted = running
    attn_out = weighted / jnp.transpose(row_total, (0, 2, 1))[..., None]
    log_total = row_max + jnp.log(row_total)
    mixed = lax.all_to_all(
        attn_out.astype(bf16), NARROW, split_axis=1, concat_axis=2, tiled=True
    ).reshape(-1, model_width)
    middle = inputs + matmul(mixed, out_full) + obias_full.astype(f32)
    mlp_set = (
        lax.all_gather(mlp_gain, BOTH, axis=0, tiled=True),
        lax.all_gather(mlp_shift, BOTH, axis=0, tiled=True),
        lax.all_gather(up_weight, BOTH, axis=0, tiled=True),
        lax.all_gather(up_bias, BOTH, axis=0, tiled=True),
        lax.all_gather(down_weight, BOTH, axis=0, tiled=True),
        lax.all_gather(down_bias, BOTH, axis=0, tiled=True),
    )
    gain_mlp, shift_mlp, up_full, ubias_full, down_full, dbias_full = mlp_set
    second_norm = normalize(middle, gain_mlp.astype(f32), shift_mlp.astype(f32)).astype(bf16)
    inner = matmul(second_norm, up_full) + ubias_full.astype(f32)
    hidden = gelu_exact(inner).astype(bf16)
    output = middle + matmul(hidden, down_full) + dbias_full.astype(f32)
    block_output = output.astype(bf16).reshape(batch, tokens, model_width)
    mlp_set = (
        lax.all_gather(mlp_gain, BOTH, axis=0, tiled=True),
        lax.all_gather(mlp_shift, BOTH, axis=0, tiled=True),
        lax.all_gather(up_weight, BOTH, axis=0, tiled=True),
        lax.all_gather(up_bias, BOTH, axis=0, tiled=True),
        lax.all_gather(down_weight, BOTH, axis=0, tiled=True),
        lax.all_gather(down_bias, BOTH, axis=0, tiled=True),
    )
    gain_mlp, shift_mlp, up_full, ubias_full, down_full, dbias_full = mlp_set
    cotan_rows = cotangent.reshape(-1, model_width)
    down_grad = outer_sum(hidden, cotan_rows)
    dbias_grad = jnp.sum(cotan_rows.astype(f32), axis=0)
    hidden_grad = times_transpose(cotan_rows, down_full)
    gelu_pull = jax.vjp(gelu_exact, inner)[1]
    inner_grad = gelu_pull(hidden_grad)[0].astype(bf16)
    up_grad = outer_sum(second_norm, inner_grad)
    ubias_grad = jnp.sum(inner_grad.astype(f32), axis=0)
    second_grad = times_transpose(inner_grad, up_full)
    mlp_pull = jax.vjp(normalize, middle, gain_mlp.astype(f32), shift_mlp.astype(f32))[1]
    middle_part, mgain_grad, mshift_grad = mlp_pull(second_grad)
    middle_grad = cotan_rows.astype(f32) + middle_part
    mlp_shards = (
        lax.psum_scatter(mgain_grad, BOTH, scatter_dimension=0, tiled=True),
        lax.psum_scatter(mshift_grad, BOTH, scatter_dimension=0, tiled=True),
        lax.psum_scatter(up_grad, BOTH, scatter_dimension=0, tiled=True),
        lax.psum_scatter(ubias_grad, BOTH, scatter_dimension=0, tiled=True),
        lax.psum_scatter(down_grad, BOTH, scatter_dimension=0, tiled=True),
        lax.psum_scatter(dbias_grad, BOTH, scatter_dimension=0, tiled=True),
    )
    attn_set = (
        lax.all_gather(attn_gain, BOTH, axis=0, tiled=True),
        lax.all_gather(attn_shift, BOTH, axis=0, tiled=True),
        lax.all_gather(query_weight, BOTH, axis=0, tiled=True),
        lax.all_gather(query_bias, BOTH, axis=0, tiled=True),
        lax.all_gather(key_weight, BOTH, axis=0, tiled=True),
        lax.all_gather(value_weight, BOTH, axis=0, tiled=True),
        lax.all_gather(value_bias, BOTH, axis=0, tiled=True),
        lax.all_gather(out_weight, BOTH, axis=0, tiled=True),
        lax.all_gather(out_bias, BOTH, axis=0, tiled=True),
    )
    (
        gain_attn,
        shift_attn,
        query_full,
        qbias_full,
        key_full,
        value_full,
        vbias_full,
        out_full,
        obias_full,
    ) = attn_set
    branch_grad = middle_grad.astype(bf16)
    out_grad = outer_sum(mixed, branch_grad)
    obias_grad = jnp.sum(branch_grad.astype(f32), axis=0)
    mixed_grad = times_transpose(branch_grad, out_full).astype(bf16).reshape(split_shape)
    dout_heads = lax.all_to_all(mixed_grad, NARROW, split_axis=2, concat_axis=1, tiled=True)
    delta = jnp.transpose(jnp.sum(dout_heads.astype(f32) * attn_out, axis=-1), (0, 2, 1))
    travelling = (key_heads, value_heads, query_segs)
    received = []
    for cycle_step in range(REACH + 1):
        if cycle_step > 0:
            travelling = shifted((travelling[0], travelling[1], travelling[2]), WIDE, 1)
        received.append(travelling)
    query_grad = jnp.zeros((batch, group_rows, heads_local, head_dim), f32)
    key_terms = []
    value_terms = []
    for cycle_step in range(REACH + 1):
        key_block, value_block, seg_block = received[cycle_step]
        allowed = block_allowed(cycle_step, seg_block)
        query_grad, key_term, value_term = backward_block(
            query_grad,
            query_heads,
            dout_heads,
            key_block,
            value_block,
            allowed,
            delta,
            log_total,
            score_scale,
        )
        key_terms.append(key_term)
        value_terms.append(value_term)
    carried = (key_terms[REACH], value_terms[REACH])
    for cycle_step in range(REACH - 1, -1, -1):
        arrived = shifted((as_sent(carried[0]), as_sent(carried[1])), WIDE, -1)
        carried = (arrived[0] + key_terms[cycle_step], arrived[1] + value_terms[cycle_step])
    key_sum, value_sum = carried
    query_back, key_back, value_back = (
        lax.all_to_all(query_grad.astype(bf16), NARROW, split_axis=1, concat_axis=2, tiled=True),
        lax.all_to_all(key_sum.astype(bf16), NARROW, split_axis=1, concat_axis=2, tiled=True),
        lax.all_to_all(value_sum.astype(bf16), NARROW, split_axis=1, concat_axis=2, tiled=True),
    )
    query_back = query_back.reshape(-1, model_width)
    key_back = key_back.reshape(-1, model_width)
    value_back = value_back.reshape(-1, model_width)
    query_wgrad = outer_sum(first_norm, query_back)
    qbias_grad = jnp.sum(query_back.astype(f32), axis=0)
    key_wgrad = outer_sum(first_norm, key_back)
    value_wgrad = outer_sum(first_norm, value_back)
    vbias_grad = jnp.sum(value_back.astype(f32), axis=0)
    first_grad = (
        times_transpose(query_back, query_full)
        + times_transpose(key_back, key_full)
        + times_transpose(value_back, value_full)
    )
    attn_pull = jax.vjp(normalize, inputs, gain_attn.astype(f32), shift_attn.astype(f32))[1]
    input_part, again_grad, ashift_grad = attn_pull(first_grad)
    input_grad = (middle_grad + input_part).reshape(batch, tokens, model_width)
    attn_shards = (
        lax.psum_scatter(again_grad, BOTH, scatter_dimension=0, tiled=True),
        lax.psum_scatter(ashift_grad, BOTH, scatter_dimension=0, tiled=True),
        lax.psum_scatter(query_wgrad, BOTH, scatter_dimension=0, tiled=True),
        lax.psum_scatter(qbias_grad, BOTH, scatter_dimension=0, tiled=True),
        lax.psum_scatter(key_wgrad, BOTH, scatter_dimension=0, tiled=True),
        lax.psum_scatter(value_wgrad, BOTH, scatter_dimension=0, tiled=True),
        lax.psum_scatter(vbias_grad, BOTH, scatter_dimension=0, tiled=True),
        lax.psum_scatter(out_grad, BOTH, scatter_dimension=0, tiled=True),
        lax.psum_scatter(obias_grad, BOTH, scatter_dimension=0, tiled=True),
    )
    return (
        block_output,
        input_grad,
        attn_shards[0],
        attn_shards[1],
        attn_shards[2],
        attn_shards[3],
        attn_shards[4],
        attn_shards[5],
        attn_shards[6],
        attn_shards[7],
        attn_shards[8],
        mlp_shards[0],
        mlp_shards[1],
        mlp_shards[2],
        mlp_shards[3],
        mlp_shards[4],
        mlp_shards[5],
    )


def flip(value, axis, bits):
    size = lax.axis_size(axis)
    return lax.ppermute(value, axis, [(i, i ^ bits) for i in range(size)])


def at(value, index, dim=0):
    return lax.dynamic_index_in_dim(value, index, dim, keepdims=False)


def cube(wide):
    steps = []
    bits = 1
    while bits < wide:
        steps.append((WIDE, bits))
        bits *= 2
    return steps + [(NARROW, 1), (NARROW, 2)]


def cube_gather(row):
    for axis, bits in cube(lax.axis_size(WIDE)):
        other = flip(row, axis, bits)
        high = (lax.axis_index(axis) & bits) > 0
        row = jnp.concatenate(
            [jnp.where(high, other, row), jnp.where(high, row, other)], axis=0
        )
    return row


def cube_scatter(table, event):
    wide = lax.axis_size(WIDE)
    steps = cube(wide)
    table = table.reshape((2,) * len(steps) + (table.shape[-1],))
    order = [len(steps) - 2, len(steps) - 1] + list(range(len(steps) - 2))[::-1]
    left = list(range(len(steps)))
    for k in order:
        axis, bits = steps[k]
        dim = len(left) - 1 - left.index(k)
        high = ((lax.axis_index(axis) & bits) > 0).astype(jnp.int32)
        table = at(table, high, dim) + flip(at(table, 1 - high, dim), axis, bits)
        left.remove(k)
        if len(left) == len(steps) - 2:
            table = hold(table, event)
    return table


def narrow_gather(own, made=None):
    across = flip(own, NARROW, 2)
    beside = flip(own, NARROW, 1)
    if made is not None:
        across = hold(across, *made(beside))
    return [own, beside, across, flip(across, NARROW, 1)]


def narrow_scatter(parts):
    f32 = jnp.float32
    far = flip(parts[3], NARROW, 1)
    near = flip(parts[1], NARROW, 1)
    passed = (parts[2].astype(f32) + far.astype(f32)).astype(jnp.bfloat16)
    across = flip(passed, NARROW, 2)
    return parts[0].astype(f32) + near.astype(f32) + across.astype(f32)


def hold(value, *events):
    return lax.optimization_barrier((value,) + events)[0]


def hold_all(values, *events):
    return lax.optimization_barrier(tuple(values) + events)[: len(values)]


def bit_of(axis, bits):
    return (lax.axis_index(axis) & bits) > 0


def in_order(relative):
    swap = bit_of(NARROW, 1)
    r = [
        jnp.where(swap, relative[k ^ 1], relative[k]) for k in range(4)
    ]
    swap = bit_of(NARROW, 2)
    return jnp.stack([jnp.where(swap, r[k ^ 2], r[k]) for k in range(4)])


def narrow_blocks(block_of):
    me = lax.axis_index(NARROW)
    return [flip(block_of(me ^ j), NARROW, j) if j else block_of(me) for j in range(4)]


def narrow_swap(block_of):
    return in_order(narrow_blocks(block_of))


def pair_swap(block_of):
    me = lax.axis_index(WIDE) & 1
    own, other = block_of(me), flip(block_of(1 - me), WIDE, 1)
    high = me > 0
    return jnp.stack([jnp.where(high, other, own), jnp.where(high, own, other)])


def spread_near(own):
    half = own.shape[1] // 2
    over_y = flip(own, WIDE, 1)
    over_x = flip(own, NARROW, 2)
    both = jnp.concatenate(
        [flip(over_y[:, :half], NARROW, 2), flip(over_x[:, half:], WIDE, 1)], axis=1
    )
    return [own, over_x, over_y, both]


def spread(own):
    near = spread_near(own)
    return near + [flip(part, NARROW, 1) for part in near]


def fold(far, near, made=None):
    f32, bf16 = jnp.float32, jnp.bfloat16
    width = far.shape[-1]
    half = width // 2
    far, near = far.reshape(4, -1, width), near.reshape(4, -1, width)
    far = flip(far, NARROW, 1)
    both = (near[3].astype(f32) + far[3].astype(f32)).astype(bf16)
    own, over_x, over_y = [near[k].astype(f32) + far[k].astype(f32) for k in range(3)]
    first = flip(both[:, :half], WIDE, 1).astype(f32)
    last = flip(both[:, half:], NARROW, 2).astype(f32)
    over_x = jnp.concatenate([over_x[:, :half] + first, over_x[:, half:]], axis=1).astype(bf16)
    over_y = jnp.concatenate([over_y[:, :half], over_y[:, half:] + last], axis=1).astype(bf16)
    last = flip(over_x, NARROW, 2)
    if made is not None:
        last = hold(last, made(over_x))
    return own + last.astype(f32) + flip(over_y, WIDE, 1).astype(f32)


def columns(wide):
    return [list(range(y, wide, 2)) for y in range(2)]


def z_gather(shard, axis):
    groups = columns(lax.axis_size(WIDE))
    return lax.all_gather(shard, WIDE, axis=axis, tiled=True, axis_index_groups=groups)


def z_scatter(full, axis):
    groups = columns(lax.axis_size(WIDE))
    return lax.psum_scatter(
        full.astype(jnp.bfloat16), WIDE, scatter_dimension=axis, tiled=True, axis_index_groups=groups
    )


def ring_order(wide):
    return list(range(0, wide, 2)) + list(range(wide - 1, 0, -2))


def ring_at(position, wide):
    position = position % wide
    return jnp.where(position < wide // 2, 2 * position, 2 * (wide - 1 - position) + 1)


def ring_position(wide):
    me = lax.axis_index(WIDE)
    return jnp.where(me % 2 == 0, me // 2, wide - 1 - me // 2)


def ring_step(value, by):
    order = ring_order(lax.axis_size(WIDE))
    size = len(order)
    return lax.ppermute(
        value, WIDE, [(order[i], order[(i + by) % size]) for i in range(size)]
    )


def ring_gather(shard):
    wide = lax.axis_size(WIDE)
    here = ring_position(wide)
    middle = shard.shape[-1] // 2
    full = jnp.zeros((wide,) + shard.shape, shard.dtype)

    def put(full, piece, position):
        return lax.dynamic_update_slice_in_dim(
            full, piece[None], ring_at(position + wide, wide), 0
        )

    full = put(full, shard, here)
    ahead = behind = shard
    for k in range(1, wide // 2):
        ahead, behind = ring_step(ahead, 1), ring_step(behind, -1)
        full = put(put(full, ahead, here - k), behind, here + k)
    ahead = ring_step(ahead[..., :middle], 1)
    behind = ring_step(behind[..., middle:], -1)
    return put(full, jnp.concatenate([ahead, behind], axis=-1), here + wide // 2)


def ring_scatter(full, beside):
    wide = lax.axis_size(WIDE)
    here = ring_position(wide)
    bf16, f32 = jnp.bfloat16, jnp.float32
    middle = full.shape[-1] // 2

    def local(position):
        return at(full, ring_at(position + wide, wide))

    far = local(here + wide // 2)
    ahead, behind = lax.optimization_barrier((far[..., :middle], far[..., middle:]))
    event = ahead
    stage = 0
    for k in range(wide // 2 - 1, -1, -1):
        ahead, behind = ring_step(ahead, 1).astype(f32), ring_step(behind, -1).astype(f32)
        values = beside(stage, event)
        stage += 1
        if k == 0:
            break
        to_ahead, to_behind = local(here + k).astype(f32), local(here - k).astype(f32)
        if k == wide // 2 - 1:
            to_ahead = jnp.concatenate(
                [to_ahead[..., :middle] + ahead, to_ahead[..., middle:]], axis=-1
            )
            to_behind = jnp.concatenate(
                [to_behind[..., :middle], to_behind[..., middle:] + behind], axis=-1
            )
        else:
            to_ahead, to_behind = to_ahead + ahead, to_behind + behind
        ahead, behind = lax.optimization_barrier(
            (to_ahead.astype(bf16), to_behind.astype(bf16)) + values
        )[:2]
        event = ahead
    return local(here).astype(f32) + ahead + behind


def wide_swap(parts):
    return lax.all_to_all(parts, WIDE, split_axis=0, concat_axis=0, tiled=True)


def wide_gather(shard, axis):
    return lax.all_gather(shard, WIDE, axis=axis, tiled=True)


def wide_scatter(full, axis):
    return lax.psum_scatter(full.astype(jnp.bfloat16), WIDE, scatter_dimension=axis, tiled=True)


def vmem_specs(count):
    return [pl.BlockSpec(memory_space=pltpu.VMEM)] * count


SMEM_SPEC = pl.BlockSpec(memory_space=pltpu.SMEM)
BIG = pltpu.CompilerParams(vmem_limit_bytes=48 << 20)
CONTRACT_LAST = (((1,), (1,)), ((), ()))
CONTRACT_FIRST = (((0,), (0,)), ((), ()))


def project_kernel(*refs, heads, by_last):
    rows, (weight_ref, bias_ref, out_ref) = refs[:-3], refs[-3:]
    units, parts, _, tokens, head_dim = out_ref.shape
    for j, rows_ref in enumerate(rows):

        @pl.when(pl.program_id(0) == j)
        def _():
            if by_last:
                acc = lax.dot_general(
                    rows_ref[...], weight_ref[...], CONTRACT_LAST, preferred_element_type=jnp.float32
                )
            else:
                acc = jnp.dot(rows_ref[...], weight_ref[...], preferred_element_type=jnp.float32)
            acc = (acc + bias_ref[...]).astype(jnp.bfloat16)
            for unit in range(units):
                b, h = divmod(unit, heads)
                for part in range(parts):
                    c = (part * heads + h) * head_dim
                    out_ref[unit, part, 0] = acc[
                        b * tokens : (b + 1) * tokens, c : c + head_dim
                    ]


def resident(shape):
    return pl.BlockSpec(shape, lambda i: (0,) * len(shape), pipeline_mode=pl.Buffered(1))


def project(rows, weight, bias, units, parts, heads, tokens, by_last):
    blocks = len(rows)
    head_dim = bias.shape[0] // (parts * heads)
    return pl.pallas_call(
        functools.partial(project_kernel, heads=heads, by_last=by_last),
        grid=(blocks,),
        out_shape=jax.ShapeDtypeStruct((units, parts, blocks, tokens, head_dim), jnp.bfloat16),
        in_specs=[resident(block.shape) for block in rows]
        + [resident(weight.shape), resident((1, bias.shape[0]))],
        out_specs=pl.BlockSpec(
            (units, parts, 1, tokens, head_dim), lambda i: (0, 0, i, 0, 0)
        ),
        compiler_params=BIG,
        name="project",
    )(*rows, weight, bias.reshape(1, -1))


def project_parts_kernel(*refs, heads, blocks):
    rows, weights, (bias_ref, out_ref) = refs[:blocks], refs[blocks:-2], refs[-2:]
    units, parts, _, tokens, head_dim = out_ref.shape
    depth = rows[0].shape[1] // len(weights)
    for j, rows_ref in enumerate(rows):

        @pl.when(pl.program_id(0) == j)
        def _():
            acc = bias_ref[...]
            for k, weight_ref in enumerate(weights):
                acc = acc + jnp.dot(
                    rows_ref[:, k * depth : (k + 1) * depth],
                    weight_ref[...].reshape(depth, -1),
                    preferred_element_type=jnp.float32,
                )
            acc = acc.astype(jnp.bfloat16)
            for unit in range(units):
                b, h = divmod(unit, heads)
                for part in range(parts):
                    c = (part * heads + h) * head_dim
                    out_ref[unit, part, 0] = acc[b * tokens : (b + 1) * tokens, c : c + head_dim]


def project_parts(rows, weight, bias, units, parts, heads, tokens):
    blocks, head_dim = len(rows), bias.shape[0] // (parts * heads)
    wide, narrow, shard, _ = weight.shape
    width = bias.shape[0]
    return pl.pallas_call(
        functools.partial(project_parts_kernel, heads=heads, blocks=blocks),
        grid=(blocks,),
        out_shape=jax.ShapeDtypeStruct((units, parts, blocks, tokens, head_dim), jnp.bfloat16),
        in_specs=[resident(block.shape) for block in rows]
        + [
            pl.BlockSpec(
                (wide, 1, shard, width), lambda i, k=k: (0, k, 0, 0), pipeline_mode=pl.Buffered(1)
            )
            for k in range(narrow)
        ]
        + [resident((1, bias.shape[0]))],
        out_specs=pl.BlockSpec((units, parts, 1, tokens, head_dim), lambda i: (0, 0, i, 0, 0)),
        compiler_params=BIG,
        name="project_parts",
    )(*rows, *[weight] * narrow, bias.reshape(1, -1))


def times_parts_kernel(rows_ref, weight_ref, out_ref):
    inner = rows_ref.shape[1]
    weight = weight_ref[...].reshape(out_ref.shape[1], -1)[:, :inner]
    acc = lax.dot_general(
        rows_ref[...], weight, CONTRACT_LAST, preferred_element_type=jnp.float32
    )
    out_ref[...] = acc.astype(jnp.bfloat16)


def times_parts(rows, block, count, weight):
    gathered, narrow, shard, _ = weight.shape
    inner = rows.shape[1]
    step = gathered * shard
    return pl.pallas_call(
        times_parts_kernel,
        grid=(narrow,),
        out_shape=jax.ShapeDtypeStruct((count, narrow * step), jnp.bfloat16),
        in_specs=[
            pl.BlockSpec((count, inner), lambda i: (block, 0), pipeline_mode=pl.Buffered(1)),
            pl.BlockSpec((gathered, 1, shard, inner), lambda i: (0, i, 0, 0)),
        ],
        out_specs=pl.BlockSpec((count, step), lambda i: (0, i)),
        compiler_params=BIG,
        name="times_parts",
    )(rows, weight)


def wide_outer_kernel(*refs):
    lefts, (right_ref, extra_ref, out_ref) = refs[:-3], refs[-3:]
    pair, narrow, shard, total = out_ref.shape
    width = right_ref.shape[1]
    more = total - width
    for n in range(narrow):
        left = jnp.concatenate([ref[...] for ref in lefts[n::narrow]], axis=0)
        acc = lax.dot_general(
            left, right_ref[...], CONTRACT_FIRST, preferred_element_type=jnp.float32
        )
        for y in range(pair):
            out_ref[y, n, :, :width] = acc[y * shard : (y + 1) * shard].astype(jnp.bfloat16)
        for y in range(pair):
            out_ref[y, n, :, width:] = extra_ref[
                y * shard : (y + 1) * shard, n * more : (n + 1) * more
            ]


def wide_outer(lefts, right, extra, wide):
    shard, narrow, width = extra.shape[0] // wide, 4, right.shape[1]
    more = extra.shape[1] // narrow
    block = lefts[0].shape[0]
    deep = wide // 2
    return pl.pallas_call(
        wide_outer_kernel,
        grid=(deep,),
        out_shape=jax.ShapeDtypeStruct((wide, narrow, shard, width + more), jnp.bfloat16),
        in_specs=[
            pl.BlockSpec((block, 2 * shard), lambda i, n=n: (0, n * deep + i))
            for _ in lefts
            for n in range(narrow)
        ]
        + [
            resident(right.shape),
            pl.BlockSpec((2 * shard, extra.shape[1]), lambda i: (i, 0)),
        ],
        out_specs=pl.BlockSpec((2, narrow, shard, width + more), lambda i: (i, 0, 0, 0)),
        compiler_params=BIG,
        name="wide_outer",
    )(*[left for left in lefts for _ in range(narrow)], right, extra)


def row_block(parts_ref, j, b, heads):
    return jnp.concatenate(
        [
            parts_ref[b * heads + h, part, j]
            for part in range(parts_ref.shape[1])
            for h in range(heads)
        ],
        axis=1,
    )


def unproject_kernel(parts_ref, weight_ref, *refs, heads, order):
    outs, rows_ref = refs[:-1], refs[-1]
    for step, j in enumerate(order):

        @pl.when(pl.program_id(0) == step)
        def _():
            rows = jnp.concatenate(
                [row_block(parts_ref, j, b, heads) for b in range(parts_ref.shape[0] // heads)],
                axis=0,
            )
            rows_ref[j] = rows
            acc = jnp.dot(rows, weight_ref[...], preferred_element_type=jnp.float32)
            outs[j][...] = acc.astype(jnp.bfloat16)


def unproject(parts, weight, heads):
    units, count, blocks, tokens, head_dim = parts.shape
    step = tokens * units // heads
    inner = count * heads * head_dim
    width = weight.shape[1]
    results = pl.pallas_call(
        functools.partial(unproject_kernel, heads=heads, order=(3, 1, 2, 0)),
        grid=(blocks,),
        out_shape=[jax.ShapeDtypeStruct((step, width), jnp.bfloat16)] * blocks
        + [jax.ShapeDtypeStruct((blocks, step, inner), jnp.bfloat16)],
        in_specs=[resident(parts.shape), resident(weight.shape)],
        out_specs=[pl.BlockSpec((step, width), lambda i: (0, 0))] * blocks
        + [pl.BlockSpec((blocks, step, inner), lambda i: (0, 0, 0))],
        compiler_params=BIG,
        name="unproject",
    )(parts, weight)
    return results[:blocks], results[blocks].reshape(blocks * step, inner)


def join_kernel(parts_ref, rows_ref, *, heads, order):
    units, tokens = parts_ref.shape[0], parts_ref.shape[3]
    row = 0
    for j in order:
        for b in range(units // heads):
            rows_ref[row : row + tokens] = row_block(parts_ref, j, b, heads)
            row += tokens


def join(parts, heads, order):
    units, count, blocks, tokens, head_dim = parts.shape
    return pl.pallas_call(
        functools.partial(join_kernel, heads=heads, order=order),
        out_shape=jax.ShapeDtypeStruct(
            (blocks * tokens * units // heads, count * heads * head_dim), jnp.bfloat16
        ),
        in_specs=vmem_specs(1),
        out_specs=vmem_specs(1)[0],
        compiler_params=BIG,
        name="join",
    )(parts)


def mask_of(segc_ref, segr_ref, i, lo):
    keys = 512 * (i + 1 - lo)
    same = segc_ref[i] == segr_ref[:, 512 * lo : 512 * (i + 1)]
    rows = lax.broadcasted_iota(jnp.int32, (512, keys), 0) + 512 * (i - lo)
    cols = lax.broadcasted_iota(jnp.int32, (512, keys), 1)
    return jnp.logical_and(same, cols <= rows)


def take(me_ref, parts_ref, part, first, last, half):
    blocks = [
        parts_ref[4 * (i % half) : 4 * (i % half) + 4, part, (i // half) ^ me_ref[0]].reshape(512, -1)
        for i in range(first, last + 1)
    ]
    return blocks[0] if len(blocks) == 1 else jnp.concatenate(blocks, axis=0)


def give(me_ref, out_ref, part, i, half, rows):
    rows = rows.astype(out_ref.dtype).reshape(4, 128, -1)
    out_ref[4 * (i % half) : 4 * (i % half) + 4, part, (i // half) ^ me_ref[0]] = rows


def fwd_kernel(me_ref, segc_ref, segr_ref, parts_ref, out_ref, lse_ref, *, blocks, scale2):
    half = blocks // 4
    for i in range(blocks):
        lo = max(i - 1, 0)
        q = take(me_ref, parts_ref, 0, i, i, half)
        k = take(me_ref, parts_ref, 1, lo, i, half)
        v = take(me_ref, parts_ref, 2, lo, i, half)
        s = lax.dot_general(q, k, CONTRACT_LAST, preferred_element_type=jnp.float32)
        s = jnp.where(mask_of(segc_ref, segr_ref, i, lo), s * scale2, neg_big)
        m = jnp.max(s, axis=-1, keepdims=True)
        p = jnp.exp2(s - m)
        total = jnp.sum(p, axis=-1, keepdims=True)
        o = jnp.dot(p.astype(jnp.bfloat16), v, preferred_element_type=jnp.float32)
        give(me_ref, out_ref, 0, i, half, o / total)
        lse_ref[i] = m + jnp.log2(total)


def bwd_kernel(
    me_ref, segc_ref, segr_ref, lse_ref, parts_ref, do_ref, grad_ref, dk_acc, dv_acc, *, blocks, scale, scale2
):
    half = blocks // 4
    f32 = jnp.float32
    for i in range(blocks):
        lo = max(i - 1, 0)
        q = take(me_ref, parts_ref, 0, i, i, half)
        k = take(me_ref, parts_ref, 1, lo, i, half)
        v = take(me_ref, parts_ref, 2, lo, i, half)
        do = take(me_ref, do_ref, 0, i, i, half)
        s = lax.dot_general(q, k, CONTRACT_LAST, preferred_element_type=f32)
        s = jnp.where(mask_of(segc_ref, segr_ref, i, lo), s * scale2, neg_big)
        p = jnp.exp2(s - lse_ref[i])
        dp = lax.dot_general(do, v, CONTRACT_LAST, preferred_element_type=f32)
        t = p * dp
        delta = jnp.sum(t, axis=-1, keepdims=True)
        ds = (t - p * delta).astype(jnp.bfloat16)
        give(me_ref, grad_ref, 0, i, half, jnp.dot(ds, k, preferred_element_type=f32) * scale)
        dk = lax.dot_general(ds, q, CONTRACT_FIRST, preferred_element_type=f32)
        dv = lax.dot_general(
            p.astype(jnp.bfloat16), do, CONTRACT_FIRST, preferred_element_type=f32
        )
        if i > 0:
            give(me_ref, grad_ref, 1, i - 1, half, (dk_acc[...] + dk[:512]) * scale)
            give(me_ref, grad_ref, 2, i - 1, half, dv_acc[...] + dv[:512])
        if i == blocks - 1:
            give(me_ref, grad_ref, 1, i, half, dk[-512:] * scale)
            give(me_ref, grad_ref, 2, i, half, dv[-512:])
        else:
            dk_acc[...] = dk[-512:]
            dv_acc[...] = dv[-512:]


def attend_fwd(me, segc, segr, parts):
    blocks = segc.shape[0]
    units, _, narrow, rows, width = parts.shape
    scale2 = math.log2(math.e) / math.sqrt(width)
    return pl.pallas_call(
        functools.partial(fwd_kernel, blocks=blocks, scale2=scale2),
        out_shape=(
            jax.ShapeDtypeStruct((units, 1, narrow, rows, width), jnp.bfloat16),
            jax.ShapeDtypeStruct((blocks, 512, 1), jnp.float32),
        ),
        in_specs=[SMEM_SPEC] + vmem_specs(3),
        out_specs=tuple(vmem_specs(2)),
        compiler_params=BIG,
        name="attend_fwd",
    )(me, segc, segr, parts)


def attend_bwd(me, segc, segr, lse, parts, dout):
    blocks = segc.shape[0]
    width = parts.shape[-1]
    scale = 1.0 / math.sqrt(width)
    return pl.pallas_call(
        functools.partial(
            bwd_kernel, blocks=blocks, scale=scale, scale2=scale * math.log2(math.e)
        ),
        out_shape=jax.ShapeDtypeStruct(parts.shape, jnp.bfloat16),
        in_specs=[SMEM_SPEC] + vmem_specs(5),
        out_specs=vmem_specs(1)[0],
        scratch_shapes=[pltpu.VMEM((512, width), jnp.float32)] * 2,
        compiler_params=BIG,
        name="attend_bwd",
    )(me, segc, segr, lse, parts, dout)


def ff_kernel(rows_ref, *refs):
    weights, (bias_ref, hidden_ref, slope_ref) = refs[:-3], refs[-3:]
    step = 256
    depth = rows_ref.shape[1] // len(weights)
    for r in range(0, rows_ref.shape[0], step):
        x = bias_ref[...]
        for n, weight_ref in enumerate(weights):
            x = x + jnp.dot(
                rows_ref[r : r + step, n * depth : (n + 1) * depth],
                weight_ref[...].reshape(depth, -1),
                preferred_element_type=jnp.float32,
            )
        below = 0.5 * (1.0 + lax.erf(x * math.sqrt(0.5)))
        hidden_ref[r : r + step] = (x * below).astype(jnp.bfloat16)
        slope_ref[r : r + step] = below + x * (
            jnp.exp(-0.5 * x * x) * (1.0 / math.sqrt(2.0 * math.pi))
        )


def feed_forward(rows, weight, bias):
    count = rows.shape[0]
    deep, narrow, shard, inner = weight.shape
    step = 256
    return pl.pallas_call(
        ff_kernel,
        grid=(inner // step,),
        out_shape=(
            jax.ShapeDtypeStruct((count, inner), jnp.bfloat16),
            jax.ShapeDtypeStruct((count, inner), jnp.float32),
        ),
        in_specs=[resident(rows.shape)]
        + [
            pl.BlockSpec((deep, 1, shard, step), lambda i, n=n: (0, n, 0, i)) for n in range(narrow)
        ]
        + [pl.BlockSpec((1, step), lambda i: (0, i))],
        out_specs=(
            pl.BlockSpec((count, step), lambda i: (0, i)),
            pl.BlockSpec((count, step), lambda i: (0, i)),
        ),
        compiler_params=BIG,
        name="feed_forward",
    )(rows, *[weight] * narrow, bias.reshape(1, -1))


def pull_kernel(rows_ref, weight_ref, slope_ref, grad_ref, sum_ref):
    step = 256
    total = jnp.zeros((1, weight_ref.shape[0]), jnp.float32)
    for r in range(0, rows_ref.shape[0], step):
        pull = lax.dot_general(
            rows_ref[r : r + step],
            weight_ref[...],
            CONTRACT_LAST,
            preferred_element_type=jnp.float32,
        )
        grad = (pull * slope_ref[r : r + step]).astype(jnp.bfloat16)
        grad_ref[r : r + step] = grad
        total = total + jnp.sum(grad.astype(jnp.float32), axis=0, keepdims=True)
    sum_ref[...] = total


def pull_back(rows, weight, slope):
    count, inner = slope.shape
    width = weight.shape[1]
    step = 256
    return pl.pallas_call(
        pull_kernel,
        grid=(inner // step,),
        out_shape=(
            jax.ShapeDtypeStruct((count, inner), jnp.bfloat16),
            jax.ShapeDtypeStruct((1, inner), jnp.float32),
        ),
        in_specs=[
            resident(rows.shape),
            pl.BlockSpec((step, width), lambda i: (i, 0)),
            pl.BlockSpec((count, step), lambda i: (0, i)),
        ],
        out_specs=(
            pl.BlockSpec((count, step), lambda i: (0, i)),
            pl.BlockSpec((1, step), lambda i: (0, i)),
        ),
        compiler_params=BIG,
        name="pull_back",
    )(rows, weight, slope)


def place_qkv_kernel(me_ref, *refs):
    pieces, outs = refs[:4], refs[4:]
    cols = pieces[0].shape[1] // len(outs)
    for part, out_ref in enumerate(outs):
        blocks = [piece[:, part * cols : (part + 1) * cols].astype(jnp.float32) for piece in pieces]
        for n in range(4):
            value = blocks[n]
            for me in range(1, 4):
                value = jnp.where(me_ref[0] == me, blocks[n ^ me], value)
            out_ref[:, n * cols : (n + 1) * cols] = value


def place_qkv(me, pieces):
    rows, width = pieces[0].shape
    shape = jax.ShapeDtypeStruct((rows, width // 3 * 4), jnp.float32)
    return pl.pallas_call(
        place_qkv_kernel,
        out_shape=(shape,) * 3,
        in_specs=[SMEM_SPEC] + vmem_specs(4),
        out_specs=tuple(vmem_specs(3)),
        compiler_params=BIG,
        name="place_qkv",
    )(me, *pieces)


def place_up_kernel(me_ref, own_ref, other_ref, out_ref, *, step):
    narrow, _, inner = own_ref.shape
    high = (me_ref[1] & 1) > 0
    for n in range(narrow):
        own, other = own_ref[n ^ me_ref[0]], other_ref[n ^ me_ref[0]]
        for z in range(inner // step):
            c = (n * (inner // step) + z) * 2 * step
            a = own[:, z * step : (z + 1) * step].astype(jnp.float32)
            b = other[:, z * step : (z + 1) * step].astype(jnp.float32)
            out_ref[:, c : c + step] = jnp.where(high, b, a)
            out_ref[:, c + step : c + 2 * step] = jnp.where(high, a, b)


def place_up(me, own, other, step):
    narrow, shard, inner = own.shape
    return pl.pallas_call(
        functools.partial(place_up_kernel, step=step),
        out_shape=jax.ShapeDtypeStruct((shard, 2 * narrow * inner), jnp.float32),
        in_specs=[SMEM_SPEC] + vmem_specs(2),
        out_specs=vmem_specs(1)[0],
        compiler_params=BIG,
        name="place_up",
    )(me, own, other)


def pick_kernel(me_ref, weight_ref, out_ref):
    _, narrow, shard, inner = out_ref.shape
    high = (me_ref[1] & 1) > 0
    step = 256
    for n in range(narrow):
        for z in range(inner // step):
            c = (n * (inner // step) + z) * 2 * step
            low_part = weight_ref[:, c : c + step]
            high_part = weight_ref[:, c + step : c + 2 * step]
            cols = slice(z * step, (z + 1) * step)
            out_ref[0, n, :, cols] = jnp.where(high, high_part, low_part)
            out_ref[1, n, :, cols] = jnp.where(high, low_part, high_part)


def pick(me, weight, narrow):
    shard, total = weight.shape
    return pl.pallas_call(
        pick_kernel,
        out_shape=jax.ShapeDtypeStruct((2, narrow, shard, total // (2 * narrow)), weight.dtype),
        in_specs=[SMEM_SPEC] + vmem_specs(1),
        out_specs=vmem_specs(1)[0],
        compiler_params=BIG,
        name="pick",
    )(me, weight)


def on_device(
    block_input,
    segment_ids,
    cotangent,
    attn_gain,
    attn_shift,
    query_weight,
    query_bias,
    key_weight,
    value_weight,
    value_bias,
    out_weight,
    out_bias,
    mlp_gain,
    mlp_shift,
    up_weight,
    up_bias,
    down_weight,
    down_bias,
):
    f32 = jnp.float32
    bf16 = jnp.bfloat16
    batch, tokens, width = block_input.shape
    narrow = lax.axis_size(NARROW)
    wide = lax.axis_size(WIDE)
    me_n = lax.axis_index(NARROW)
    me_w = lax.axis_index(WIDE)
    me = jnp.stack([me_n, me_w]).astype(jnp.int32)
    rows = batch * tokens
    heads = HEADS // narrow
    head_dim = width // HEADS
    cols = heads * head_dim
    shard = width // (narrow * wide)
    deep = wide // 2
    ff_shard = up_bias.shape[0]
    ff_local = ff_shard * deep
    me_y = me_w & 1

    def qkv_block(n):
        return jnp.concatenate(
            [
                lax.dynamic_slice_in_dim(weight, n * cols, cols, 1)
                for weight in (query_weight, key_weight, value_weight)
            ],
            axis=1,
        )

    out_w = wide_gather(out_weight, 0)
    qkv_shard = narrow_swap(qkv_block)
    attn_parts = ring_gather(qkv_shard)

    smalls = [
        attn_gain, attn_shift, out_bias, mlp_gain, mlp_shift, down_bias, query_bias, value_bias, up_bias
    ]
    ids = segment_ids.astype(bf16).reshape(-1)
    small = cube_gather(jnp.concatenate(smalls + [ids])[None])

    def full_vector(k):
        return small[:, k * shard : (k + 1) * shard].reshape(-1).astype(f32)

    gain_attn, shift_attn, obias, gain_mlp, shift_mlp, dbias = [full_vector(k) for k in range(6)]
    mine = lax.dynamic_slice_in_dim(small, me_n * wide, wide, 0)
    qbias = mine[:, 6 * shard : 7 * shard].reshape(-1).astype(f32)
    vbias = mine[:, 7 * shard : 8 * shard].reshape(-1).astype(f32)
    ubias = mine[:, 8 * shard : 8 * shard + ff_shard].reshape(deep, 2, ff_shard)
    ubias = at(ubias, me_y, 1).reshape(-1).astype(f32)
    qkv_bias = jnp.concatenate([qbias, jnp.zeros_like(qbias), vbias])

    inputs = block_input.astype(f32).reshape(rows, width)
    first_norm = narrow_gather(normalize(inputs, gain_attn, shift_attn).astype(bf16))
    cotan_own = cotangent.reshape(rows, width)
    attn_parts = hold(attn_parts, out_w)
    sent = project_parts(first_norm, attn_parts, qkv_bias, wide, 3, heads, tokens)
    qkv = wide_swap(sent)

    picked = pick(me, hold(up_weight, first_norm[3]), narrow)
    high = me_y > 0
    here, there = picked[0], flip(hold(picked[1], sent), WIDE, 1)
    up_pair = jnp.stack([jnp.where(high, there, here), jnp.where(high, here, there)], axis=1)
    up_shard = narrow_swap(lambda n: at(up_pair, n)).reshape(narrow, 2 * shard, ff_local)
    ids = hold(small, sent)[:, -batch * tokens :].reshape(narrow * wide, batch, tokens)
    unit_ids = at(ids, me_w // heads, 1).reshape(-1).astype(jnp.int32)
    segc = unit_ids.reshape(-1, 512, 1)
    segr = unit_ids.reshape(1, -1)
    qkv = hold(qkv, up_shard)
    unit_out, lse = attend_fwd(me, segc, segr, qkv)
    up_parts = z_gather(hold(up_shard, unit_out)[None], 0)
    unit_back = wide_swap(unit_out)
    near = spread_near(hold(cotan_own, unit_out))
    unit_back = hold(unit_back, *near)
    cotan = jnp.concatenate(near + [flip(hold(part, unit_back), NARROW, 1) for part in near], axis=0)
    partial, mixed = unproject(unit_back, out_w, heads)
    middle = inputs + narrow_scatter(partial) + obias
    down_late, middle = lax.optimization_barrier((down_weight, middle, up_parts, cotan))[:2]
    down_w = z_gather(down_late, 0)

    second_norm = spread(normalize(middle, gain_mlp, shift_mlp).astype(bf16))
    second_norm = jnp.concatenate(second_norm, axis=0)
    hidden, slope = feed_forward(second_norm, up_parts, ubias)
    down_grad = outer_sum(hidden, cotan).astype(bf16)
    slope = hold(slope, down_grad)
    down_grad = z_scatter(down_grad, 0)
    inner_grad, ubias_grad = pull_back(cotan, down_w, slope)
    split = inner_grad.shape[0] // 2
    far = times_parts(inner_grad, 1, split, up_parts)
    near = times_parts(hold(inner_grad, far), 0, split, up_parts)
    up_made = []

    def make_up_grad(event):
        up_made.append(outer_sum(second_norm, hold(inner_grad, event)).astype(bf16))
        return up_made[0]

    second_grad = fold(far, near, make_up_grad)
    mlp_pull = jax.vjp(normalize, middle, gain_mlp, shift_mlp)[1]
    middle_part, mgain_grad, mshift_grad = mlp_pull(second_grad)
    middle_grad = cotan_own.astype(f32) + middle_part
    branch_own = middle_grad.astype(bf16)
    dbias_grad = jnp.sum(cotan_own.astype(f32), axis=0)

    obias_grad = jnp.sum(branch_own.astype(f32), axis=0)
    out_made = []

    def make_outputs(beside):
        late = hold(hidden, beside)
        out_made.append(matmul(late[split:], down_w).astype(bf16))
        out_made.append(matmul(late[:split], down_w).astype(bf16))
        return out_made

    branch = narrow_gather(branch_own, make_outputs)
    up_grad = hold(up_made[0], out_made[1], down_grad)
    up_grad = z_scatter(up_grad.reshape(narrow, 2 * deep * shard, ff_local), 1)
    no_bias = jnp.zeros((cols,), f32)
    sent = project(branch, out_w, no_bias, wide, 1, heads, tokens, True)
    out_grad = outer_sum(hold(mixed, sent), jnp.concatenate(branch, axis=0)).astype(bf16)
    output = middle + fold(*hold_all(out_made, sent)) + dbias
    block_output = output.astype(bf16).reshape(batch, tokens, width)
    dout = hold(wide_swap(sent), out_grad, block_output)
    unit_grads = attend_bwd(me, segc, segr, lse, qkv, dout)
    grads = wide_swap(unit_grads)
    up_rows = hold(up_grad, unit_grads).reshape(narrow, 2, shard, ff_local)
    up_sent = up_rows
    up_rows = narrow_blocks(lambda n: at(up_sent, n))
    up_own = jnp.stack([at(block, me_y) for block in up_rows])
    up_other = flip(jnp.stack([at(block, 1 - me_y) for block in up_rows]), WIDE, 1)
    up_back = place_up(me, up_own, up_other, ff_shard)
    down_grad = down_grad.astype(f32)
    grads = hold(grads, up_back)
    order = (1, 3, 0, 2)
    back = join(grads, heads, order)
    sums = wide_outer([first_norm[j] for j in order], back, out_grad, wide)
    made = {}

    def beside(stage, event):
        if stage == 0:
            far = times_parts(hold(back, event), 0, 2 * rows, attn_parts)
            made["far"] = far.reshape(2, rows, width)
            return (far,)
        if stage == 1:
            far = made["far"]
            near = times_parts(hold(back, event), 1, 2 * rows, attn_parts)
            near = near.reshape(2, rows, width)
            made["first"] = narrow_scatter([near[0], far[0], near[1], far[1]])
            return (near,)
        if stage == 2:
            attn_pull = jax.vjp(normalize, inputs, gain_attn, shift_attn)[1]
            input_part, again_grad, ashift_grad = attn_pull(made["first"])
            made["pulled"] = middle_grad + input_part, again_grad, ashift_grad
            return made["pulled"] + (down_grad,)
        return ()

    qkv_rows = ring_scatter(sums, beside).astype(bf16)
    out_grad = qkv_rows[..., 3 * cols :].transpose(1, 0, 2).reshape(shard, width)
    qkv_rows = qkv_rows[..., : 3 * cols]
    swapped = narrow_blocks(lambda n: at(qkv_rows, n))
    qkv_grad = place_qkv(me, swapped)
    back_sums = jnp.sum(back.astype(f32), axis=0)
    input_grad, again_grad, ashift_grad = made["pulled"]
    input_grad = input_grad.reshape(batch, tokens, width)

    fulls = [again_grad, ashift_grad, obias_grad, mgain_grad, mshift_grad, dbias_grad]
    fulls = jnp.concatenate([v.reshape(narrow * wide, shard) for v in fulls], axis=1)
    ubias_rows = jnp.zeros((deep, 2, ff_shard), f32)
    ubias_rows = lax.dynamic_update_slice_in_dim(
        ubias_rows,
        ubias_grad.reshape(deep, 1, ff_shard),
        me_y,
        1,
    )
    slices = [back_sums[:cols], back_sums[2 * cols :], ubias_rows]
    slices = jnp.concatenate([v.reshape(wide, -1) for v in slices], axis=1)
    placed = jnp.zeros((narrow * wide, slices.shape[1]), f32)
    placed = lax.dynamic_update_slice_in_dim(placed, slices, me_n * wide, 0)
    vectors = cube_scatter(jnp.concatenate([fulls, placed], axis=1), swapped[1])

    def vector(k):
        return vectors[k * shard : (k + 1) * shard]

    return (
        block_output,
        input_grad,
        vector(0),
        vector(1),
        qkv_grad[0],
        vector(6),
        qkv_grad[1],
        qkv_grad[2],
        vector(7),
        out_grad.astype(f32),
        vector(2),
        vector(3),
        vector(4),
        up_back,
        vectors[8 * shard :],
        down_grad,
        vector(5),
    )


def body_of(mesh):
    def body(*args):
        batch, tokens, width = args[0].shape
        narrow, wide = mesh.shape[NARROW], mesh.shape[WIDE]
        one_unit = batch * (HEADS // narrow) == wide and tokens == 128 and narrow == 4
        return (on_device if one_unit else on_device_ring)(*args)

    return body


def solution(mesh):
    return jax.shard_map(
        body_of(mesh),
        mesh=mesh,
        in_specs=(
            P(None, BOTH, None),
            P(None, BOTH),
            P(None, BOTH, None),
            P(BOTH),
            P(BOTH),
            P(BOTH, None),
            P(BOTH),
            P(BOTH, None),
            P(BOTH, None),
            P(BOTH),
            P(BOTH, None),
            P(BOTH),
            P(BOTH),
            P(BOTH),
            P(BOTH, None),
            P(BOTH),
            P(BOTH, None),
            P(BOTH),
        ),
        out_specs=(
            P(None, BOTH, None),
            P(None, BOTH, None),
            P(BOTH),
            P(BOTH),
            P(BOTH, None),
            P(BOTH),
            P(BOTH, None),
            P(BOTH, None),
            P(BOTH),
            P(BOTH, None),
            P(BOTH),
            P(BOTH),
            P(BOTH),
            P(BOTH, None),
            P(BOTH),
            P(BOTH, None),
            P(BOTH),
        ),
        check_vma=False,
    )
```

```python
import functools
import math
import jax
import jax.numpy as jnp
from jax import lax
from jax.experimental import pallas as pl
from jax.experimental.pallas import tpu as pltpu
from jax.sharding import PartitionSpec as P
HEADS = 16
NARROW, WIDE = "narrow", "wide"
BOTH = (NARROW, WIDE)
REACH = 4
eps = 1e-05
neg_big = -1e30


def shifted(value, axis, by):
    devices = lax.axis_size(axis)
    return lax.ppermute(value, axis, [(i, (i + by) % devices) for i in range(devices)])


def as_sent(value):

    def short(part):
        return part.astype(jnp.bfloat16) if part.dtype == jnp.float32 else part

    return jax.tree.map(short, value)


def normalize(values, gain, shift):
    center = jnp.mean(values, axis=-1, keepdims=True)
    centered = values - center
    spread = jnp.mean(centered * centered, axis=-1, keepdims=True)
    return centered * lax.rsqrt(spread + eps) * gain + shift


def gelu_exact(values):
    return jax.nn.gelu(values, approximate=False)


def matmul(left, right):
    return jnp.dot(left, right, preferred_element_type=jnp.float32)


def outer_sum(left, right):
    return lax.dot_general(
        left, right, (((0,), (0,)), ((), ())), preferred_element_type=jnp.float32
    )


def times_transpose(left, right):
    return lax.dot_general(
        left, right, (((1,), (1,)), ((), ())), preferred_element_type=jnp.float32
    )


def key_positions(first_row, row_count, tokens, narrow_size, wide_size):
    row_ids = first_row + jnp.arange(row_count, dtype=jnp.int32)
    source_wide = row_ids // (tokens * narrow_size)
    source_narrow = row_ids // tokens % narrow_size
    return (source_narrow * wide_size + source_wide) * tokens + row_ids % tokens


def block_mask(query_segs, query_pos, key_segs, key_pos):
    same_doc = query_segs[:, :, None] == key_segs[:, None, :]
    causal = key_pos[None, None, :] <= query_pos[None, :, None]
    return jnp.logical_and(same_doc, causal)


def raw_scores(query_rows, key_rows, score_scale, allowed):
    scores = (
        jnp.einsum("bqhd,bkhd->bhqk", query_rows, key_rows, preferred_element_type=jnp.float32)
        * score_scale
    )
    return jnp.where(allowed[:, None], scores, neg_big)


def forward_block(running, query_heads, key_block, value_block, allowed, score_scale):
    row_max, row_total, weighted = running
    scores = raw_scores(query_heads, key_block, score_scale, allowed)
    new_max = jnp.maximum(row_max, jnp.max(scores, axis=-1))
    rescale = jnp.exp(row_max - new_max)
    exp_terms = jnp.where(allowed[:, None], jnp.exp(scores - new_max[..., None]), 0.0)
    row_total = row_total * rescale + jnp.sum(exp_terms, axis=-1)
    added = jnp.einsum(
        "bhqk,bkhd->bqhd",
        exp_terms.astype(jnp.bfloat16),
        value_block,
        preferred_element_type=jnp.float32,
    )
    weighted = weighted * jnp.transpose(rescale, (0, 2, 1))[..., None] + added
    return (new_max, row_total, weighted)


def backward_block(
    query_grad,
    query_heads,
    dout_heads,
    key_block,
    value_block,
    allowed,
    delta,
    log_total,
    score_scale,
):
    scores = raw_scores(query_heads, key_block, score_scale, allowed)
    attn_probs = jnp.where(allowed[:, None], jnp.exp(scores - log_total[..., None]), 0.0)
    prob_grad = jnp.einsum(
        "bqhd,bkhd->bhqk", dout_heads, value_block, preferred_element_type=jnp.float32
    )
    score_grad = (attn_probs * (prob_grad - delta[..., None])).astype(jnp.bfloat16)
    query_grad = query_grad + score_scale * jnp.einsum(
        "bhqk,bkhd->bqhd", score_grad, key_block, preferred_element_type=jnp.float32
    )
    key_grad = score_scale * jnp.einsum(
        "bhqk,bqhd->bkhd", score_grad, query_heads, preferred_element_type=jnp.float32
    )
    value_grad = jnp.einsum(
        "bhqk,bqhd->bkhd",
        attn_probs.astype(jnp.bfloat16),
        dout_heads,
        preferred_element_type=jnp.float32,
    )
    return (query_grad, key_grad, value_grad)


def on_device_ring(
    block_input,
    segment_ids,
    cotangent,
    attn_gain,
    attn_shift,
    query_weight,
    query_bias,
    key_weight,
    value_weight,
    value_bias,
    out_weight,
    out_bias,
    mlp_gain,
    mlp_shift,
    up_weight,
    up_bias,
    down_weight,
    down_bias,
):
    batch, tokens, model_width = block_input.shape
    narrow_size = lax.axis_size(NARROW)
    wide_size = lax.axis_size(WIDE)
    wide_index = lax.axis_index(WIDE)
    group_rows = tokens * narrow_size
    heads_local = HEADS // narrow_size
    head_dim = model_width // HEADS
    score_scale = 1.0 / math.sqrt(head_dim)
    f32 = jnp.float32
    bf16 = jnp.bfloat16
    attn_set = (
        lax.all_gather(attn_gain, BOTH, axis=0, tiled=True),
        lax.all_gather(attn_shift, BOTH, axis=0, tiled=True),
        lax.all_gather(query_weight, BOTH, axis=0, tiled=True),
        lax.all_gather(query_bias, BOTH, axis=0, tiled=True),
        lax.all_gather(key_weight, BOTH, axis=0, tiled=True),
        lax.all_gather(value_weight, BOTH, axis=0, tiled=True),
        lax.all_gather(value_bias, BOTH, axis=0, tiled=True),
        lax.all_gather(out_weight, BOTH, axis=0, tiled=True),
        lax.all_gather(out_bias, BOTH, axis=0, tiled=True),
    )
    (
        gain_attn,
        shift_attn,
        query_full,
        qbias_full,
        key_full,
        value_full,
        vbias_full,
        out_full,
        obias_full,
    ) = attn_set
    inputs = block_input.astype(f32).reshape(-1, model_width)
    first_norm = normalize(inputs, gain_attn.astype(f32), shift_attn.astype(f32)).astype(bf16)
    split_shape = (batch, tokens, HEADS, head_dim)
    queries = (
        (matmul(first_norm, query_full) + qbias_full.astype(f32)).astype(bf16).reshape(split_shape)
    )
    key_rows = matmul(first_norm, key_full).astype(bf16).reshape(split_shape)
    value_rows = (
        (matmul(first_norm, value_full) + vbias_full.astype(f32)).astype(bf16).reshape(split_shape)
    )
    query_heads, key_heads, value_heads = (
        lax.all_to_all(queries, NARROW, split_axis=2, concat_axis=1, tiled=True),
        lax.all_to_all(key_rows, NARROW, split_axis=2, concat_axis=1, tiled=True),
        lax.all_to_all(value_rows, NARROW, split_axis=2, concat_axis=1, tiled=True),
    )
    query_segs = lax.all_gather(segment_ids, NARROW, axis=1, tiled=True)
    query_pos = key_positions(wide_index * group_rows, group_rows, tokens, narrow_size, wide_size)

    def block_allowed(cycle_step, seg_block):
        source = (wide_index - cycle_step) % wide_size
        key_pos = key_positions(source * group_rows, group_rows, tokens, narrow_size, wide_size)
        return block_mask(query_segs, query_pos, seg_block, key_pos)

    running = (
        jnp.full((batch, heads_local, group_rows), neg_big, f32),
        jnp.zeros((batch, heads_local, group_rows), f32),
        jnp.zeros((batch, group_rows, heads_local, head_dim), f32),
    )
    travelling = (key_heads, value_heads, query_segs)
    received = []
    for cycle_step in range(REACH + 1):
        if cycle_step > 0:
            travelling = shifted((travelling[0], travelling[1], travelling[2]), WIDE, 1)
        received.append(travelling)
        key_block, value_block, seg_block = travelling
        allowed = block_allowed(cycle_step, seg_block)
        running = forward_block(running, query_heads, key_block, value_block, allowed, score_scale)
    row_max, row_total, weighted = running
    attn_out = weighted / jnp.transpose(row_total, (0, 2, 1))[..., None]
    log_total = row_max + jnp.log(row_total)
    mixed = lax.all_to_all(
        attn_out.astype(bf16), NARROW, split_axis=1, concat_axis=2, tiled=True
    ).reshape(-1, model_width)
    middle = inputs + matmul(mixed, out_full) + obias_full.astype(f32)
    mlp_set = (
        lax.all_gather(mlp_gain, BOTH, axis=0, tiled=True),
        lax.all_gather(mlp_shift, BOTH, axis=0, tiled=True),
        lax.all_gather(up_weight, BOTH, axis=0, tiled=True),
        lax.all_gather(up_bias, BOTH, axis=0, tiled=True),
        lax.all_gather(down_weight, BOTH, axis=0, tiled=True),
        lax.all_gather(down_bias, BOTH, axis=0, tiled=True),
    )
    gain_mlp, shift_mlp, up_full, ubias_full, down_full, dbias_full = mlp_set
    second_norm = normalize(middle, gain_mlp.astype(f32), shift_mlp.astype(f32)).astype(bf16)
    inner = matmul(second_norm, up_full) + ubias_full.astype(f32)
    hidden = gelu_exact(inner).astype(bf16)
    output = middle + matmul(hidden, down_full) + dbias_full.astype(f32)
    block_output = output.astype(bf16).reshape(batch, tokens, model_width)
    mlp_set = (
        lax.all_gather(mlp_gain, BOTH, axis=0, tiled=True),
        lax.all_gather(mlp_shift, BOTH, axis=0, tiled=True),
        lax.all_gather(up_weight, BOTH, axis=0, tiled=True),
        lax.all_gather(up_bias, BOTH, axis=0, tiled=True),
        lax.all_gather(down_weight, BOTH, axis=0, tiled=True),
        lax.all_gather(down_bias, BOTH, axis=0, tiled=True),
    )
    gain_mlp, shift_mlp, up_full, ubias_full, down_full, dbias_full = mlp_set
    cotan_rows = cotangent.reshape(-1, model_width)
    down_grad = outer_sum(hidden, cotan_rows)
    dbias_grad = jnp.sum(cotan_rows.astype(f32), axis=0)
    hidden_grad = times_transpose(cotan_rows, down_full)
    gelu_pull = jax.vjp(gelu_exact, inner)[1]
    inner_grad = gelu_pull(hidden_grad)[0].astype(bf16)
    up_grad = outer_sum(second_norm, inner_grad)
    ubias_grad = jnp.sum(inner_grad.astype(f32), axis=0)
    second_grad = times_transpose(inner_grad, up_full)
    mlp_pull = jax.vjp(normalize, middle, gain_mlp.astype(f32), shift_mlp.astype(f32))[1]
    middle_part, mgain_grad, mshift_grad = mlp_pull(second_grad)
    middle_grad = cotan_rows.astype(f32) + middle_part
    mlp_shards = (
        lax.psum_scatter(mgain_grad, BOTH, scatter_dimension=0, tiled=True),
        lax.psum_scatter(mshift_grad, BOTH, scatter_dimension=0, tiled=True),
        lax.psum_scatter(up_grad, BOTH, scatter_dimension=0, tiled=True),
        lax.psum_scatter(ubias_grad, BOTH, scatter_dimension=0, tiled=True),
        lax.psum_scatter(down_grad, BOTH, scatter_dimension=0, tiled=True),
        lax.psum_scatter(dbias_grad, BOTH, scatter_dimension=0, tiled=True),
    )
    attn_set = (
        lax.all_gather(attn_gain, BOTH, axis=0, tiled=True),
        lax.all_gather(attn_shift, BOTH, axis=0, tiled=True),
        lax.all_gather(query_weight, BOTH, axis=0, tiled=True),
        lax.all_gather(query_bias, BOTH, axis=0, tiled=True),
        lax.all_gather(key_weight, BOTH, axis=0, tiled=True),
        lax.all_gather(value_weight, BOTH, axis=0, tiled=True),
        lax.all_gather(value_bias, BOTH, axis=0, tiled=True),
        lax.all_gather(out_weight, BOTH, axis=0, tiled=True),
        lax.all_gather(out_bias, BOTH, axis=0, tiled=True),
    )
    (
        gain_attn,
        shift_attn,
        query_full,
        qbias_full,
        key_full,
        value_full,
        vbias_full,
        out_full,
        obias_full,
    ) = attn_set
    branch_grad = middle_grad.astype(bf16)
    out_grad = outer_sum(mixed, branch_grad)
    obias_grad = jnp.sum(branch_grad.astype(f32), axis=0)
    mixed_grad = times_transpose(branch_grad, out_full).astype(bf16).reshape(split_shape)
    dout_heads = lax.all_to_all(mixed_grad, NARROW, split_axis=2, concat_axis=1, tiled=True)
    delta = jnp.transpose(jnp.sum(dout_heads.astype(f32) * attn_out, axis=-1), (0, 2, 1))
    travelling = (key_heads, value_heads, query_segs)
    received = []
    for cycle_step in range(REACH + 1):
        if cycle_step > 0:
            travelling = shifted((travelling[0], travelling[1], travelling[2]), WIDE, 1)
        received.append(travelling)
    query_grad = jnp.zeros((batch, group_rows, heads_local, head_dim), f32)
    key_terms = []
    value_terms = []
    for cycle_step in range(REACH + 1):
        key_block, value_block, seg_block = received[cycle_step]
        allowed = block_allowed(cycle_step, seg_block)
        query_grad, key_term, value_term = backward_block(
            query_grad,
            query_heads,
            dout_heads,
            key_block,
            value_block,
            allowed,
            delta,
            log_total,
            score_scale,
        )
        key_terms.append(key_term)
        value_terms.append(value_term)
    carried = (key_terms[REACH], value_terms[REACH])
    for cycle_step in range(REACH - 1, -1, -1):
        arrived = shifted((as_sent(carried[0]), as_sent(carried[1])), WIDE, -1)
        carried = (arrived[0] + key_terms[cycle_step], arrived[1] + value_terms[cycle_step])
    key_sum, value_sum = carried
    query_back, key_back, value_back = (
        lax.all_to_all(query_grad.astype(bf16), NARROW, split_axis=1, concat_axis=2, tiled=True),
        lax.all_to_all(key_sum.astype(bf16), NARROW, split_axis=1, concat_axis=2, tiled=True),
        lax.all_to_all(value_sum.astype(bf16), NARROW, split_axis=1, concat_axis=2, tiled=True),
    )
    query_back = query_back.reshape(-1, model_width)
    key_back = key_back.reshape(-1, model_width)
    value_back = value_back.reshape(-1, model_width)
    query_wgrad = outer_sum(first_norm, query_back)
    qbias_grad = jnp.sum(query_back.astype(f32), axis=0)
    key_wgrad = outer_sum(first_norm, key_back)
    value_wgrad = outer_sum(first_norm, value_back)
    vbias_grad = jnp.sum(value_back.astype(f32), axis=0)
    first_grad = (
        times_transpose(query_back, query_full)
        + times_transpose(key_back, key_full)
        + times_transpose(value_back, value_full)
    )
    attn_pull = jax.vjp(normalize, inputs, gain_attn.astype(f32), shift_attn.astype(f32))[1]
    input_part, again_grad, ashift_grad = attn_pull(first_grad)
    input_grad = (middle_grad + input_part).reshape(batch, tokens, model_width)
    attn_shards = (
        lax.psum_scatter(again_grad, BOTH, scatter_dimension=0, tiled=True),
        lax.psum_scatter(ashift_grad, BOTH, scatter_dimension=0, tiled=True),
        lax.psum_scatter(query_wgrad, BOTH, scatter_dimension=0, tiled=True),
        lax.psum_scatter(qbias_grad, BOTH, scatter_dimension=0, tiled=True),
        lax.psum_scatter(key_wgrad, BOTH, scatter_dimension=0, tiled=True),
        lax.psum_scatter(value_wgrad, BOTH, scatter_dimension=0, tiled=True),
        lax.psum_scatter(vbias_grad, BOTH, scatter_dimension=0, tiled=True),
        lax.psum_scatter(out_grad, BOTH, scatter_dimension=0, tiled=True),
        lax.psum_scatter(obias_grad, BOTH, scatter_dimension=0, tiled=True),
    )
    return (
        block_output,
        input_grad,
        attn_shards[0],
        attn_shards[1],
        attn_shards[2],
        attn_shards[3],
        attn_shards[4],
        attn_shards[5],
        attn_shards[6],
        attn_shards[7],
        attn_shards[8],
        mlp_shards[0],
        mlp_shards[1],
        mlp_shards[2],
        mlp_shards[3],
        mlp_shards[4],
        mlp_shards[5],
    )


def flip(value, axis, bits):
    size = lax.axis_size(axis)
    return lax.ppermute(value, axis, [(i, i ^ bits) for i in range(size)])


def at(value, index, dim=0):
    return lax.dynamic_index_in_dim(value, index, dim, keepdims=False)


def cube(wide):
    steps = []
    bits = 1
    while bits < wide:
        steps.append((WIDE, bits))
        bits *= 2
    return steps + [(NARROW, 1), (NARROW, 2)]


def cube_gather(row):
    for axis, bits in cube(lax.axis_size(WIDE)):
        other = flip(row, axis, bits)
        high = (lax.axis_index(axis) & bits) > 0
        row = jnp.concatenate(
            [jnp.where(high, other, row), jnp.where(high, row, other)], axis=0
        )
    return row


def cube_scatter(table, event):
    wide = lax.axis_size(WIDE)
    steps = cube(wide)
    table = table.reshape((2,) * len(steps) + (table.shape[-1],))
    order = [len(steps) - 2, len(steps) - 1] + list(range(len(steps) - 2))[::-1]
    left = list(range(len(steps)))
    for k in order:
        axis, bits = steps[k]
        dim = len(left) - 1 - left.index(k)
        high = ((lax.axis_index(axis) & bits) > 0).astype(jnp.int32)
        table = at(table, high, dim) + flip(at(table, 1 - high, dim), axis, bits)
        left.remove(k)
        if len(left) == len(steps) - 2:
            table = hold(table, event)
    return table


def narrow_gather(own, made=None):
    across = flip(own, NARROW, 2)
    beside = flip(own, NARROW, 1)
    if made is not None:
        across = hold(across, *made(beside))
    return [own, beside, across, flip(across, NARROW, 1)]


def narrow_scatter(parts):
    f32 = jnp.float32
    far = flip(parts[3], NARROW, 1)
    near = flip(parts[1], NARROW, 1)
    passed = (parts[2].astype(f32) + far.astype(f32)).astype(jnp.bfloat16)
    across = flip(passed, NARROW, 2)
    return parts[0].astype(f32) + near.astype(f32) + across.astype(f32)


def hold(value, *events):
    return lax.optimization_barrier((value,) + events)[0]


def hold_all(values, *events):
    return lax.optimization_barrier(tuple(values) + events)[: len(values)]


def bit_of(axis, bits):
    return (lax.axis_index(axis) & bits) > 0


def in_order(relative):
    swap = bit_of(NARROW, 1)
    r = [
        jnp.where(swap, relative[k ^ 1], relative[k]) for k in range(4)
    ]
    swap = bit_of(NARROW, 2)
    return jnp.stack([jnp.where(swap, r[k ^ 2], r[k]) for k in range(4)])


def narrow_blocks(block_of):
    me = lax.axis_index(NARROW)
    return [flip(block_of(me ^ j), NARROW, j) if j else block_of(me) for j in range(4)]


def narrow_swap(block_of):
    return in_order(narrow_blocks(block_of))


def pair_swap(block_of):
    me = lax.axis_index(WIDE) & 1
    own, other = block_of(me), flip(block_of(1 - me), WIDE, 1)
    high = me > 0
    return jnp.stack([jnp.where(high, other, own), jnp.where(high, own, other)])


def spread_near(own):
    half = own.shape[1] // 2
    over_y = flip(own, WIDE, 1)
    over_x = flip(own, NARROW, 2)
    both = jnp.concatenate(
        [flip(over_y[:, :half], NARROW, 2), flip(over_x[:, half:], WIDE, 1)], axis=1
    )
    return [own, over_x, over_y, both]


def spread(own):
    near = spread_near(own)
    return near + [flip(part, NARROW, 1) for part in near]


def fold_first(far, near):
    f32, bf16 = jnp.float32, jnp.bfloat16
    width = far.shape[-1]
    half = width // 2
    far, near = far.reshape(4, -1, width), near.reshape(4, -1, width)
    far = flip(far, NARROW, 1)
    both = (near[3].astype(f32) + far[3].astype(f32)).astype(bf16)
    own, over_x, over_y = [near[k].astype(f32) + far[k].astype(f32) for k in range(3)]
    first = flip(both[:, :half], WIDE, 1).astype(f32)
    last = flip(both[:, half:], NARROW, 2).astype(f32)
    over_x = jnp.concatenate([over_x[:, :half] + first, over_x[:, half:]], axis=1).astype(bf16)
    over_y = jnp.concatenate([over_y[:, :half], over_y[:, half:] + last], axis=1).astype(bf16)
    return own, over_x, over_y


def fold_last(own, over_x, over_y, made=None):
    f32 = jnp.float32
    last = flip(over_x, NARROW, 2)
    if made is not None:
        last = hold(last, made(over_x))
    return own + last.astype(f32) + flip(over_y, WIDE, 1).astype(f32)


def columns(wide):
    return [list(range(y, wide, 2)) for y in range(2)]


def z_gather(shard, axis):
    groups = columns(lax.axis_size(WIDE))
    return lax.all_gather(shard, WIDE, axis=axis, tiled=True, axis_index_groups=groups)


def z_scatter(full, axis):
    groups = columns(lax.axis_size(WIDE))
    return lax.psum_scatter(
        full.astype(jnp.bfloat16), WIDE, scatter_dimension=axis, tiled=True, axis_index_groups=groups
    )


def ring_order(wide):
    return list(range(0, wide, 2)) + list(range(wide - 1, 0, -2))


def ring_at(position, wide):
    position = position % wide
    return jnp.where(position < wide // 2, 2 * position, 2 * (wide - 1 - position) + 1)


def ring_position(wide):
    me = lax.axis_index(WIDE)
    return jnp.where(me % 2 == 0, me // 2, wide - 1 - me // 2)


def ring_step(value, by):
    order = ring_order(lax.axis_size(WIDE))
    size = len(order)
    return lax.ppermute(
        value, WIDE, [(order[i], order[(i + by) % size]) for i in range(size)]
    )


def ring_gather(shard, chunks):
    wide = lax.axis_size(WIDE)
    here = ring_position(wide)
    full = jnp.zeros((wide,) + shard.shape, shard.dtype)
    zero = jnp.int32(0)

    def put(full, piece, position, column):
        where = (ring_at(position + wide, wide).astype(jnp.int32), zero, zero, jnp.int32(column))
        return lax.dynamic_update_slice(full, piece[None], where)

    full = put(full, shard, here, 0)
    step = shard.shape[-1] // chunks
    middle = step // 2
    ahead = [shard[..., c * step : (c + 1) * step] for c in range(chunks)]
    behind = list(ahead)
    for k in range(1, wide // 2):
        for c in range(chunks):
            ahead[c], behind[c] = ring_step(ahead[c], 1), ring_step(behind[c], -1)
        for c in range(chunks):
            full = put(full, ahead[c], here - k, c * step)
            full = put(full, behind[c], here + k, c * step)
    for c in range(chunks):
        left = ring_step(ahead[c][..., :middle], 1)
        right = ring_step(behind[c][..., middle:], -1)
        full = put(full, left, here + wide // 2, c * step)
        full = put(full, right, here + wide // 2, c * step + middle)
    return full


def ring_scatter(full, beside, chunks):
    wide = lax.axis_size(WIDE)
    here = ring_position(wide)
    bf16, f32 = jnp.bfloat16, jnp.float32
    step = full.shape[-1] // chunks
    middle = step // 2

    def local(position, c):
        return at(full, ring_at(position + wide, wide))[..., c * step : (c + 1) * step]

    sent = []
    for c in range(chunks):
        far = local(here + wide // 2, c)
        sent.append(lax.optimization_barrier((far[..., :middle], far[..., middle:])))
    event = sent[0][0]
    for stage, k in enumerate(range(wide // 2 - 1, -1, -1)):
        came = [
            (ring_step(sent[c][0], 1).astype(f32), ring_step(sent[c][1], -1).astype(f32))
            for c in range(chunks)
        ]
        values = beside(stage, event)
        if k == 0:
            break
        sent = []
        for c in range(chunks):
            ahead, behind = came[c]
            to_ahead, to_behind = local(here + k, c).astype(f32), local(here - k, c).astype(f32)
            if k == wide // 2 - 1:
                to_ahead = jnp.concatenate(
                    [to_ahead[..., :middle] + ahead, to_ahead[..., middle:]], axis=-1
                )
                to_behind = jnp.concatenate(
                    [to_behind[..., :middle], to_behind[..., middle:] + behind], axis=-1
                )
            else:
                to_ahead, to_behind = to_ahead + ahead, to_behind + behind
            terms = (to_ahead.astype(bf16), to_behind.astype(bf16)) + (values if c == 0 else ())
            sent.append(lax.optimization_barrier(terms)[:2])
        event = sent[0][0]
    return [
        (local(here, c).astype(f32) + came[c][0] + came[c][1]).astype(bf16) for c in range(chunks)
    ]


def wide_swap(parts):
    return lax.all_to_all(parts, WIDE, split_axis=0, concat_axis=0, tiled=True)


def wide_gather(shard, axis):
    return lax.all_gather(shard, WIDE, axis=axis, tiled=True)


def wide_scatter(full, axis):
    return lax.psum_scatter(full.astype(jnp.bfloat16), WIDE, scatter_dimension=axis, tiled=True)


def vmem_specs(count):
    return [pl.BlockSpec(memory_space=pltpu.VMEM)] * count


SMEM_SPEC = pl.BlockSpec(memory_space=pltpu.SMEM)
BIG = pltpu.CompilerParams(vmem_limit_bytes=48 << 20)
CONTRACT_LAST = (((1,), (1,)), ((), ()))
CONTRACT_FIRST = (((0,), (0,)), ((), ()))


def project_kernel(*refs, heads, by_last):
    rows, (weight_ref, bias_ref, out_ref) = refs[:-3], refs[-3:]
    units, parts, _, tokens, head_dim = out_ref.shape
    for j, rows_ref in enumerate(rows):

        @pl.when(pl.program_id(0) == j)
        def _():
            if by_last:
                acc = lax.dot_general(
                    rows_ref[...], weight_ref[...], CONTRACT_LAST, preferred_element_type=jnp.float32
                )
            else:
                acc = jnp.dot(rows_ref[...], weight_ref[...], preferred_element_type=jnp.float32)
            acc = (acc + bias_ref[...]).astype(jnp.bfloat16)
            for unit in range(units):
                b, h = divmod(unit, heads)
                for part in range(parts):
                    c = (part * heads + h) * head_dim
                    out_ref[unit, part, 0] = acc[
                        b * tokens : (b + 1) * tokens, c : c + head_dim
                    ]


def resident(shape):
    return pl.BlockSpec(shape, lambda i: (0,) * len(shape), pipeline_mode=pl.Buffered(1))


def project(rows, weight, bias, units, parts, heads, tokens, by_last):
    blocks = len(rows)
    head_dim = bias.shape[0] // (parts * heads)
    return pl.pallas_call(
        functools.partial(project_kernel, heads=heads, by_last=by_last),
        grid=(blocks,),
        out_shape=jax.ShapeDtypeStruct((units, parts, blocks, tokens, head_dim), jnp.bfloat16),
        in_specs=[resident(block.shape) for block in rows]
        + [resident(weight.shape), resident((1, bias.shape[0]))],
        out_specs=pl.BlockSpec(
            (units, parts, 1, tokens, head_dim), lambda i: (0, 0, i, 0, 0)
        ),
        compiler_params=BIG,
        name="project",
    )(*rows, weight, bias.reshape(1, -1))


def project_parts_kernel(*refs, heads, blocks):
    rows, weights, (bias_ref, out_ref) = refs[:blocks], refs[blocks:-2], refs[-2:]
    units, parts, _, tokens, head_dim = out_ref.shape
    depth = rows[0].shape[1] // len(weights)
    for j, rows_ref in enumerate(rows):

        @pl.when(pl.program_id(0) == j)
        def _():
            acc = bias_ref[...]
            for k, weight_ref in enumerate(weights):
                acc = acc + jnp.dot(
                    rows_ref[:, k * depth : (k + 1) * depth],
                    weight_ref[...].reshape(depth, -1),
                    preferred_element_type=jnp.float32,
                )
            acc = acc.astype(jnp.bfloat16)
            for unit in range(units):
                b, h = divmod(unit, heads)
                for part in range(parts):
                    c = (part * heads + h) * head_dim
                    out_ref[unit, part, 0] = acc[b * tokens : (b + 1) * tokens, c : c + head_dim]


def project_parts(rows, weight, bias, units, parts, heads, tokens):
    blocks, head_dim = len(rows), bias.shape[0] // (parts * heads)
    wide, narrow, shard, _ = weight.shape
    width = bias.shape[0]
    return pl.pallas_call(
        functools.partial(project_parts_kernel, heads=heads, blocks=blocks),
        grid=(blocks,),
        out_shape=jax.ShapeDtypeStruct((units, parts, blocks, tokens, head_dim), jnp.bfloat16),
        in_specs=[resident(block.shape) for block in rows]
        + [
            pl.BlockSpec(
                (wide, 1, shard, width), lambda i, k=k: (0, k, 0, 0), pipeline_mode=pl.Buffered(1)
            )
            for k in range(narrow)
        ]
        + [resident((1, bias.shape[0]))],
        out_specs=pl.BlockSpec((units, parts, 1, tokens, head_dim), lambda i: (0, 0, i, 0, 0)),
        compiler_params=BIG,
        name="project_parts",
    )(*rows, *[weight] * narrow, bias.reshape(1, -1))


def times_parts_kernel(rows_ref, weight_ref, out_ref):
    inner = rows_ref.shape[1]
    weight = weight_ref[...].reshape(out_ref.shape[1], -1)[:, :inner]
    acc = lax.dot_general(
        rows_ref[...], weight, CONTRACT_LAST, preferred_element_type=jnp.float32
    )
    out_ref[...] = acc.astype(jnp.bfloat16)


def times_parts(rows, block, count, weight):
    gathered, narrow, shard, _ = weight.shape
    inner = rows.shape[1]
    step = gathered * shard
    return pl.pallas_call(
        times_parts_kernel,
        grid=(narrow,),
        out_shape=jax.ShapeDtypeStruct((count, narrow * step), jnp.bfloat16),
        in_specs=[
            pl.BlockSpec((count, inner), lambda i: (block, 0), pipeline_mode=pl.Buffered(1)),
            pl.BlockSpec((gathered, 1, shard, inner), lambda i: (0, i, 0, 0)),
        ],
        out_specs=pl.BlockSpec((count, step), lambda i: (0, i)),
        compiler_params=BIG,
        name="times_parts",
    )(rows, weight)


def wide_outer_kernel(*refs, heads, order):
    lefts, (parts_ref, extra_ref, out_ref, rows_ref) = refs[:-4], refs[-4:]
    pair, narrow, shard, total = out_ref.shape
    width = rows_ref.shape[1]
    more = total - width

    @pl.when(pl.program_id(0) == 0)
    def _():
        tokens = parts_ref.shape[3]
        row = 0
        for j in order:
            for b in range(parts_ref.shape[0] // heads):
                rows_ref[row : row + tokens] = row_block(parts_ref, j, b, heads)
                row += tokens

    for n in range(narrow):
        left = jnp.concatenate([ref[...] for ref in lefts[n::narrow]], axis=0)
        acc = lax.dot_general(
            left, rows_ref[...], CONTRACT_FIRST, preferred_element_type=jnp.float32
        )
        for y in range(pair):
            out_ref[y, n, :, :width] = acc[y * shard : (y + 1) * shard].astype(jnp.bfloat16)
            out_ref[y, n, :, width:] = extra_ref[
                y * shard : (y + 1) * shard, n * more : (n + 1) * more
            ]


def wide_outer(lefts, parts, extra, wide, heads, order):
    narrow = len(lefts)
    units, count, blocks, tokens, head_dim = parts.shape
    shard, width = extra.shape[0] // wide, count * heads * head_dim
    more = extra.shape[1] // narrow
    block = lefts[0].shape[0]
    rows = blocks * tokens * units // heads
    deep = wide // 2
    return pl.pallas_call(
        functools.partial(wide_outer_kernel, heads=heads, order=order),
        grid=(deep,),
        out_shape=(
            jax.ShapeDtypeStruct((wide, narrow, shard, width + more), jnp.bfloat16),
            jax.ShapeDtypeStruct((rows, width), jnp.bfloat16),
        ),
        in_specs=[
            pl.BlockSpec((block, 2 * shard), lambda i, n=n: (0, n * deep + i))
            for _ in lefts
            for n in range(narrow)
        ]
        + [
            resident(parts.shape),
            pl.BlockSpec((2 * shard, extra.shape[1]), lambda i: (i, 0)),
        ],
        out_specs=(
            pl.BlockSpec((2, narrow, shard, width + more), lambda i: (i, 0, 0, 0)),
            pl.BlockSpec((rows, width), lambda i: (0, 0)),
        ),
        compiler_params=BIG,
        name="wide_outer",
    )(*[left for left in lefts for _ in range(narrow)], parts, extra)


def row_block(parts_ref, j, b, heads):
    return jnp.concatenate(
        [
            parts_ref[b * heads + h, part, j]
            for part in range(parts_ref.shape[1])
            for h in range(heads)
        ],
        axis=1,
    )


def unproject_kernel(parts_ref, weight_ref, *refs, heads, order):
    outs, rows_ref = refs[:-1], refs[-1]
    for step, j in enumerate(order):

        @pl.when(pl.program_id(0) == step)
        def _():
            rows = jnp.concatenate(
                [row_block(parts_ref, j, b, heads) for b in range(parts_ref.shape[0] // heads)],
                axis=0,
            )
            rows_ref[j] = rows
            acc = jnp.dot(rows, weight_ref[...], preferred_element_type=jnp.float32)
            outs[j][...] = acc.astype(jnp.bfloat16)


def unproject(parts, weight, heads):
    units, count, blocks, tokens, head_dim = parts.shape
    step = tokens * units // heads
    inner = count * heads * head_dim
    width = weight.shape[1]
    results = pl.pallas_call(
        functools.partial(unproject_kernel, heads=heads, order=(3, 1, 2, 0)),
        grid=(blocks,),
        out_shape=[jax.ShapeDtypeStruct((step, width), jnp.bfloat16)] * blocks
        + [jax.ShapeDtypeStruct((blocks, step, inner), jnp.bfloat16)],
        in_specs=[resident(parts.shape), resident(weight.shape)],
        out_specs=[pl.BlockSpec((step, width), lambda i: (0, 0))] * blocks
        + [pl.BlockSpec((blocks, step, inner), lambda i: (0, 0, 0))],
        compiler_params=BIG,
        name="unproject",
    )(parts, weight)
    return results[:blocks], results[blocks].reshape(blocks * step, inner)


def mask_of(segc_ref, segr_ref, i, lo):
    keys = 512 * (i + 1 - lo)
    same = segc_ref[i] == segr_ref[:, 512 * lo : 512 * (i + 1)]
    rows = lax.broadcasted_iota(jnp.int32, (512, keys), 0) + 512 * (i - lo)
    cols = lax.broadcasted_iota(jnp.int32, (512, keys), 1)
    return jnp.logical_and(same, cols <= rows)


def take(me_ref, parts_ref, part, first, last, half):
    blocks = [
        parts_ref[4 * (i % half) : 4 * (i % half) + 4, part, (i // half) ^ me_ref[0]].reshape(512, -1)
        for i in range(first, last + 1)
    ]
    return blocks[0] if len(blocks) == 1 else jnp.concatenate(blocks, axis=0)


def give(me_ref, out_ref, part, i, half, rows):
    rows = rows.astype(out_ref.dtype).reshape(4, 128, -1)
    out_ref[4 * (i % half) : 4 * (i % half) + 4, part, (i // half) ^ me_ref[0]] = rows


def fwd_kernel(me_ref, segc_ref, segr_ref, parts_ref, out_ref, lse_ref, *, blocks, scale2):
    half = blocks // 4
    for i in range(blocks):
        lo = max(i - 1, 0)
        q = take(me_ref, parts_ref, 0, i, i, half)
        k = take(me_ref, parts_ref, 1, lo, i, half)
        v = take(me_ref, parts_ref, 2, lo, i, half)
        s = lax.dot_general(q, k, CONTRACT_LAST, preferred_element_type=jnp.float32)
        s = jnp.where(mask_of(segc_ref, segr_ref, i, lo), s * scale2, neg_big)
        m = jnp.max(s, axis=-1, keepdims=True)
        p = jnp.exp2(s - m)
        total = jnp.sum(p, axis=-1, keepdims=True)
        o = jnp.dot(p.astype(jnp.bfloat16), v, preferred_element_type=jnp.float32)
        give(me_ref, out_ref, 0, i, half, o / total)
        lse_ref[i] = m + jnp.log2(total)


def bwd_kernel(
    me_ref, segc_ref, segr_ref, lse_ref, parts_ref, do_ref, grad_ref, dk_acc, dv_acc, *, blocks, scale, scale2
):
    half = blocks // 4
    f32 = jnp.float32
    for i in range(blocks):
        lo = max(i - 1, 0)
        q = take(me_ref, parts_ref, 0, i, i, half)
        k = take(me_ref, parts_ref, 1, lo, i, half)
        v = take(me_ref, parts_ref, 2, lo, i, half)
        do = take(me_ref, do_ref, 0, i, i, half)
        s = lax.dot_general(q, k, CONTRACT_LAST, preferred_element_type=f32)
        s = jnp.where(mask_of(segc_ref, segr_ref, i, lo), s * scale2, neg_big)
        p = jnp.exp2(s - lse_ref[i])
        dp = lax.dot_general(do, v, CONTRACT_LAST, preferred_element_type=f32)
        t = p * dp
        delta = jnp.sum(t, axis=-1, keepdims=True)
        ds = (t - p * delta).astype(jnp.bfloat16)
        give(me_ref, grad_ref, 0, i, half, jnp.dot(ds, k, preferred_element_type=f32) * scale)
        dk = lax.dot_general(ds, q, CONTRACT_FIRST, preferred_element_type=f32)
        dv = lax.dot_general(
            p.astype(jnp.bfloat16), do, CONTRACT_FIRST, preferred_element_type=f32
        )
        if i > 0:
            give(me_ref, grad_ref, 1, i - 1, half, (dk_acc[...] + dk[:512]) * scale)
            give(me_ref, grad_ref, 2, i - 1, half, dv_acc[...] + dv[:512])
        if i == blocks - 1:
            give(me_ref, grad_ref, 1, i, half, dk[-512:] * scale)
            give(me_ref, grad_ref, 2, i, half, dv[-512:])
        else:
            dk_acc[...] = dk[-512:]
            dv_acc[...] = dv[-512:]


def attend_fwd(me, segc, segr, parts):
    blocks = segc.shape[0]
    units, _, narrow, rows, width = parts.shape
    scale2 = math.log2(math.e) / math.sqrt(width)
    return pl.pallas_call(
        functools.partial(fwd_kernel, blocks=blocks, scale2=scale2),
        out_shape=(
            jax.ShapeDtypeStruct((units, 1, narrow, rows, width), jnp.bfloat16),
            jax.ShapeDtypeStruct((blocks, 512, 1), jnp.float32),
        ),
        in_specs=[SMEM_SPEC] + vmem_specs(3),
        out_specs=tuple(vmem_specs(2)),
        compiler_params=BIG,
        name="attend_fwd",
    )(me, segc, segr, parts)


def attend_bwd(me, segc, segr, lse, parts, dout):
    blocks = segc.shape[0]
    width = parts.shape[-1]
    scale = 1.0 / math.sqrt(width)
    return pl.pallas_call(
        functools.partial(
            bwd_kernel, blocks=blocks, scale=scale, scale2=scale * math.log2(math.e)
        ),
        out_shape=jax.ShapeDtypeStruct(parts.shape, jnp.bfloat16),
        in_specs=[SMEM_SPEC] + vmem_specs(5),
        out_specs=vmem_specs(1)[0],
        scratch_shapes=[pltpu.VMEM((512, width), jnp.float32)] * 2,
        compiler_params=BIG,
        name="attend_bwd",
    )(me, segc, segr, lse, parts, dout)


def ff_kernel(rows_ref, *refs):
    weights, (bias_ref, right_ref, hidden_ref, slope_ref, outer_ref) = refs[:-5], refs[-5:]
    step = 256
    depth = rows_ref.shape[1] // len(weights)
    for r in range(0, rows_ref.shape[0], step):
        x = bias_ref[...]
        for n, weight_ref in enumerate(weights):
            x = x + jnp.dot(
                rows_ref[r : r + step, n * depth : (n + 1) * depth],
                weight_ref[...].reshape(depth, -1),
                preferred_element_type=jnp.float32,
            )
        below = 0.5 * (1.0 + lax.erf(x * math.sqrt(0.5)))
        hidden_ref[r : r + step] = (x * below).astype(jnp.bfloat16)
        slope_ref[r : r + step] = below + x * (
            jnp.exp(-0.5 * x * x) * (1.0 / math.sqrt(2.0 * math.pi))
        )
    outer_ref[...] = lax.dot_general(
        hidden_ref[...], right_ref[...], CONTRACT_FIRST, preferred_element_type=jnp.float32
    ).astype(jnp.bfloat16)


def feed_forward(rows, weight, bias, right):
    count, width = right.shape
    deep, narrow, shard, inner = weight.shape
    step = 256
    return pl.pallas_call(
        ff_kernel,
        grid=(inner // step,),
        out_shape=(
            jax.ShapeDtypeStruct((count, inner), jnp.bfloat16),
            jax.ShapeDtypeStruct((count, inner), jnp.float32),
            jax.ShapeDtypeStruct((inner, width), jnp.bfloat16),
        ),
        in_specs=[resident(rows.shape)]
        + [
            pl.BlockSpec((deep, 1, shard, step), lambda i, n=n: (0, n, 0, i)) for n in range(narrow)
        ]
        + [pl.BlockSpec((1, step), lambda i: (0, i)), resident(right.shape)],
        out_specs=(
            pl.BlockSpec((count, step), lambda i: (0, i)),
            pl.BlockSpec((count, step), lambda i: (0, i)),
            pl.BlockSpec((step, width), lambda i: (i, 0)),
        ),
        compiler_params=BIG,
        name="feed_forward",
    )(rows, *[weight] * narrow, bias.reshape(1, -1), right)


def pull_kernel(rows_ref, weight_ref, slope_ref, grad_ref, sum_ref):
    step = 256
    total = jnp.zeros((1, weight_ref.shape[0]), jnp.float32)
    for r in range(0, rows_ref.shape[0], step):
        pull = lax.dot_general(
            rows_ref[r : r + step],
            weight_ref[...],
            CONTRACT_LAST,
            preferred_element_type=jnp.float32,
        )
        grad = (pull * slope_ref[r : r + step]).astype(jnp.bfloat16)
        grad_ref[r : r + step] = grad
        total = total + jnp.sum(grad.astype(jnp.float32), axis=0, keepdims=True)
    sum_ref[...] = total


def pull_back(rows, weight, slope):
    count, inner = slope.shape
    width = weight.shape[1]
    step = 256
    return pl.pallas_call(
        pull_kernel,
        grid=(inner // step,),
        out_shape=(
            jax.ShapeDtypeStruct((count, inner), jnp.bfloat16),
            jax.ShapeDtypeStruct((1, inner), jnp.float32),
        ),
        in_specs=[
            resident(rows.shape),
            pl.BlockSpec((step, width), lambda i: (i, 0)),
            pl.BlockSpec((count, step), lambda i: (0, i)),
        ],
        out_specs=(
            pl.BlockSpec((count, step), lambda i: (0, i)),
            pl.BlockSpec((1, step), lambda i: (0, i)),
        ),
        compiler_params=BIG,
        name="pull_back",
    )(rows, weight, slope)


def place_qkv_kernel(me_ref, *refs):
    pieces, outs = refs[:4], refs[4:]
    cols = pieces[0].shape[1] // len(outs)
    for part, out_ref in enumerate(outs):
        blocks = [piece[:, part * cols : (part + 1) * cols].astype(jnp.float32) for piece in pieces]
        for n in range(4):
            value = blocks[n]
            for me in range(1, 4):
                value = jnp.where(me_ref[0] == me, blocks[n ^ me], value)
            out_ref[:, n * cols : (n + 1) * cols] = value


def place_qkv(me, pieces):
    rows, width = pieces[0].shape
    shape = jax.ShapeDtypeStruct((rows, width // 3 * 4), jnp.float32)
    return pl.pallas_call(
        place_qkv_kernel,
        out_shape=(shape,) * 3,
        in_specs=[SMEM_SPEC] + vmem_specs(4),
        out_specs=tuple(vmem_specs(3)),
        compiler_params=BIG,
        name="place_qkv",
    )(me, *pieces)


def place_up_kernel(me_ref, own_ref, other_ref, out_ref, *, step):
    narrow, _, inner = own_ref.shape
    high = (me_ref[1] & 1) > 0
    for n in range(narrow):
        own, other = own_ref[n ^ me_ref[0]], other_ref[n ^ me_ref[0]]
        for z in range(inner // step):
            c = (n * (inner // step) + z) * 2 * step
            a = own[:, z * step : (z + 1) * step].astype(jnp.float32)
            b = other[:, z * step : (z + 1) * step].astype(jnp.float32)
            out_ref[:, c : c + step] = jnp.where(high, b, a)
            out_ref[:, c + step : c + 2 * step] = jnp.where(high, a, b)


def place_up(me, own, other, step):
    narrow, shard, inner = own.shape
    return pl.pallas_call(
        functools.partial(place_up_kernel, step=step),
        out_shape=jax.ShapeDtypeStruct((shard, 2 * narrow * inner), jnp.float32),
        in_specs=[SMEM_SPEC] + vmem_specs(2),
        out_specs=vmem_specs(1)[0],
        compiler_params=BIG,
        name="place_up",
    )(me, own, other)


def pick_kernel(me_ref, weight_ref, out_ref):
    _, narrow, shard, inner = out_ref.shape
    high = (me_ref[1] & 1) > 0
    step = 256
    for n in range(narrow):
        for z in range(inner // step):
            c = (n * (inner // step) + z) * 2 * step
            low_part = weight_ref[:, c : c + step]
            high_part = weight_ref[:, c + step : c + 2 * step]
            cols = slice(z * step, (z + 1) * step)
            out_ref[0, n, :, cols] = jnp.where(high, high_part, low_part)
            out_ref[1, n, :, cols] = jnp.where(high, low_part, high_part)


def pick(me, weight, narrow):
    shard, total = weight.shape
    return pl.pallas_call(
        pick_kernel,
        out_shape=jax.ShapeDtypeStruct((2, narrow, shard, total // (2 * narrow)), weight.dtype),
        in_specs=[SMEM_SPEC] + vmem_specs(1),
        out_specs=vmem_specs(1)[0],
        compiler_params=BIG,
        name="pick",
    )(me, weight)


def on_device(
    block_input,
    segment_ids,
    cotangent,
    attn_gain,
    attn_shift,
    query_weight,
    query_bias,
    key_weight,
    value_weight,
    value_bias,
    out_weight,
    out_bias,
    mlp_gain,
    mlp_shift,
    up_weight,
    up_bias,
    down_weight,
    down_bias,
):
    f32 = jnp.float32
    bf16 = jnp.bfloat16
    batch, tokens, width = block_input.shape
    narrow = lax.axis_size(NARROW)
    wide = lax.axis_size(WIDE)
    me_n = lax.axis_index(NARROW)
    me_w = lax.axis_index(WIDE)
    me = jnp.stack([me_n, me_w]).astype(jnp.int32)
    rows = batch * tokens
    heads = HEADS // narrow
    head_dim = width // HEADS
    cols = heads * head_dim
    shard = width // (narrow * wide)
    deep = wide // 2
    ff_shard = up_bias.shape[0]
    ff_local = ff_shard * deep
    me_y = me_w & 1

    def qkv_block(n):
        return jnp.concatenate(
            [
                lax.dynamic_slice_in_dim(weight, n * cols, cols, 1)
                for weight in (query_weight, key_weight, value_weight)
            ],
            axis=1,
        )

    out_w = wide_gather(out_weight, 0)
    qkv_shard = narrow_swap(qkv_block)
    attn_parts = ring_gather(qkv_shard, 1)

    smalls = [
        attn_gain, attn_shift, out_bias, mlp_gain, mlp_shift, down_bias, query_bias, value_bias, up_bias
    ]
    ids = segment_ids.astype(bf16).reshape(-1)
    small = cube_gather(jnp.concatenate(smalls + [ids])[None])

    def full_vector(k):
        return small[:, k * shard : (k + 1) * shard].reshape(-1).astype(f32)

    gain_attn, shift_attn, obias, gain_mlp, shift_mlp, dbias = [full_vector(k) for k in range(6)]
    mine = lax.dynamic_slice_in_dim(small, me_n * wide, wide, 0)
    qbias = mine[:, 6 * shard : 7 * shard].reshape(-1).astype(f32)
    vbias = mine[:, 7 * shard : 8 * shard].reshape(-1).astype(f32)
    ubias = mine[:, 8 * shard : 8 * shard + ff_shard].reshape(deep, 2, ff_shard)
    ubias = at(ubias, me_y, 1).reshape(-1).astype(f32)
    qkv_bias = jnp.concatenate([qbias, jnp.zeros_like(qbias), vbias])

    inputs = block_input.astype(f32).reshape(rows, width)
    first_norm = narrow_gather(normalize(inputs, gain_attn, shift_attn).astype(bf16))
    cotan_own = cotangent.reshape(rows, width)
    attn_parts = hold(attn_parts, out_w)
    sent = project_parts(first_norm, attn_parts, qkv_bias, wide, 3, heads, tokens)
    qkv = wide_swap(sent)

    picked = pick(me, hold(up_weight, first_norm[3]), narrow)
    high = me_y > 0
    here, there = picked[0], flip(hold(picked[1], sent), WIDE, 1)
    up_pair = jnp.stack([jnp.where(high, there, here), jnp.where(high, here, there)], axis=1)
    up_shard = narrow_swap(lambda n: at(up_pair, n)).reshape(narrow, 2 * shard, ff_local)
    ids = hold(small, sent)[:, -batch * tokens :].reshape(narrow * wide, batch, tokens)
    unit_ids = at(ids, me_w // heads, 1).reshape(-1).astype(jnp.int32)
    segc = unit_ids.reshape(-1, 512, 1)
    segr = unit_ids.reshape(1, -1)
    qkv = hold(qkv, up_shard)
    unit_out, lse = attend_fwd(me, segc, segr, qkv)
    up_parts = z_gather(hold(up_shard, unit_out)[None], 0)
    unit_back = wide_swap(unit_out)
    near = spread_near(hold(cotan_own, unit_out))
    unit_back = hold(unit_back, *near)
    cotan = jnp.concatenate(near + [flip(hold(part, unit_back), NARROW, 1) for part in near], axis=0)
    partial, mixed = unproject(unit_back, out_w, heads)
    middle = inputs + narrow_scatter(partial) + obias
    down_late, middle = lax.optimization_barrier((down_weight, middle, up_parts, cotan))[:2]
    down_w = z_gather(down_late, 0)

    second_norm = spread(normalize(middle, gain_mlp, shift_mlp).astype(bf16))
    second_norm = jnp.concatenate(second_norm, axis=0)
    hidden, slope, down_grad = feed_forward(second_norm, up_parts, ubias, cotan)
    down_grad = z_scatter(down_grad, 0)
    inner_grad, ubias_grad = pull_back(cotan, down_w, slope)
    split = inner_grad.shape[0] // 2
    far = times_parts(inner_grad, 1, split, up_parts)
    near = times_parts(hold(inner_grad, far), 0, split, up_parts)
    up_made = []

    def make_up_grad(event):
        up_made.append(outer_sum(second_norm, hold(inner_grad, event)).astype(bf16))
        return up_made[0]

    second_grad = fold_last(*fold_first(far, near), make_up_grad)
    mlp_pull = jax.vjp(normalize, middle, gain_mlp, shift_mlp)[1]
    middle_part, mgain_grad, mshift_grad = mlp_pull(second_grad)
    middle_grad = cotan_own.astype(f32) + middle_part
    branch_own = middle_grad.astype(bf16)
    dbias_grad = jnp.sum(cotan_own.astype(f32), axis=0)

    obias_grad = jnp.sum(branch_own.astype(f32), axis=0)
    out_made = []

    def make_outputs(beside):
        late = hold(hidden, beside)
        out_made.append(matmul(late[split:], down_w).astype(bf16))
        out_made.append(matmul(late[:split], down_w).astype(bf16))
        return out_made

    branch = narrow_gather(branch_own, make_outputs)
    up_grad = hold(up_made[0], out_made[1], down_grad)
    up_grad = z_scatter(up_grad.reshape(narrow, 2 * deep * shard, ff_local), 1)
    no_bias = jnp.zeros((cols,), f32)
    sent = project(branch, out_w, no_bias, wide, 1, heads, tokens, True)
    out_grad = outer_sum(hold(mixed, sent), jnp.concatenate(branch, axis=0)).astype(bf16)
    own, over_x, over_y = fold_first(*hold_all(out_made, sent))
    dout, over_x, over_y = hold_all((wide_swap(sent), over_x, over_y), out_grad)
    output = middle + fold_last(own, over_x, over_y) + dbias
    block_output = output.astype(bf16).reshape(batch, tokens, width)
    unit_grads = attend_bwd(me, segc, segr, lse, qkv, dout)
    unit_grads = hold(unit_grads, block_output)
    grads = wide_swap(unit_grads)
    up_rows = hold(up_grad, unit_grads).reshape(narrow, 2, shard, ff_local)
    up_sent = up_rows
    up_rows = narrow_blocks(lambda n: at(up_sent, n))
    up_own = jnp.stack([at(block, me_y) for block in up_rows])
    up_other = flip(jnp.stack([at(block, 1 - me_y) for block in up_rows]), WIDE, 1)
    up_back = place_up(me, up_own, up_other, ff_shard)
    down_grad = down_grad.astype(f32)
    grads = hold(grads, up_back)
    order = (1, 3, 0, 2)
    sums, back = wide_outer(
        [first_norm[j] for j in order], grads, out_grad, wide, heads, order
    )
    made = {}

    def beside(stage, event):
        if stage == 0:
            far = times_parts(hold(back, event), 0, 2 * rows, attn_parts)
            made["far"] = far.reshape(2, rows, width)
            return (far,)
        if stage == 1:
            far = made["far"]
            near = times_parts(hold(back, event), 1, 2 * rows, attn_parts)
            near = near.reshape(2, rows, width)
            made["first"] = narrow_scatter([near[0], far[0], near[1], far[1]])
            return (near,)
        if stage == 2:
            attn_pull = jax.vjp(normalize, inputs, gain_attn, shift_attn)[1]
            input_part, again_grad, ashift_grad = attn_pull(made["first"])
            made["pulled"] = middle_grad + input_part, again_grad, ashift_grad
            return made["pulled"] + (down_grad,)
        return ()

    qkv_rows = jnp.concatenate(ring_scatter(sums, beside, 1), axis=-1)
    out_grad = qkv_rows[..., 3 * cols :].transpose(1, 0, 2).reshape(shard, width)
    qkv_rows = qkv_rows[..., : 3 * cols]
    swapped = narrow_blocks(lambda n: at(qkv_rows, n))
    qkv_grad = place_qkv(me, swapped)
    back_sums = jnp.sum(back.astype(f32), axis=0)
    input_grad, again_grad, ashift_grad = made["pulled"]
    input_grad = input_grad.reshape(batch, tokens, width)

    fulls = [again_grad, ashift_grad, obias_grad, mgain_grad, mshift_grad, dbias_grad]
    fulls = jnp.concatenate([v.reshape(narrow * wide, shard) for v in fulls], axis=1)
    ubias_rows = jnp.zeros((deep, 2, ff_shard), f32)
    ubias_rows = lax.dynamic_update_slice_in_dim(
        ubias_rows,
        ubias_grad.reshape(deep, 1, ff_shard),
        me_y,
        1,
    )
    slices = [back_sums[:cols], back_sums[2 * cols :], ubias_rows]
    slices = jnp.concatenate([v.reshape(wide, -1) for v in slices], axis=1)
    placed = jnp.zeros((narrow * wide, slices.shape[1]), f32)
    placed = lax.dynamic_update_slice_in_dim(placed, slices, me_n * wide, 0)
    vectors = cube_scatter(jnp.concatenate([fulls, placed], axis=1), swapped[1])

    def vector(k):
        return vectors[k * shard : (k + 1) * shard]

    return (
        block_output,
        input_grad,
        vector(0),
        vector(1),
        qkv_grad[0],
        vector(6),
        qkv_grad[1],
        qkv_grad[2],
        vector(7),
        out_grad.astype(f32),
        vector(2),
        vector(3),
        vector(4),
        up_back,
        vectors[8 * shard :],
        down_grad,
        vector(5),
    )


def body_of(mesh):
    def body(*args):
        batch, tokens, width = args[0].shape
        narrow, wide = mesh.shape[NARROW], mesh.shape[WIDE]
        one_unit = batch * (HEADS // narrow) == wide and tokens == 128 and narrow == 4
        return (on_device if one_unit else on_device_ring)(*args)

    return body


def solution(mesh):
    return jax.shard_map(
        body_of(mesh),
        mesh=mesh,
        in_specs=(
            P(None, BOTH, None),
            P(None, BOTH),
            P(None, BOTH, None),
            P(BOTH),
            P(BOTH),
            P(BOTH, None),
            P(BOTH),
            P(BOTH, None),
            P(BOTH, None),
            P(BOTH),
            P(BOTH, None),
            P(BOTH),
            P(BOTH),
            P(BOTH),
            P(BOTH, None),
            P(BOTH),
            P(BOTH, None),
            P(BOTH),
        ),
        out_specs=(
            P(None, BOTH, None),
            P(None, BOTH, None),
            P(BOTH),
            P(BOTH),
            P(BOTH, None),
            P(BOTH),
            P(BOTH, None),
            P(BOTH, None),
            P(BOTH),
            P(BOTH, None),
            P(BOTH),
            P(BOTH),
            P(BOTH),
            P(BOTH, None),
            P(BOTH),
            P(BOTH, None),
            P(BOTH),
        ),
        check_vma=False,
    )
```

```python
import functools
import math
import jax
import jax.numpy as jnp
from jax import lax
from jax.experimental import pallas as pl
from jax.experimental.pallas import tpu as pltpu
from jax.sharding import PartitionSpec as P
HEADS = 16
NARROW, WIDE = "narrow", "wide"
BOTH = (NARROW, WIDE)
REACH = 4
eps = 1e-05
neg_big = -1e30


def shifted(value, axis, by):
    devices = lax.axis_size(axis)
    return lax.ppermute(value, axis, [(i, (i + by) % devices) for i in range(devices)])


def as_sent(value):

    def short(part):
        return part.astype(jnp.bfloat16) if part.dtype == jnp.float32 else part

    return jax.tree.map(short, value)


def normalize(values, gain, shift):
    center = jnp.mean(values, axis=-1, keepdims=True)
    centered = values - center
    spread = jnp.mean(centered * centered, axis=-1, keepdims=True)
    return centered * lax.rsqrt(spread + eps) * gain + shift


def gelu_exact(values):
    return jax.nn.gelu(values, approximate=False)


def matmul(left, right):
    return jnp.dot(left, right, preferred_element_type=jnp.float32)


def outer_sum(left, right):
    return lax.dot_general(
        left, right, (((0,), (0,)), ((), ())), preferred_element_type=jnp.float32
    )


def times_transpose(left, right):
    return lax.dot_general(
        left, right, (((1,), (1,)), ((), ())), preferred_element_type=jnp.float32
    )


def key_positions(first_row, row_count, tokens, narrow_size, wide_size):
    row_ids = first_row + jnp.arange(row_count, dtype=jnp.int32)
    source_wide = row_ids // (tokens * narrow_size)
    source_narrow = row_ids // tokens % narrow_size
    return (source_narrow * wide_size + source_wide) * tokens + row_ids % tokens


def block_mask(query_segs, query_pos, key_segs, key_pos):
    same_doc = query_segs[:, :, None] == key_segs[:, None, :]
    causal = key_pos[None, None, :] <= query_pos[None, :, None]
    return jnp.logical_and(same_doc, causal)


def raw_scores(query_rows, key_rows, score_scale, allowed):
    scores = (
        jnp.einsum("bqhd,bkhd->bhqk", query_rows, key_rows, preferred_element_type=jnp.float32)
        * score_scale
    )
    return jnp.where(allowed[:, None], scores, neg_big)


def forward_block(running, query_heads, key_block, value_block, allowed, score_scale):
    row_max, row_total, weighted = running
    scores = raw_scores(query_heads, key_block, score_scale, allowed)
    new_max = jnp.maximum(row_max, jnp.max(scores, axis=-1))
    rescale = jnp.exp(row_max - new_max)
    exp_terms = jnp.where(allowed[:, None], jnp.exp(scores - new_max[..., None]), 0.0)
    row_total = row_total * rescale + jnp.sum(exp_terms, axis=-1)
    added = jnp.einsum(
        "bhqk,bkhd->bqhd",
        exp_terms.astype(jnp.bfloat16),
        value_block,
        preferred_element_type=jnp.float32,
    )
    weighted = weighted * jnp.transpose(rescale, (0, 2, 1))[..., None] + added
    return (new_max, row_total, weighted)


def backward_block(
    query_grad,
    query_heads,
    dout_heads,
    key_block,
    value_block,
    allowed,
    delta,
    log_total,
    score_scale,
):
    scores = raw_scores(query_heads, key_block, score_scale, allowed)
    attn_probs = jnp.where(allowed[:, None], jnp.exp(scores - log_total[..., None]), 0.0)
    prob_grad = jnp.einsum(
        "bqhd,bkhd->bhqk", dout_heads, value_block, preferred_element_type=jnp.float32
    )
    score_grad = (attn_probs * (prob_grad - delta[..., None])).astype(jnp.bfloat16)
    query_grad = query_grad + score_scale * jnp.einsum(
        "bhqk,bkhd->bqhd", score_grad, key_block, preferred_element_type=jnp.float32
    )
    key_grad = score_scale * jnp.einsum(
        "bhqk,bqhd->bkhd", score_grad, query_heads, preferred_element_type=jnp.float32
    )
    value_grad = jnp.einsum(
        "bhqk,bqhd->bkhd",
        attn_probs.astype(jnp.bfloat16),
        dout_heads,
        preferred_element_type=jnp.float32,
    )
    return (query_grad, key_grad, value_grad)


def on_device_ring(
    block_input,
    segment_ids,
    cotangent,
    attn_gain,
    attn_shift,
    query_weight,
    query_bias,
    key_weight,
    value_weight,
    value_bias,
    out_weight,
    out_bias,
    mlp_gain,
    mlp_shift,
    up_weight,
    up_bias,
    down_weight,
    down_bias,
):
    batch, tokens, model_width = block_input.shape
    narrow_size = lax.axis_size(NARROW)
    wide_size = lax.axis_size(WIDE)
    wide_index = lax.axis_index(WIDE)
    group_rows = tokens * narrow_size
    heads_local = HEADS // narrow_size
    head_dim = model_width // HEADS
    score_scale = 1.0 / math.sqrt(head_dim)
    f32 = jnp.float32
    bf16 = jnp.bfloat16
    attn_set = (
        lax.all_gather(attn_gain, BOTH, axis=0, tiled=True),
        lax.all_gather(attn_shift, BOTH, axis=0, tiled=True),
        lax.all_gather(query_weight, BOTH, axis=0, tiled=True),
        lax.all_gather(query_bias, BOTH, axis=0, tiled=True),
        lax.all_gather(key_weight, BOTH, axis=0, tiled=True),
        lax.all_gather(value_weight, BOTH, axis=0, tiled=True),
        lax.all_gather(value_bias, BOTH, axis=0, tiled=True),
        lax.all_gather(out_weight, BOTH, axis=0, tiled=True),
        lax.all_gather(out_bias, BOTH, axis=0, tiled=True),
    )
    (
        gain_attn,
        shift_attn,
        query_full,
        qbias_full,
        key_full,
        value_full,
        vbias_full,
        out_full,
        obias_full,
    ) = attn_set
    inputs = block_input.astype(f32).reshape(-1, model_width)
    first_norm = normalize(inputs, gain_attn.astype(f32), shift_attn.astype(f32)).astype(bf16)
    split_shape = (batch, tokens, HEADS, head_dim)
    queries = (
        (matmul(first_norm, query_full) + qbias_full.astype(f32)).astype(bf16).reshape(split_shape)
    )
    key_rows = matmul(first_norm, key_full).astype(bf16).reshape(split_shape)
    value_rows = (
        (matmul(first_norm, value_full) + vbias_full.astype(f32)).astype(bf16).reshape(split_shape)
    )
    query_heads, key_heads, value_heads = (
        lax.all_to_all(queries, NARROW, split_axis=2, concat_axis=1, tiled=True),
        lax.all_to_all(key_rows, NARROW, split_axis=2, concat_axis=1, tiled=True),
        lax.all_to_all(value_rows, NARROW, split_axis=2, concat_axis=1, tiled=True),
    )
    query_segs = lax.all_gather(segment_ids, NARROW, axis=1, tiled=True)
    query_pos = key_positions(wide_index * group_rows, group_rows, tokens, narrow_size, wide_size)

    def block_allowed(cycle_step, seg_block):
        source = (wide_index - cycle_step) % wide_size
        key_pos = key_positions(source * group_rows, group_rows, tokens, narrow_size, wide_size)
        return block_mask(query_segs, query_pos, seg_block, key_pos)

    running = (
        jnp.full((batch, heads_local, group_rows), neg_big, f32),
        jnp.zeros((batch, heads_local, group_rows), f32),
        jnp.zeros((batch, group_rows, heads_local, head_dim), f32),
    )
    travelling = (key_heads, value_heads, query_segs)
    received = []
    for cycle_step in range(REACH + 1):
        if cycle_step > 0:
            travelling = shifted((travelling[0], travelling[1], travelling[2]), WIDE, 1)
        received.append(travelling)
        key_block, value_block, seg_block = travelling
        allowed = block_allowed(cycle_step, seg_block)
        running = forward_block(running, query_heads, key_block, value_block, allowed, score_scale)
    row_max, row_total, weighted = running
    attn_out = weighted / jnp.transpose(row_total, (0, 2, 1))[..., None]
    log_total = row_max + jnp.log(row_total)
    mixed = lax.all_to_all(
        attn_out.astype(bf16), NARROW, split_axis=1, concat_axis=2, tiled=True
    ).reshape(-1, model_width)
    middle = inputs + matmul(mixed, out_full) + obias_full.astype(f32)
    mlp_set = (
        lax.all_gather(mlp_gain, BOTH, axis=0, tiled=True),
        lax.all_gather(mlp_shift, BOTH, axis=0, tiled=True),
        lax.all_gather(up_weight, BOTH, axis=0, tiled=True),
        lax.all_gather(up_bias, BOTH, axis=0, tiled=True),
        lax.all_gather(down_weight, BOTH, axis=0, tiled=True),
        lax.all_gather(down_bias, BOTH, axis=0, tiled=True),
    )
    gain_mlp, shift_mlp, up_full, ubias_full, down_full, dbias_full = mlp_set
    second_norm = normalize(middle, gain_mlp.astype(f32), shift_mlp.astype(f32)).astype(bf16)
    inner = matmul(second_norm, up_full) + ubias_full.astype(f32)
    hidden = gelu_exact(inner).astype(bf16)
    output = middle + matmul(hidden, down_full) + dbias_full.astype(f32)
    block_output = output.astype(bf16).reshape(batch, tokens, model_width)
    mlp_set = (
        lax.all_gather(mlp_gain, BOTH, axis=0, tiled=True),
        lax.all_gather(mlp_shift, BOTH, axis=0, tiled=True),
        lax.all_gather(up_weight, BOTH, axis=0, tiled=True),
        lax.all_gather(up_bias, BOTH, axis=0, tiled=True),
        lax.all_gather(down_weight, BOTH, axis=0, tiled=True),
        lax.all_gather(down_bias, BOTH, axis=0, tiled=True),
    )
    gain_mlp, shift_mlp, up_full, ubias_full, down_full, dbias_full = mlp_set
    cotan_rows = cotangent.reshape(-1, model_width)
    down_grad = outer_sum(hidden, cotan_rows)
    dbias_grad = jnp.sum(cotan_rows.astype(f32), axis=0)
    hidden_grad = times_transpose(cotan_rows, down_full)
    gelu_pull = jax.vjp(gelu_exact, inner)[1]
    inner_grad = gelu_pull(hidden_grad)[0].astype(bf16)
    up_grad = outer_sum(second_norm, inner_grad)
    ubias_grad = jnp.sum(inner_grad.astype(f32), axis=0)
    second_grad = times_transpose(inner_grad, up_full)
    mlp_pull = jax.vjp(normalize, middle, gain_mlp.astype(f32), shift_mlp.astype(f32))[1]
    middle_part, mgain_grad, mshift_grad = mlp_pull(second_grad)
    middle_grad = cotan_rows.astype(f32) + middle_part
    mlp_shards = (
        lax.psum_scatter(mgain_grad, BOTH, scatter_dimension=0, tiled=True),
        lax.psum_scatter(mshift_grad, BOTH, scatter_dimension=0, tiled=True),
        lax.psum_scatter(up_grad, BOTH, scatter_dimension=0, tiled=True),
        lax.psum_scatter(ubias_grad, BOTH, scatter_dimension=0, tiled=True),
        lax.psum_scatter(down_grad, BOTH, scatter_dimension=0, tiled=True),
        lax.psum_scatter(dbias_grad, BOTH, scatter_dimension=0, tiled=True),
    )
    attn_set = (
        lax.all_gather(attn_gain, BOTH, axis=0, tiled=True),
        lax.all_gather(attn_shift, BOTH, axis=0, tiled=True),
        lax.all_gather(query_weight, BOTH, axis=0, tiled=True),
        lax.all_gather(query_bias, BOTH, axis=0, tiled=True),
        lax.all_gather(key_weight, BOTH, axis=0, tiled=True),
        lax.all_gather(value_weight, BOTH, axis=0, tiled=True),
        lax.all_gather(value_bias, BOTH, axis=0, tiled=True),
        lax.all_gather(out_weight, BOTH, axis=0, tiled=True),
        lax.all_gather(out_bias, BOTH, axis=0, tiled=True),
    )
    (
        gain_attn,
        shift_attn,
        query_full,
        qbias_full,
        key_full,
        value_full,
        vbias_full,
        out_full,
        obias_full,
    ) = attn_set
    branch_grad = middle_grad.astype(bf16)
    out_grad = outer_sum(mixed, branch_grad)
    obias_grad = jnp.sum(branch_grad.astype(f32), axis=0)
    mixed_grad = times_transpose(branch_grad, out_full).astype(bf16).reshape(split_shape)
    dout_heads = lax.all_to_all(mixed_grad, NARROW, split_axis=2, concat_axis=1, tiled=True)
    delta = jnp.transpose(jnp.sum(dout_heads.astype(f32) * attn_out, axis=-1), (0, 2, 1))
    travelling = (key_heads, value_heads, query_segs)
    received = []
    for cycle_step in range(REACH + 1):
        if cycle_step > 0:
            travelling = shifted((travelling[0], travelling[1], travelling[2]), WIDE, 1)
        received.append(travelling)
    query_grad = jnp.zeros((batch, group_rows, heads_local, head_dim), f32)
    key_terms = []
    value_terms = []
    for cycle_step in range(REACH + 1):
        key_block, value_block, seg_block = received[cycle_step]
        allowed = block_allowed(cycle_step, seg_block)
        query_grad, key_term, value_term = backward_block(
            query_grad,
            query_heads,
            dout_heads,
            key_block,
            value_block,
            allowed,
            delta,
            log_total,
            score_scale,
        )
        key_terms.append(key_term)
        value_terms.append(value_term)
    carried = (key_terms[REACH], value_terms[REACH])
    for cycle_step in range(REACH - 1, -1, -1):
        arrived = shifted((as_sent(carried[0]), as_sent(carried[1])), WIDE, -1)
        carried = (arrived[0] + key_terms[cycle_step], arrived[1] + value_terms[cycle_step])
    key_sum, value_sum = carried
    query_back, key_back, value_back = (
        lax.all_to_all(query_grad.astype(bf16), NARROW, split_axis=1, concat_axis=2, tiled=True),
        lax.all_to_all(key_sum.astype(bf16), NARROW, split_axis=1, concat_axis=2, tiled=True),
        lax.all_to_all(value_sum.astype(bf16), NARROW, split_axis=1, concat_axis=2, tiled=True),
    )
    query_back = query_back.reshape(-1, model_width)
    key_back = key_back.reshape(-1, model_width)
    value_back = value_back.reshape(-1, model_width)
    query_wgrad = outer_sum(first_norm, query_back)
    qbias_grad = jnp.sum(query_back.astype(f32), axis=0)
    key_wgrad = outer_sum(first_norm, key_back)
    value_wgrad = outer_sum(first_norm, value_back)
    vbias_grad = jnp.sum(value_back.astype(f32), axis=0)
    first_grad = (
        times_transpose(query_back, query_full)
        + times_transpose(key_back, key_full)
        + times_transpose(value_back, value_full)
    )
    attn_pull = jax.vjp(normalize, inputs, gain_attn.astype(f32), shift_attn.astype(f32))[1]
    input_part, again_grad, ashift_grad = attn_pull(first_grad)
    input_grad = (middle_grad + input_part).reshape(batch, tokens, model_width)
    attn_shards = (
        lax.psum_scatter(again_grad, BOTH, scatter_dimension=0, tiled=True),
        lax.psum_scatter(ashift_grad, BOTH, scatter_dimension=0, tiled=True),
        lax.psum_scatter(query_wgrad, BOTH, scatter_dimension=0, tiled=True),
        lax.psum_scatter(qbias_grad, BOTH, scatter_dimension=0, tiled=True),
        lax.psum_scatter(key_wgrad, BOTH, scatter_dimension=0, tiled=True),
        lax.psum_scatter(value_wgrad, BOTH, scatter_dimension=0, tiled=True),
        lax.psum_scatter(vbias_grad, BOTH, scatter_dimension=0, tiled=True),
        lax.psum_scatter(out_grad, BOTH, scatter_dimension=0, tiled=True),
        lax.psum_scatter(obias_grad, BOTH, scatter_dimension=0, tiled=True),
    )
    return (
        block_output,
        input_grad,
        attn_shards[0],
        attn_shards[1],
        attn_shards[2],
        attn_shards[3],
        attn_shards[4],
        attn_shards[5],
        attn_shards[6],
        attn_shards[7],
        attn_shards[8],
        mlp_shards[0],
        mlp_shards[1],
        mlp_shards[2],
        mlp_shards[3],
        mlp_shards[4],
        mlp_shards[5],
    )


def flip(value, axis, bits):
    size = lax.axis_size(axis)
    return lax.ppermute(value, axis, [(i, i ^ bits) for i in range(size)])


def at(value, index, dim=0):
    return lax.dynamic_index_in_dim(value, index, dim, keepdims=False)


def cube(wide):
    steps = []
    bits = 1
    while bits < wide:
        steps.append((WIDE, bits))
        bits *= 2
    return steps + [(NARROW, 1), (NARROW, 2)]


def cube_gather(row):
    for axis, bits in cube(lax.axis_size(WIDE)):
        other = flip(row, axis, bits)
        high = (lax.axis_index(axis) & bits) > 0
        row = jnp.concatenate(
            [jnp.where(high, other, row), jnp.where(high, row, other)], axis=0
        )
    return row


def cube_scatter(table, event):
    wide = lax.axis_size(WIDE)
    steps = cube(wide)
    table = table.reshape((2,) * len(steps) + (table.shape[-1],))
    order = [len(steps) - 2, len(steps) - 1] + list(range(len(steps) - 2))[::-1]
    left = list(range(len(steps)))
    for k in order:
        axis, bits = steps[k]
        dim = len(left) - 1 - left.index(k)
        high = ((lax.axis_index(axis) & bits) > 0).astype(jnp.int32)
        table = at(table, high, dim) + flip(at(table, 1 - high, dim), axis, bits)
        left.remove(k)
        if len(left) == len(steps) - 2:
            table = hold(table, event)
    return table


def narrow_gather(own, made=None):
    across = flip(own, NARROW, 2)
    beside = flip(own, NARROW, 1)
    if made is not None:
        across = hold(across, *made(beside))
    return [own, beside, across, flip(across, NARROW, 1)]


def narrow_scatter(parts):
    f32 = jnp.float32
    far = flip(parts[3], NARROW, 1)
    near = flip(parts[1], NARROW, 1)
    passed = (parts[2].astype(f32) + far.astype(f32)).astype(jnp.bfloat16)
    across = flip(passed, NARROW, 2)
    return parts[0].astype(f32) + near.astype(f32) + across.astype(f32)


def hold(value, *events):
    return lax.optimization_barrier((value,) + events)[0]


def hold_all(values, *events):
    return lax.optimization_barrier(tuple(values) + events)[: len(values)]


def bit_of(axis, bits):
    return (lax.axis_index(axis) & bits) > 0


def in_order(relative):
    swap = bit_of(NARROW, 1)
    r = [
        jnp.where(swap, relative[k ^ 1], relative[k]) for k in range(4)
    ]
    swap = bit_of(NARROW, 2)
    return jnp.stack([jnp.where(swap, r[k ^ 2], r[k]) for k in range(4)])


def narrow_blocks(block_of):
    me = lax.axis_index(NARROW)
    return [flip(block_of(me ^ j), NARROW, j) if j else block_of(me) for j in range(4)]


def narrow_swap(block_of):
    return in_order(narrow_blocks(block_of))


def pair_swap(block_of):
    me = lax.axis_index(WIDE) & 1
    own, other = block_of(me), flip(block_of(1 - me), WIDE, 1)
    high = me > 0
    return jnp.stack([jnp.where(high, other, own), jnp.where(high, own, other)])


def spread_near(own):
    half = own.shape[1] // 2
    over_y = flip(own, WIDE, 1)
    over_x = flip(own, NARROW, 2)
    both = jnp.concatenate(
        [flip(over_y[:, :half], NARROW, 2), flip(over_x[:, half:], WIDE, 1)], axis=1
    )
    return [own, over_x, over_y, both]


def spread(own):
    near = spread_near(own)
    return near + [flip(part, NARROW, 1) for part in near]


def fold_first(far, near):
    f32, bf16 = jnp.float32, jnp.bfloat16
    width = far.shape[-1]
    half = width // 2
    far, near = far.reshape(4, -1, width), near.reshape(4, -1, width)
    far = flip(far, NARROW, 1)
    both = (near[3].astype(f32) + far[3].astype(f32)).astype(bf16)
    own, over_x, over_y = [near[k].astype(f32) + far[k].astype(f32) for k in range(3)]
    first = flip(both[:, :half], WIDE, 1).astype(f32)
    last = flip(both[:, half:], NARROW, 2).astype(f32)
    over_x = jnp.concatenate([over_x[:, :half] + first, over_x[:, half:]], axis=1).astype(bf16)
    over_y = jnp.concatenate([over_y[:, :half], over_y[:, half:] + last], axis=1).astype(bf16)
    return own, over_x, over_y


def fold_last(own, over_x, over_y, made=None):
    f32 = jnp.float32
    last = flip(over_x, NARROW, 2)
    if made is not None:
        last = hold(last, made(over_x))
    return own + last.astype(f32) + flip(over_y, WIDE, 1).astype(f32)


def columns(wide):
    return [list(range(y, wide, 2)) for y in range(2)]


def z_gather(shard, axis):
    groups = columns(lax.axis_size(WIDE))
    return lax.all_gather(shard, WIDE, axis=axis, tiled=True, axis_index_groups=groups)


def z_scatter(full, axis):
    groups = columns(lax.axis_size(WIDE))
    return lax.psum_scatter(
        full.astype(jnp.bfloat16), WIDE, scatter_dimension=axis, tiled=True, axis_index_groups=groups
    )


def ring_order(wide):
    return list(range(0, wide, 2)) + list(range(wide - 1, 0, -2))


def ring_at(position, wide):
    position = position % wide
    return jnp.where(position < wide // 2, 2 * position, 2 * (wide - 1 - position) + 1)


def ring_position(wide):
    me = lax.axis_index(WIDE)
    return jnp.where(me % 2 == 0, me // 2, wide - 1 - me // 2)


def ring_step(value, by):
    order = ring_order(lax.axis_size(WIDE))
    size = len(order)
    return lax.ppermute(
        value, WIDE, [(order[i], order[(i + by) % size]) for i in range(size)]
    )


def ring_gather(shard, chunks):
    wide = lax.axis_size(WIDE)
    here = ring_position(wide)
    full = jnp.zeros((wide,) + shard.shape, shard.dtype)
    zero = jnp.int32(0)

    def put(full, piece, position, column):
        where = (ring_at(position + wide, wide).astype(jnp.int32), zero, zero, jnp.int32(column))
        return lax.dynamic_update_slice(full, piece[None], where)

    full = put(full, shard, here, 0)
    step = shard.shape[-1] // chunks
    middle = step // 2
    ahead = [shard[..., c * step : (c + 1) * step] for c in range(chunks)]
    behind = list(ahead)
    for k in range(1, wide // 2):
        for c in range(chunks):
            ahead[c], behind[c] = ring_step(ahead[c], 1), ring_step(behind[c], -1)
        for c in range(chunks):
            full = put(full, ahead[c], here - k, c * step)
            full = put(full, behind[c], here + k, c * step)
    for c in range(chunks):
        left = ring_step(ahead[c][..., :middle], 1)
        right = ring_step(behind[c][..., middle:], -1)
        full = put(full, left, here + wide // 2, c * step)
        full = put(full, right, here + wide // 2, c * step + middle)
    return full


def ring_scatter(full, beside, chunks):
    wide = lax.axis_size(WIDE)
    here = ring_position(wide)
    bf16, f32 = jnp.bfloat16, jnp.float32
    step = full.shape[-1] // chunks
    middle = step // 2

    def local(position, c):
        return at(full, ring_at(position + wide, wide))[..., c * step : (c + 1) * step]

    sent = []
    for c in range(chunks):
        far = local(here + wide // 2, c)
        sent.append(lax.optimization_barrier((far[..., :middle], far[..., middle:])))
    event = sent[0][0]
    for stage, k in enumerate(range(wide // 2 - 1, -1, -1)):
        came = [
            (ring_step(sent[c][0], 1).astype(f32), ring_step(sent[c][1], -1).astype(f32))
            for c in range(chunks)
        ]
        values = beside(stage, event)
        if k == 0:
            break
        sent = []
        for c in range(chunks):
            ahead, behind = came[c]
            to_ahead, to_behind = local(here + k, c).astype(f32), local(here - k, c).astype(f32)
            if k == wide // 2 - 1:
                to_ahead = jnp.concatenate(
                    [to_ahead[..., :middle] + ahead, to_ahead[..., middle:]], axis=-1
                )
                to_behind = jnp.concatenate(
                    [to_behind[..., :middle], to_behind[..., middle:] + behind], axis=-1
                )
            else:
                to_ahead, to_behind = to_ahead + ahead, to_behind + behind
            terms = (to_ahead.astype(bf16), to_behind.astype(bf16)) + (values if c == 0 else ())
            sent.append(lax.optimization_barrier(terms)[:2])
        event = sent[0][0]
    return [
        (local(here, c).astype(f32) + came[c][0] + came[c][1]).astype(bf16) for c in range(chunks)
    ]


def wide_swap(parts):
    return lax.all_to_all(parts, WIDE, split_axis=0, concat_axis=0, tiled=True)


def wide_gather(shard, axis):
    return lax.all_gather(shard, WIDE, axis=axis, tiled=True)


def wide_scatter(full, axis):
    return lax.psum_scatter(full.astype(jnp.bfloat16), WIDE, scatter_dimension=axis, tiled=True)


def vmem_specs(count):
    return [pl.BlockSpec(memory_space=pltpu.VMEM)] * count


SMEM_SPEC = pl.BlockSpec(memory_space=pltpu.SMEM)
BIG = pltpu.CompilerParams(vmem_limit_bytes=48 << 20)
CONTRACT_LAST = (((1,), (1,)), ((), ()))
CONTRACT_FIRST = (((0,), (0,)), ((), ()))


def project_kernel(*refs, heads, by_last):
    rows, (weight_ref, bias_ref, out_ref) = refs[:-3], refs[-3:]
    units, parts, _, tokens, head_dim = out_ref.shape
    for j, rows_ref in enumerate(rows):

        @pl.when(pl.program_id(0) == j)
        def _():
            if by_last:
                acc = lax.dot_general(
                    rows_ref[...], weight_ref[...], CONTRACT_LAST, preferred_element_type=jnp.float32
                )
            else:
                acc = jnp.dot(rows_ref[...], weight_ref[...], preferred_element_type=jnp.float32)
            acc = (acc + bias_ref[...]).astype(jnp.bfloat16)
            for unit in range(units):
                b, h = divmod(unit, heads)
                for part in range(parts):
                    c = (part * heads + h) * head_dim
                    out_ref[unit, part, 0] = acc[
                        b * tokens : (b + 1) * tokens, c : c + head_dim
                    ]


def resident(shape):
    return pl.BlockSpec(shape, lambda i: (0,) * len(shape), pipeline_mode=pl.Buffered(1))


def project(rows, weight, bias, units, parts, heads, tokens, by_last):
    blocks = len(rows)
    head_dim = bias.shape[0] // (parts * heads)
    return pl.pallas_call(
        functools.partial(project_kernel, heads=heads, by_last=by_last),
        grid=(blocks,),
        out_shape=jax.ShapeDtypeStruct((units, parts, blocks, tokens, head_dim), jnp.bfloat16),
        in_specs=[resident(block.shape) for block in rows]
        + [resident(weight.shape), resident((1, bias.shape[0]))],
        out_specs=pl.BlockSpec(
            (units, parts, 1, tokens, head_dim), lambda i: (0, 0, i, 0, 0)
        ),
        compiler_params=BIG,
        name="project",
    )(*rows, weight, bias.reshape(1, -1))


def project_parts_kernel(*refs, heads, blocks):
    rows, weights, (bias_ref, out_ref) = refs[:blocks], refs[blocks:-2], refs[-2:]
    units, parts, _, tokens, head_dim = out_ref.shape
    depth = rows[0].shape[1] // len(weights)
    for j, rows_ref in enumerate(rows):

        @pl.when(pl.program_id(0) == j)
        def _():
            acc = bias_ref[...]
            for k, weight_ref in enumerate(weights):
                acc = acc + jnp.dot(
                    rows_ref[:, k * depth : (k + 1) * depth],
                    weight_ref[...].reshape(depth, -1),
                    preferred_element_type=jnp.float32,
                )
            acc = acc.astype(jnp.bfloat16)
            for unit in range(units):
                b, h = divmod(unit, heads)
                for part in range(parts):
                    c = (part * heads + h) * head_dim
                    out_ref[unit, part, 0] = acc[b * tokens : (b + 1) * tokens, c : c + head_dim]


def project_parts(rows, weight, bias, units, parts, heads, tokens):
    blocks, head_dim = len(rows), bias.shape[0] // (parts * heads)
    wide, narrow, shard, _ = weight.shape
    width = bias.shape[0]
    return pl.pallas_call(
        functools.partial(project_parts_kernel, heads=heads, blocks=blocks),
        grid=(blocks,),
        out_shape=jax.ShapeDtypeStruct((units, parts, blocks, tokens, head_dim), jnp.bfloat16),
        in_specs=[resident(block.shape) for block in rows]
        + [
            pl.BlockSpec(
                (wide, 1, shard, width), lambda i, k=k: (0, k, 0, 0), pipeline_mode=pl.Buffered(1)
            )
            for k in range(narrow)
        ]
        + [resident((1, bias.shape[0]))],
        out_specs=pl.BlockSpec((units, parts, 1, tokens, head_dim), lambda i: (0, 0, i, 0, 0)),
        compiler_params=BIG,
        name="project_parts",
    )(*rows, *[weight] * narrow, bias.reshape(1, -1))


def times_parts_kernel(rows_ref, weight_ref, out_ref):
    inner = rows_ref.shape[1]
    weight = weight_ref[...].reshape(out_ref.shape[1], -1)[:, :inner]
    acc = lax.dot_general(
        rows_ref[...], weight, CONTRACT_LAST, preferred_element_type=jnp.float32
    )
    out_ref[...] = acc.astype(jnp.bfloat16)


def times_parts(rows, block, count, weight):
    gathered, narrow, shard, _ = weight.shape
    inner = rows.shape[1]
    step = gathered * shard
    return pl.pallas_call(
        times_parts_kernel,
        grid=(narrow,),
        out_shape=jax.ShapeDtypeStruct((count, narrow * step), jnp.bfloat16),
        in_specs=[
            pl.BlockSpec((count, inner), lambda i: (block, 0), pipeline_mode=pl.Buffered(1)),
            pl.BlockSpec((gathered, 1, shard, inner), lambda i: (0, i, 0, 0)),
        ],
        out_specs=pl.BlockSpec((count, step), lambda i: (0, i)),
        compiler_params=BIG,
        name="times_parts",
    )(rows, weight)


def wide_outer_kernel(*refs, heads, order):
    lefts, (parts_ref, out_ref, rows_ref) = refs[:-3], refs[-3:]
    pair, narrow, shard, _ = out_ref.shape

    @pl.when(pl.program_id(0) == 0)
    def _():
        tokens = parts_ref.shape[3]
        row = 0
        for j in order:
            for b in range(parts_ref.shape[0] // heads):
                rows_ref[row : row + tokens] = row_block(parts_ref, j, b, heads)
                row += tokens

    for n in range(narrow):
        left = jnp.concatenate([ref[...] for ref in lefts[n::narrow]], axis=0)
        acc = lax.dot_general(
            left, rows_ref[...], CONTRACT_FIRST, preferred_element_type=jnp.float32
        )
        for y in range(pair):
            out_ref[y, n] = acc[y * shard : (y + 1) * shard].astype(jnp.bfloat16)


def wide_outer(lefts, parts, wide, heads, order):
    narrow = len(lefts)
    units, count, blocks, tokens, head_dim = parts.shape
    shard, width = lefts[0].shape[1] // (wide * narrow), count * heads * head_dim
    block = lefts[0].shape[0]
    rows = blocks * tokens * units // heads
    deep = wide // 2
    return pl.pallas_call(
        functools.partial(wide_outer_kernel, heads=heads, order=order),
        grid=(deep,),
        out_shape=(
            jax.ShapeDtypeStruct((wide, narrow, shard, width), jnp.bfloat16),
            jax.ShapeDtypeStruct((rows, width), jnp.bfloat16),
        ),
        in_specs=[
            pl.BlockSpec((block, 2 * shard), lambda i, n=n: (0, n * deep + i))
            for _ in lefts
            for n in range(narrow)
        ]
        + [resident(parts.shape)],
        out_specs=(
            pl.BlockSpec((2, narrow, shard, width), lambda i: (i, 0, 0, 0)),
            pl.BlockSpec((rows, width), lambda i: (0, 0)),
        ),
        compiler_params=BIG,
        name="wide_outer",
    )(*[left for left in lefts for _ in range(narrow)], parts)


def row_block(parts_ref, j, b, heads):
    return jnp.concatenate(
        [
            parts_ref[b * heads + h, part, j]
            for part in range(parts_ref.shape[1])
            for h in range(heads)
        ],
        axis=1,
    )


def unproject_kernel(parts_ref, weight_ref, *refs, heads, order):
    outs, rows_ref = refs[:-1], refs[-1]
    for step, j in enumerate(order):

        @pl.when(pl.program_id(0) == step)
        def _():
            rows = jnp.concatenate(
                [row_block(parts_ref, j, b, heads) for b in range(parts_ref.shape[0] // heads)],
                axis=0,
            )
            rows_ref[j] = rows
            acc = jnp.dot(rows, weight_ref[...], preferred_element_type=jnp.float32)
            outs[j][...] = acc.astype(jnp.bfloat16)


def unproject(parts, weight, heads):
    units, count, blocks, tokens, head_dim = parts.shape
    step = tokens * units // heads
    inner = count * heads * head_dim
    width = weight.shape[1]
    results = pl.pallas_call(
        functools.partial(unproject_kernel, heads=heads, order=(3, 1, 2, 0)),
        grid=(blocks,),
        out_shape=[jax.ShapeDtypeStruct((step, width), jnp.bfloat16)] * blocks
        + [jax.ShapeDtypeStruct((blocks, step, inner), jnp.bfloat16)],
        in_specs=[resident(parts.shape), resident(weight.shape)],
        out_specs=[pl.BlockSpec((step, width), lambda i: (0, 0))] * blocks
        + [pl.BlockSpec((blocks, step, inner), lambda i: (0, 0, 0))],
        compiler_params=BIG,
        name="unproject",
    )(parts, weight)
    return results[:blocks], results[blocks].reshape(blocks * step, inner)


def mask_of(segc_ref, segr_ref, i, lo):
    keys = 512 * (i + 1 - lo)
    same = segc_ref[i] == segr_ref[:, 512 * lo : 512 * (i + 1)]
    rows = lax.broadcasted_iota(jnp.int32, (512, keys), 0) + 512 * (i - lo)
    cols = lax.broadcasted_iota(jnp.int32, (512, keys), 1)
    return jnp.logical_and(same, cols <= rows)


def take(me_ref, parts_ref, part, first, last, half):
    blocks = [
        parts_ref[4 * (i % half) : 4 * (i % half) + 4, part, (i // half) ^ me_ref[0]].reshape(512, -1)
        for i in range(first, last + 1)
    ]
    return blocks[0] if len(blocks) == 1 else jnp.concatenate(blocks, axis=0)


def give(me_ref, out_ref, part, i, half, rows):
    rows = rows.astype(out_ref.dtype).reshape(4, 128, -1)
    out_ref[4 * (i % half) : 4 * (i % half) + 4, part, (i // half) ^ me_ref[0]] = rows


def fwd_kernel(me_ref, segc_ref, segr_ref, parts_ref, out_ref, lse_ref, *, blocks, scale2):
    half = blocks // 4
    for i in range(blocks):
        lo = max(i - 1, 0)
        q = take(me_ref, parts_ref, 0, i, i, half)
        k = take(me_ref, parts_ref, 1, lo, i, half)
        v = take(me_ref, parts_ref, 2, lo, i, half)
        s = lax.dot_general(q, k, CONTRACT_LAST, preferred_element_type=jnp.float32)
        s = jnp.where(mask_of(segc_ref, segr_ref, i, lo), s * scale2, neg_big)
        m = jnp.max(s, axis=-1, keepdims=True)
        p = jnp.exp2(s - m)
        total = jnp.sum(p, axis=-1, keepdims=True)
        o = jnp.dot(p.astype(jnp.bfloat16), v, preferred_element_type=jnp.float32)
        give(me_ref, out_ref, 0, i, half, o / total)
        lse_ref[i] = m + jnp.log2(total)


def bwd_kernel(
    me_ref, segc_ref, segr_ref, lse_ref, parts_ref, do_ref, grad_ref, dk_acc, dv_acc, *, blocks, scale, scale2
):
    half = blocks // 4
    f32 = jnp.float32
    for i in range(blocks):
        lo = max(i - 1, 0)
        q = take(me_ref, parts_ref, 0, i, i, half)
        k = take(me_ref, parts_ref, 1, lo, i, half)
        v = take(me_ref, parts_ref, 2, lo, i, half)
        do = take(me_ref, do_ref, 0, i, i, half)
        s = lax.dot_general(q, k, CONTRACT_LAST, preferred_element_type=f32)
        s = jnp.where(mask_of(segc_ref, segr_ref, i, lo), s * scale2, neg_big)
        p = jnp.exp2(s - lse_ref[i])
        dp = lax.dot_general(do, v, CONTRACT_LAST, preferred_element_type=f32)
        t = p * dp
        delta = jnp.sum(t, axis=-1, keepdims=True)
        ds = (t - p * delta).astype(jnp.bfloat16)
        give(me_ref, grad_ref, 0, i, half, jnp.dot(ds, k, preferred_element_type=f32) * scale)
        dk = lax.dot_general(ds, q, CONTRACT_FIRST, preferred_element_type=f32)
        dv = lax.dot_general(
            p.astype(jnp.bfloat16), do, CONTRACT_FIRST, preferred_element_type=f32
        )
        if i > 0:
            give(me_ref, grad_ref, 1, i - 1, half, (dk_acc[...] + dk[:512]) * scale)
            give(me_ref, grad_ref, 2, i - 1, half, dv_acc[...] + dv[:512])
        if i == blocks - 1:
            give(me_ref, grad_ref, 1, i, half, dk[-512:] * scale)
            give(me_ref, grad_ref, 2, i, half, dv[-512:])
        else:
            dk_acc[...] = dk[-512:]
            dv_acc[...] = dv[-512:]


def attend_fwd(me, segc, segr, parts):
    blocks = segc.shape[0]
    units, _, narrow, rows, width = parts.shape
    scale2 = math.log2(math.e) / math.sqrt(width)
    return pl.pallas_call(
        functools.partial(fwd_kernel, blocks=blocks, scale2=scale2),
        out_shape=(
            jax.ShapeDtypeStruct((units, 1, narrow, rows, width), jnp.bfloat16),
            jax.ShapeDtypeStruct((blocks, 512, 1), jnp.float32),
        ),
        in_specs=[SMEM_SPEC] + vmem_specs(3),
        out_specs=tuple(vmem_specs(2)),
        compiler_params=BIG,
        name="attend_fwd",
    )(me, segc, segr, parts)


def attend_bwd(me, segc, segr, lse, parts, dout):
    blocks = segc.shape[0]
    width = parts.shape[-1]
    scale = 1.0 / math.sqrt(width)
    return pl.pallas_call(
        functools.partial(
            bwd_kernel, blocks=blocks, scale=scale, scale2=scale * math.log2(math.e)
        ),
        out_shape=jax.ShapeDtypeStruct(parts.shape, jnp.bfloat16),
        in_specs=[SMEM_SPEC] + vmem_specs(5),
        out_specs=vmem_specs(1)[0],
        scratch_shapes=[pltpu.VMEM((512, width), jnp.float32)] * 2,
        compiler_params=BIG,
        name="attend_bwd",
    )(me, segc, segr, lse, parts, dout)


def ff_kernel(rows_ref, *refs):
    weights, (bias_ref, right_ref, hidden_ref, slope_ref, outer_ref) = refs[:-5], refs[-5:]
    step = 256
    depth = rows_ref.shape[1] // len(weights)
    for r in range(0, rows_ref.shape[0], step):
        x = bias_ref[...]
        for n, weight_ref in enumerate(weights):
            x = x + jnp.dot(
                rows_ref[r : r + step, n * depth : (n + 1) * depth],
                weight_ref[...].reshape(depth, -1),
                preferred_element_type=jnp.float32,
            )
        below = 0.5 * (1.0 + lax.erf(x * math.sqrt(0.5)))
        hidden_ref[r : r + step] = (x * below).astype(jnp.bfloat16)
        slope_ref[r : r + step] = below + x * (
            jnp.exp(-0.5 * x * x) * (1.0 / math.sqrt(2.0 * math.pi))
        )
    outer_ref[...] = lax.dot_general(
        hidden_ref[...], right_ref[...], CONTRACT_FIRST, preferred_element_type=jnp.float32
    ).astype(jnp.bfloat16)


def feed_forward(rows, weight, bias, right):
    count, width = right.shape
    deep, narrow, shard, inner = weight.shape
    step = 256
    return pl.pallas_call(
        ff_kernel,
        grid=(inner // step,),
        out_shape=(
            jax.ShapeDtypeStruct((count, inner), jnp.bfloat16),
            jax.ShapeDtypeStruct((count, inner), jnp.float32),
            jax.ShapeDtypeStruct((inner, width), jnp.bfloat16),
        ),
        in_specs=[resident(rows.shape)]
        + [
            pl.BlockSpec((deep, 1, shard, step), lambda i, n=n: (0, n, 0, i)) for n in range(narrow)
        ]
        + [pl.BlockSpec((1, step), lambda i: (0, i)), resident(right.shape)],
        out_specs=(
            pl.BlockSpec((count, step), lambda i: (0, i)),
            pl.BlockSpec((count, step), lambda i: (0, i)),
            pl.BlockSpec((step, width), lambda i: (i, 0)),
        ),
        compiler_params=BIG,
        name="feed_forward",
    )(rows, *[weight] * narrow, bias.reshape(1, -1), right)


def pull_kernel(rows_ref, weight_ref, slope_ref, grad_ref, sum_ref):
    step = 256
    total = jnp.zeros((1, weight_ref.shape[0]), jnp.float32)
    for r in range(0, rows_ref.shape[0], step):
        pull = lax.dot_general(
            rows_ref[r : r + step],
            weight_ref[...],
            CONTRACT_LAST,
            preferred_element_type=jnp.float32,
        )
        grad = (pull * slope_ref[r : r + step]).astype(jnp.bfloat16)
        grad_ref[r : r + step] = grad
        total = total + jnp.sum(grad.astype(jnp.float32), axis=0, keepdims=True)
    sum_ref[...] = total


def pull_back(rows, weight, slope):
    count, inner = slope.shape
    width = weight.shape[1]
    step = 256
    return pl.pallas_call(
        pull_kernel,
        grid=(inner // step,),
        out_shape=(
            jax.ShapeDtypeStruct((count, inner), jnp.bfloat16),
            jax.ShapeDtypeStruct((1, inner), jnp.float32),
        ),
        in_specs=[
            resident(rows.shape),
            pl.BlockSpec((step, width), lambda i: (i, 0)),
            pl.BlockSpec((count, step), lambda i: (0, i)),
        ],
        out_specs=(
            pl.BlockSpec((count, step), lambda i: (0, i)),
            pl.BlockSpec((1, step), lambda i: (0, i)),
        ),
        compiler_params=BIG,
        name="pull_back",
    )(rows, weight, slope)


def place_qkv_kernel(me_ref, *refs):
    pieces, outs = refs[:4], refs[4:]
    cols = pieces[0].shape[1] // len(outs)
    for part, out_ref in enumerate(outs):
        blocks = [piece[:, part * cols : (part + 1) * cols].astype(jnp.float32) for piece in pieces]
        for n in range(4):
            value = blocks[n]
            for me in range(1, 4):
                value = jnp.where(me_ref[0] == me, blocks[n ^ me], value)
            out_ref[:, n * cols : (n + 1) * cols] = value


def place_qkv(me, pieces):
    rows, width = pieces[0].shape
    shape = jax.ShapeDtypeStruct((rows, width // 3 * 4), jnp.float32)
    return pl.pallas_call(
        place_qkv_kernel,
        out_shape=(shape,) * 3,
        in_specs=[SMEM_SPEC] + vmem_specs(4),
        out_specs=tuple(vmem_specs(3)),
        compiler_params=BIG,
        name="place_qkv",
    )(me, *pieces)


def place_up_kernel(me_ref, own_ref, other_ref, out_ref, *, step):
    narrow, _, inner = own_ref.shape
    high = (me_ref[1] & 1) > 0
    for n in range(narrow):
        own, other = own_ref[n ^ me_ref[0]], other_ref[n ^ me_ref[0]]
        for z in range(inner // step):
            c = (n * (inner // step) + z) * 2 * step
            a = own[:, z * step : (z + 1) * step].astype(jnp.float32)
            b = other[:, z * step : (z + 1) * step].astype(jnp.float32)
            out_ref[:, c : c + step] = jnp.where(high, b, a)
            out_ref[:, c + step : c + 2 * step] = jnp.where(high, a, b)


def place_up(me, own, other, step):
    narrow, shard, inner = own.shape
    return pl.pallas_call(
        functools.partial(place_up_kernel, step=step),
        out_shape=jax.ShapeDtypeStruct((shard, 2 * narrow * inner), jnp.float32),
        in_specs=[SMEM_SPEC] + vmem_specs(2),
        out_specs=vmem_specs(1)[0],
        compiler_params=BIG,
        name="place_up",
    )(me, own, other)


def pick_kernel(me_ref, weight_ref, out_ref):
    _, narrow, shard, inner = out_ref.shape
    high = (me_ref[1] & 1) > 0
    step = 256
    for n in range(narrow):
        for z in range(inner // step):
            c = (n * (inner // step) + z) * 2 * step
            low_part = weight_ref[:, c : c + step]
            high_part = weight_ref[:, c + step : c + 2 * step]
            cols = slice(z * step, (z + 1) * step)
            out_ref[0, n, :, cols] = jnp.where(high, high_part, low_part)
            out_ref[1, n, :, cols] = jnp.where(high, low_part, high_part)


def pick(me, weight, narrow):
    shard, total = weight.shape
    return pl.pallas_call(
        pick_kernel,
        out_shape=jax.ShapeDtypeStruct((2, narrow, shard, total // (2 * narrow)), weight.dtype),
        in_specs=[SMEM_SPEC] + vmem_specs(1),
        out_specs=vmem_specs(1)[0],
        compiler_params=BIG,
        name="pick",
    )(me, weight)


def on_device(
    block_input,
    segment_ids,
    cotangent,
    attn_gain,
    attn_shift,
    query_weight,
    query_bias,
    key_weight,
    value_weight,
    value_bias,
    out_weight,
    out_bias,
    mlp_gain,
    mlp_shift,
    up_weight,
    up_bias,
    down_weight,
    down_bias,
):
    f32 = jnp.float32
    bf16 = jnp.bfloat16
    batch, tokens, width = block_input.shape
    narrow = lax.axis_size(NARROW)
    wide = lax.axis_size(WIDE)
    me_n = lax.axis_index(NARROW)
    me_w = lax.axis_index(WIDE)
    me = jnp.stack([me_n, me_w]).astype(jnp.int32)
    rows = batch * tokens
    heads = HEADS // narrow
    head_dim = width // HEADS
    cols = heads * head_dim
    shard = width // (narrow * wide)
    deep = wide // 2
    ff_shard = up_bias.shape[0]
    ff_local = ff_shard * deep
    me_y = me_w & 1

    def qkv_block(n):
        return jnp.concatenate(
            [
                lax.dynamic_slice_in_dim(weight, n * cols, cols, 1)
                for weight in (query_weight, key_weight, value_weight)
            ],
            axis=1,
        )

    out_w = wide_gather(out_weight, 0)
    qkv_shard = narrow_swap(qkv_block)
    attn_parts = ring_gather(qkv_shard, 1)

    smalls = [
        attn_gain, attn_shift, out_bias, mlp_gain, mlp_shift, down_bias, query_bias, value_bias, up_bias
    ]
    ids = segment_ids.astype(bf16).reshape(-1)
    small = cube_gather(jnp.concatenate(smalls + [ids])[None])

    def full_vector(k):
        return small[:, k * shard : (k + 1) * shard].reshape(-1).astype(f32)

    gain_attn, shift_attn, obias, gain_mlp, shift_mlp, dbias = [full_vector(k) for k in range(6)]
    mine = lax.dynamic_slice_in_dim(small, me_n * wide, wide, 0)
    qbias = mine[:, 6 * shard : 7 * shard].reshape(-1).astype(f32)
    vbias = mine[:, 7 * shard : 8 * shard].reshape(-1).astype(f32)
    ubias = mine[:, 8 * shard : 8 * shard + ff_shard].reshape(deep, 2, ff_shard)
    ubias = at(ubias, me_y, 1).reshape(-1).astype(f32)
    qkv_bias = jnp.concatenate([qbias, jnp.zeros_like(qbias), vbias])

    inputs = block_input.astype(f32).reshape(rows, width)
    first_norm = narrow_gather(normalize(inputs, gain_attn, shift_attn).astype(bf16))
    cotan_own = cotangent.reshape(rows, width)
    attn_parts = hold(attn_parts, out_w)
    sent = project_parts(first_norm, attn_parts, qkv_bias, wide, 3, heads, tokens)
    qkv = wide_swap(sent)

    picked = pick(me, hold(up_weight, first_norm[3]), narrow)
    high = me_y > 0
    here, there = picked[0], flip(hold(picked[1], sent), WIDE, 1)
    up_pair = jnp.stack([jnp.where(high, there, here), jnp.where(high, here, there)], axis=1)
    up_shard = narrow_swap(lambda n: at(up_pair, n)).reshape(narrow, 2 * shard, ff_local)
    ids = hold(small, sent)[:, -batch * tokens :].reshape(narrow * wide, batch, tokens)
    unit_ids = at(ids, me_w // heads, 1).reshape(-1).astype(jnp.int32)
    segc = unit_ids.reshape(-1, 512, 1)
    segr = unit_ids.reshape(1, -1)
    qkv = hold(qkv, up_shard)
    unit_out, lse = attend_fwd(me, segc, segr, qkv)
    up_parts = z_gather(hold(up_shard, unit_out)[None], 0)
    unit_back = wide_swap(unit_out)
    near = spread_near(hold(cotan_own, unit_out))
    unit_back = hold(unit_back, *near)
    cotan = jnp.concatenate(near + [flip(hold(part, unit_back), NARROW, 1) for part in near], axis=0)
    partial, mixed = unproject(unit_back, out_w, heads)
    middle = inputs + narrow_scatter(partial) + obias
    down_late, middle = lax.optimization_barrier((down_weight, middle, up_parts, cotan))[:2]
    down_w = z_gather(down_late, 0)

    second_norm = spread(normalize(middle, gain_mlp, shift_mlp).astype(bf16))
    second_norm = jnp.concatenate(second_norm, axis=0)
    hidden, slope, down_grad = feed_forward(second_norm, up_parts, ubias, cotan)
    down_grad = z_scatter(down_grad, 0)
    inner_grad, ubias_grad = pull_back(cotan, down_w, slope)
    split = inner_grad.shape[0] // 2
    far = times_parts(inner_grad, 1, split, up_parts)
    near = times_parts(hold(inner_grad, far), 0, split, up_parts)
    up_made = []

    def make_up_grad(event):
        up_made.append(outer_sum(second_norm, hold(inner_grad, event)).astype(bf16))
        return up_made[0]

    second_grad = fold_last(*fold_first(far, near), make_up_grad)
    mlp_pull = jax.vjp(normalize, middle, gain_mlp, shift_mlp)[1]
    middle_part, mgain_grad, mshift_grad = mlp_pull(second_grad)
    middle_grad = cotan_own.astype(f32) + middle_part
    branch_own = middle_grad.astype(bf16)
    dbias_grad = jnp.sum(cotan_own.astype(f32), axis=0)

    obias_grad = jnp.sum(branch_own.astype(f32), axis=0)
    out_made = []

    def make_outputs(beside):
        late = hold(hidden, beside)
        out_made.append(matmul(late[split:], down_w).astype(bf16))
        out_made.append(matmul(late[:split], down_w).astype(bf16))
        return out_made

    branch = narrow_gather(branch_own, make_outputs)
    up_grad = hold(up_made[0], out_made[1], down_grad)
    up_grad = z_scatter(up_grad.reshape(narrow, 2 * deep * shard, ff_local), 1)
    no_bias = jnp.zeros((cols,), f32)
    sent = project(branch, out_w, no_bias, wide, 1, heads, tokens, True)
    out_grad = outer_sum(hold(mixed, sent), jnp.concatenate(branch, axis=0)).astype(bf16)
    own, over_x, over_y = fold_first(*hold_all(out_made, sent))
    dout, over_x, over_y = hold_all((wide_swap(sent), over_x, over_y), out_grad)
    output = middle + fold_last(own, over_x, over_y) + dbias
    block_output = output.astype(bf16).reshape(batch, tokens, width)
    unit_grads = attend_bwd(me, segc, segr, lse, qkv, dout)
    unit_grads = hold(unit_grads, block_output)
    grads = wide_swap(unit_grads)
    up_rows = hold(up_grad, unit_grads).reshape(narrow, 2, shard, ff_local)
    up_sent = up_rows
    up_rows = narrow_blocks(lambda n: at(up_sent, n))
    up_own = jnp.stack([at(block, me_y) for block in up_rows])
    up_other = flip(jnp.stack([at(block, 1 - me_y) for block in up_rows]), WIDE, 1)
    up_back = place_up(me, up_own, up_other, ff_shard)
    down_grad = down_grad.astype(f32)
    grads = hold(grads, up_back)
    order = (1, 3, 0, 2)
    sums, back = wide_outer(
        [first_norm[j] for j in order], grads, wide, heads, order
    )
    made = {}

    def beside(stage, event):
        if stage == 0:
            far = times_parts(hold(back, event), 0, 2 * rows, attn_parts)
            made["far"] = far.reshape(2, rows, width)
            return (far,)
        if stage == 1:
            far = made["far"]
            near = times_parts(hold(back, event), 1, 2 * rows, attn_parts)
            near = near.reshape(2, rows, width)
            made["first"] = narrow_scatter([near[0], far[0], near[1], far[1]])
            return (near,)
        if stage == 2:
            attn_pull = jax.vjp(normalize, inputs, gain_attn, shift_attn)[1]
            input_part, again_grad, ashift_grad = attn_pull(made["first"])
            made["pulled"] = middle_grad + input_part, again_grad, ashift_grad
            return made["pulled"] + (down_grad,)
        return ()

    qkv_rows = jnp.concatenate(ring_scatter(sums, beside, 1), axis=-1)
    out_grad = wide_scatter(hold(out_grad, back), 0)
    swapped = narrow_blocks(lambda n: at(qkv_rows, n))
    qkv_grad = place_qkv(me, swapped)
    back_sums = jnp.sum(back.astype(f32), axis=0)
    input_grad, again_grad, ashift_grad = made["pulled"]
    input_grad = input_grad.reshape(batch, tokens, width)

    fulls = [again_grad, ashift_grad, obias_grad, mgain_grad, mshift_grad, dbias_grad]
    fulls = jnp.concatenate([v.reshape(narrow * wide, shard) for v in fulls], axis=1)
    ubias_rows = jnp.zeros((deep, 2, ff_shard), f32)
    ubias_rows = lax.dynamic_update_slice_in_dim(
        ubias_rows,
        ubias_grad.reshape(deep, 1, ff_shard),
        me_y,
        1,
    )
    slices = [back_sums[:cols], back_sums[2 * cols :], ubias_rows]
    slices = jnp.concatenate([v.reshape(wide, -1) for v in slices], axis=1)
    placed = jnp.zeros((narrow * wide, slices.shape[1]), f32)
    placed = lax.dynamic_update_slice_in_dim(placed, slices, me_n * wide, 0)
    vectors = cube_scatter(jnp.concatenate([fulls, placed], axis=1), swapped[1])

    def vector(k):
        return vectors[k * shard : (k + 1) * shard]

    return (
        block_output,
        input_grad,
        vector(0),
        vector(1),
        qkv_grad[0],
        vector(6),
        qkv_grad[1],
        qkv_grad[2],
        vector(7),
        out_grad.astype(f32),
        vector(2),
        vector(3),
        vector(4),
        up_back,
        vectors[8 * shard :],
        down_grad,
        vector(5),
    )


def body_of(mesh):
    def body(*args):
        batch, tokens, width = args[0].shape
        narrow, wide = mesh.shape[NARROW], mesh.shape[WIDE]
        one_unit = batch * (HEADS // narrow) == wide and tokens == 128 and narrow == 4
        return (on_device if one_unit else on_device_ring)(*args)

    return body


def solution(mesh):
    return jax.shard_map(
        body_of(mesh),
        mesh=mesh,
        in_specs=(
            P(None, BOTH, None),
            P(None, BOTH),
            P(None, BOTH, None),
            P(BOTH),
            P(BOTH),
            P(BOTH, None),
            P(BOTH),
            P(BOTH, None),
            P(BOTH, None),
            P(BOTH),
            P(BOTH, None),
            P(BOTH),
            P(BOTH),
            P(BOTH),
            P(BOTH, None),
            P(BOTH),
            P(BOTH, None),
            P(BOTH),
        ),
        out_specs=(
            P(None, BOTH, None),
            P(None, BOTH, None),
            P(BOTH),
            P(BOTH),
            P(BOTH, None),
            P(BOTH),
            P(BOTH, None),
            P(BOTH, None),
            P(BOTH),
            P(BOTH, None),
            P(BOTH),
            P(BOTH),
            P(BOTH),
            P(BOTH, None),
            P(BOTH),
            P(BOTH, None),
            P(BOTH),
        ),
        check_vma=False,
    )
```
